32 devices in a mesh: lat: 4 (over y, x), lon: 2 (over core), fsdp: 4 (over z).
Axes of the slice: x: 2, y: 2, z: 4, core: 2. Of those that a mesh axis runs over, the one named last changes fastest.
Arguments:
- latent: bfloat16 [4, 2, 24, 24, 512], P('fsdp', None, 'lat', 'lon'), may hold values from -6 to 6
- norm_gain: float32 [2, 512], replicated, may hold values from 0.1 to 1.9
- qkv_weight: bfloat16 [2, 512, 1536], P(None, 'fsdp'), may hold values from -0.25 to 0.25
- out_weight: bfloat16 [2, 512, 512], P(None, 'fsdp'), may hold values from -0.25 to 0.25
- rel_bias: float32 [2, 759, 16], replicated, may hold values from -4 to 304, as said below
- bias_index: int32 [144, 144], replicated, may hold values from 0 to 758
- region_ids: int32 [2, 24, 24], P(None, 'lat', 'lon'), may hold values from 0 to 3
Outputs:
- mixed: bfloat16 [4, 2, 24, 24, 512], P('fsdp', None, 'lat', 'lon')
The draws below stay inside these ranges and needn't reach their ends.
Inputs may be any that keep to these rules, and one draw needn't show every extreme that they name: `rel_bias`: in the hidden draw.
All inputs are finite; a program needn't handle non-finite values.
Results may differ from the reference program's by a relative error of at most 0.012.
Values may be sent and summed in bfloat16 or wider, within the bound.
No kernel may reach another device: no remote copies, remote signals or barrier semaphores. Data moves between devices by JAX's collectives and lax.ppermute only.
A program may use at most 64 MiB of HBM per device.

```python
import jax
import jax.numpy as jnp
from jax import lax

D = 512
HEADS = 16
HEAD_DIM = 32
WZ = 2
WH = 6
WW = 12
WIN = 144
BIAS_ROWS = 759
LEVELS = 2
SAMPLES = 4
NLAT = 24
NLON = 24


def draw_rel_bias(key, part):
    values = jnp.clip(jax.random.normal(jax.random.fold_in(key, 11), (2, BIAS_ROWS, HEADS), jnp.float32), -4.0, 4.0)
    return values


def touch_ends(array, rng, smallest, largest):
    longest = array.shape.index(max(array.shape))
    spots = []
    for shift in (0, 1):
        where = [jax.random.randint(jax.random.fold_in(rng, axis), (), 0, length) for axis, length in enumerate(array.shape)]
        where[longest] = (where[longest] + shift) % array.shape[longest]
        spots.append(tuple(where))
    return array.at[spots[0]].set(smallest).at[spots[1]].set(largest)


def shard_levels(own_key, extent, cuts, low, top_value):
    def one(position, shards_of):
        draws = jax.random.uniform(jax.random.fold_in(jax.random.fold_in(own_key, 6), position), (shards_of,), jnp.float32, low / len(cuts), top_value / len(cuts))
        return jnp.repeat(jnp.exp(draws), extent[position] // shards_of).reshape((-1,) + (1,) * (len(extent) - position - 1))

    level = one(*cuts[0])
    for cut in cuts[1:]:
        level = level * one(*cut)
    return level


def gaussian(own_key, dims, scale, limit, shards=(), held_as=jnp.bfloat16):
    entries = jax.random.normal(own_key, dims, jnp.float32) * scale
    if len(shards) > 0:
        entries = shard_levels(own_key, dims, shards, -0.22, 0.18) * entries
    return jnp.clip(entries, min=-limit, max=limit).astype(held_as)


def setup_inputs(seed: int = 0) -> dict:
    key_of = jax.random.split(jax.random.key(seed), 8)
    latent = gaussian(key_of[0], (SAMPLES, LEVELS, NLAT, NLON, D), 1.0, 6.0, ((0, 4), (2, 4), (3, 2)))
    norm_gain = jnp.clip(1.0 + 0.18 * jax.random.normal(key_of[1], (2, D), jnp.float32), 0.1, 1.9)
    qkv_weight = gaussian(key_of[2], (2, D, 3 * D), D ** -0.5, 0.25, ((1, 4),))
    out_weight = gaussian(key_of[3], (2, D, D), D ** -0.5, 0.25, ((1, 4),))
    rel_bias = draw_rel_bias(jax.random.fold_in(key_of[7], 71), 0)
    bias_index = touch_ends(jax.random.randint(key_of[5], (WIN, WIN), 0, BIAS_ROWS), jax.random.fold_in(key_of[5], 1), 0, BIAS_ROWS - 1).astype(jnp.int32)
    region_ids = touch_ends(jax.random.randint(key_of[6], (LEVELS, NLAT, NLON), 0, 4), jax.random.fold_in(key_of[6], 1), 0, 3).astype(jnp.int32)
    return dict(latent=latent, norm_gain=norm_gain, qkv_weight=qkv_weight, out_weight=out_weight, rel_bias=rel_bias, bias_index=bias_index, region_ids=region_ids)


def layer_norm(hidden, gain_row):
    values = hidden.astype(jnp.float32)
    centre = lax.optimization_barrier(jnp.mean(values, axis=-1, keepdims=True))
    shifted = values - centre
    variance = lax.optimization_barrier(jnp.mean(shifted * shifted, axis=-1, keepdims=True))
    return (shifted * lax.rsqrt(variance + 1e-05) * gain_row).astype(jnp.bfloat16)

def bias_table(rel_bias, bias_index, block_index):
    return jnp.take(jnp.transpose(rel_bias[block_index]), bias_index, axis=1)

def split_bands(field_tile):
    level_count, row_count, col_count, feature_width = field_tile.shape
    pieces = field_tile.reshape(level_count // WZ, WZ, row_count // WH, WH, col_count // WW, WW, feature_width)
    pieces = jnp.transpose(pieces, (2, 0, 4, 1, 3, 5, 6))
    return pieces.reshape(row_count // WH, level_count // WZ * (col_count // WW), WIN, feature_width)

def merge_bands(band_windows, level_count, col_count):
    band_count = band_windows.shape[0]
    feature_width = band_windows.shape[3]
    pieces = band_windows.reshape(band_count, level_count // WZ, col_count // WW, WZ, WH, WW, feature_width)
    pieces = jnp.transpose(pieces, (1, 3, 0, 4, 2, 5, 6))
    return pieces.reshape(level_count, band_count * WH, col_count, feature_width)

def window_attention(normed, weight, bias_heads, region_tags):
    group_count = normed.shape[0]
    packed = jnp.dot(normed.reshape(-1, D), weight, preferred_element_type=jnp.float32).astype(jnp.bfloat16)
    packed = packed.reshape(group_count, WIN, 3, HEADS, HEAD_DIM)
    scores = jnp.einsum('gqhd,gkhd->ghqk', packed[:, :, 0].astype(jnp.float32), packed[:, :, 1].astype(jnp.float32))
    scores = scores * HEAD_DIM ** (-0.5) + bias_heads[None]
    if region_tags is not None:
        allowed = region_tags[:, :, None] == region_tags[:, None, :]
        scores = jnp.where(allowed[:, None], scores, -jnp.inf)
    row_peak = lax.optimization_barrier(jnp.max(scores, axis=-1, keepdims=True))
    exponent = jnp.exp(scores - row_peak)
    row_total = lax.optimization_barrier(jnp.sum(exponent, axis=-1, keepdims=True))
    attn_probs = (exponent / row_total).astype(jnp.bfloat16)
    mixed_out = jnp.einsum('ghqk,gkhd->gqhd', attn_probs.astype(jnp.float32), packed[:, :, 2].astype(jnp.float32))
    return mixed_out.astype(jnp.bfloat16).reshape(group_count, WIN, D)

def reference(latent, norm_gain, qkv_weight, out_weight, rel_bias, bias_index, region_ids):
    first_bias = bias_table(rel_bias, bias_index, 0)
    second_bias = bias_table(rel_bias, bias_index, 1)
    level_pos = lax.broadcasted_iota(jnp.int32, region_ids.shape, 0)
    row_pos = lax.broadcasted_iota(jnp.int32, region_ids.shape, 1)
    region_tags = region_ids * 4 + (level_pos == LEVELS - 1).astype(jnp.int32) * 2
    region_tags = region_tags + (row_pos >= NLAT - WH // 2).astype(jnp.int32)
    tag_bands = split_bands(region_tags[..., None])[..., 0]

    def first_band(band_rows):
        return window_attention(band_rows, qkv_weight[0], first_bias, None)

    def second_band(band_pair):
        return window_attention(band_pair[0], qkv_weight[1], second_bias, band_pair[1])

    def one_sample(sample):
        normed = layer_norm(sample, norm_gain[0])
        mixed_out = merge_bands(lax.map(first_band, split_bands(normed)), LEVELS, NLON)
        projected = jnp.dot(mixed_out.reshape(-1, D), out_weight[0], preferred_element_type=jnp.float32)
        middle = (sample.astype(jnp.float32) + projected.reshape(sample.shape)).astype(jnp.bfloat16)
        normed = layer_norm(middle, norm_gain[1])
        rolled = jnp.roll(normed, (-1, -(WH // 2), -(WW // 2)), axis=(0, 1, 2))
        mixed_out = lax.map(second_band, (split_bands(rolled), tag_bands))
        mixed_out = merge_bands(mixed_out, LEVELS, NLON)
        mixed_out = jnp.roll(mixed_out, (1, WH // 2, WW // 2), axis=(0, 1, 2))
        projected = jnp.dot(mixed_out.reshape(-1, D), out_weight[1], preferred_element_type=jnp.float32)
        return (middle.astype(jnp.float32) + projected.reshape(sample.shape)).astype(jnp.bfloat16)
    return lax.map(one_sample, latent)
```

```python
import functools

import jax
import jax.numpy as jnp
import numpy as np
from jax import lax
from jax.experimental import pallas as pl
from jax.experimental.pallas import tpu as pltpu
from jax.sharding import PartitionSpec as P

D = 512
HEADS = 16
HEAD_DIM = 32
WZ = 2
WH = 6
WW = 12
WIN = 144
BIAS_ROWS = 759
HALF = WIN // 2
LOG2E = 1.4426950408889634
SCALE2 = HEAD_DIM ** (-0.5) * LOG2E
NEG = -1e30


def passed_along(block, axis, distance):
    devices = range(lax.axis_size(axis))
    route = [((i - distance) % len(devices), i) for i in devices]
    return lax.ppermute(block, axis, route)


def layer_norm(hidden, gain_row):
    values = hidden.astype(jnp.float32)
    centre = jnp.mean(values, axis=-1, keepdims=True)
    shifted = values - centre
    variance = jnp.mean(shifted * shifted, axis=-1, keepdims=True)
    return (shifted * lax.rsqrt(variance + 1e-05) * gain_row).astype(jnp.bfloat16)


def bias_table(rel_bias, bias_index, block_index):
    return jnp.take(jnp.transpose(rel_bias[block_index]), bias_index, axis=1)


def split_tile(field_tile):
    sample_count, level_count, row_count, col_count, feature_width = field_tile.shape
    pieces = field_tile.reshape(
        sample_count, level_count // WZ, WZ, row_count // WH, WH, col_count // WW, WW, feature_width
    )
    pieces = jnp.transpose(pieces, (0, 1, 3, 5, 2, 4, 6, 7))
    return pieces.reshape(-1, WIN, feature_width)


def merge_tile(windows, tile_shape):
    sample_count, level_count, row_count, col_count, feature_width = tile_shape
    pieces = windows.reshape(
        sample_count, level_count // WZ, row_count // WH, col_count // WW, WZ, WH, WW, feature_width
    )
    pieces = jnp.transpose(pieces, (0, 1, 4, 2, 5, 3, 6, 7))
    return pieces.reshape(tile_shape)


def attend(normed, weight, bias_heads, region_tags):
    packed = jnp.dot(normed.reshape(-1, D), weight, preferred_element_type=jnp.float32).astype(
        jnp.bfloat16
    )
    packed = split_tile(packed.reshape(normed.shape[:-1] + (3 * D,)))
    packed = packed.reshape(-1, WIN, 3, HEADS, HEAD_DIM)
    scores = jnp.einsum(
        "gqhd,gkhd->ghqk", packed[:, :, 0], packed[:, :, 1], preferred_element_type=jnp.float32
    )
    scores = scores * HEAD_DIM ** (-0.5) + bias_heads[None]
    if region_tags is not None:
        window_tags = split_tile(region_tags[..., None])[..., 0]
        allowed = window_tags[:, :, None] == window_tags[:, None, :]
        blocked = jnp.where(allowed, jnp.float32(0.0), -jnp.inf)
        scores = scores + blocked[:, None]
    row_peak = jnp.max(scores, axis=-1, keepdims=True)
    exponent = jnp.exp(scores - row_peak)
    row_total = jnp.sum(exponent, axis=-1, keepdims=True)
    attn_probs = (exponent / row_total).astype(jnp.bfloat16)
    mixed_out = jnp.einsum(
        "ghqk,gkhd->gqhd", attn_probs, packed[:, :, 2], preferred_element_type=jnp.float32
    )
    return merge_tile(mixed_out.astype(jnp.bfloat16).reshape(-1, WIN, D), normed.shape)


def any_mesh(latent, norm_gain, qkv_weight, out_weight, rel_bias, bias_index, region_ids):
    half_rows = WH // 2
    half_cols = WW // 2
    row_count = latent.shape[2]
    col_count = latent.shape[3]
    gathered_qkv, gathered_out = (
        lax.all_gather(qkv_weight, "fsdp", axis=1, tiled=True),
        lax.all_gather(out_weight, "fsdp", axis=1, tiled=True),
    )

    def fetch_weights(block_index):
        return (gathered_qkv[block_index], gathered_out[block_index])

    first_qkv, first_out = fetch_weights(0)
    normed = layer_norm(latent, norm_gain[0])
    mixed_out = attend(normed, first_qkv, bias_table(rel_bias, bias_index, 0), None)
    projected = jnp.dot(mixed_out.reshape(-1, D), first_out, preferred_element_type=jnp.float32)
    middle = (latent.astype(jnp.float32) + projected.reshape(latent.shape)).astype(jnp.bfloat16)
    second_qkv, second_out = fetch_weights(1)
    normed = jnp.roll(layer_norm(middle, norm_gain[1]), -1, axis=1)
    east_strip = passed_along(normed[:, :, :, :half_cols], "lon", -1)
    widened = jnp.concatenate([normed[:, :, :, half_cols:], east_strip], axis=3)
    north_strip = passed_along(widened[:, :, :half_rows], "lat", -1)
    rolled = jnp.concatenate([widened[:, :, half_rows:], north_strip], axis=2)
    level_pos = lax.broadcasted_iota(jnp.int32, region_ids.shape, 0)
    row_pos = (
        lax.broadcasted_iota(jnp.int32, region_ids.shape, 1) + lax.axis_index("lat") * row_count
    )
    region_tags = region_ids * 4 + (level_pos == region_ids.shape[0] - 1).astype(jnp.int32) * 2
    region_tags = region_tags + (row_pos >= row_count * lax.axis_size("lat") - half_rows).astype(
        jnp.int32
    )
    region_tags = region_tags[None]
    mixed_out = attend(rolled, second_qkv, bias_table(rel_bias, bias_index, 1), region_tags)
    south_strip = passed_along(mixed_out[:, :, row_count - half_rows :], "lat", 1)
    widened = jnp.concatenate([south_strip, mixed_out[:, :, : row_count - half_rows]], axis=2)
    west_strip = passed_along(widened[:, :, :, col_count - half_cols :], "lon", 1)
    mixed_out = jnp.concatenate([west_strip, widened[:, :, :, : col_count - half_cols]], axis=3)
    mixed_out = jnp.roll(mixed_out, 1, axis=1)
    projected = jnp.dot(mixed_out.reshape(-1, D), second_out, preferred_element_type=jnp.float32)
    return (middle.astype(jnp.float32) + projected.reshape(latent.shape)).astype(jnp.bfloat16)


PAIR = 2
MY_HEADS = HEADS // PAIR
MINE = MY_HEADS * HEAD_DIM
QKV = 3 * MINE
COLS = QKV + D // PAIR
TALL = 3 * WIN
KEEP0 = 64
KEEP1 = TALL - 64
KEPT = KEEP1 - KEEP0
PART = WIN - KEEP0
REGION_ROWS = 8
GROUP = 128 // HEAD_DIM
F32 = jnp.float32
BF16 = jnp.bfloat16


def window_sources():
    src = np.zeros((2, 2, WH, WW, WZ), np.int32)
    for a in range(2):
        for v in range(2):
            for dh in range(WH):
                for dw in range(WW):
                    for dz in range(WZ):
                        row = dh + (WH // 2 if a else -(WH // 2))
                        col = (WW // 2 + WW * v + dw) % (2 * WW)
                        level = (dz + 1) % WZ
                        t = (row + WH) * WW * WZ + (col % WW) * WZ + level
                        src[a, v, dh, dw, dz] = (col // WW) * KEPT + t - KEEP0
    return src.reshape(-1, 1)


def tile_sources():
    src = np.zeros((2, WH, WW, WZ), np.int32)
    for l in range(2):
        for row in range(WH):
            for cw in range(WW):
                for level in range(WZ):
                    a = 0 if row < WH // 2 else 1
                    dh = (row + WH // 2) % WH
                    col = (WW * l + cw - WW // 2) % (2 * WW)
                    dz = (level - 1) % WZ
                    t = dh * WW * WZ + (col % WW) * WZ + dz - (0 if a else KEEP0)
                    src[l, row, cw, level] = (a * 2 + col // WW) * PART + t
    return src.reshape(-1, 1)


def one_hot(sources, width):
    lanes = lax.broadcasted_iota(jnp.int32, (sources.shape[0], width), 1)
    return jnp.where(lanes == sources, 1.0, 0.0).astype(BF16)


def nt_dot(a, b):
    return lax.dot_general(a, b, (((1,), (1,)), ((), ())), preferred_element_type=F32)


def nn_dot(a, b):
    return jnp.dot(a, b, preferred_element_type=F32)


def norm_rows(values, gain_row):
    centre = jnp.mean(values, axis=-1, keepdims=True)
    shifted = values - centre
    variance = jnp.mean(shifted * shifted, axis=-1, keepdims=True)
    return (shifted * lax.rsqrt(variance + 1e-05) * gain_row).astype(BF16)


def bias_kernel(table_ref, index_ref, first_ref, second_ref, table, index):
    me = lax.axis_index("lon")
    for b in range(2):
        heads = table_ref[b, pl.ds(pl.multiple_of(MY_HEADS * me, MY_HEADS), MY_HEADS), :]
        table[b, :, 0:BIAS_ROWS] = heads * LOG2E
    to = lax.broadcasted_iota(jnp.int32, (WIN, WIN), 0)
    frm = lax.broadcasted_iota(jnp.int32, (WIN, WIN), 1)
    move = jnp.where((to & 1) * HALF + (to >> 1) == frm, 1.0, 0.0).astype(BF16)

    def moved(a):
        a = nn_dot(move, a.astype(F32).astype(BF16)).astype(BF16)
        return nt_dot(a, move).astype(jnp.int32)

    whole = index_ref[...]
    index[:, 0:WIN] = moved(whole >> 8) * 256 + moved(whole & 255)
    outs = (first_ref, second_ref)
    chunks = (BIAS_ROWS + 127) // 128

    def step(g, carry):
        rows = pl.ds(pl.multiple_of(g * 8, 8), 8)
        for lo, hi in ((0, 128), (128, WIN)):
            at = index[rows, lo : lo + 128]
            low = at & 127
            chunk = at >> 7
            masks = [chunk == k for k in range(chunks)]
            for b in range(2):
                for h in range(MY_HEADS):
                    acc = None
                    for k in range(chunks):
                        row = jnp.broadcast_to(
                            table[b, h : h + 1, 128 * k : 128 * k + 128], (8, 128)
                        )
                        got = jnp.take_along_axis(row, low, axis=1, mode="promise_in_bounds")
                        acc = got if acc is None else jnp.where(masks[k], got, acc)
                    outs[b][h, rows, lo:hi] = acc[:, : hi - lo]
        return carry

    lax.fori_loop(0, WIN // 8, step, 0)


def bias_call(table, index):
    out = jax.ShapeDtypeStruct((MY_HEADS, WIN, WIN), F32)
    return pl.pallas_call(
        bias_kernel,
        out_shape=(out, out),
        scratch_shapes=[
            pltpu.VMEM((2, MY_HEADS, (BIAS_ROWS + 127) // 128 * 128), F32),
            pltpu.VMEM((WIN, 256), jnp.int32),
        ],
        cost_estimate=pl.CostEstimate(flops=10**9, bytes_accessed=2 * 10**6, transcendentals=0),
        name="bias",
    )(table, index)


def enter_kernel(mine_ref, other_ref, gain_ref, x_ref, n_ref, row_ref, col_ref):
    me = lax.axis_index("lon")
    n_lat = lax.axis_size("lat")
    lat = lax.axis_index("lat")
    for k in range(3):
        for ref, l in ((mine_ref, me), (other_ref, 1 - me)):
            tokens = ref[k, 0:WIN, :]
            x_ref[l, WIN * k : WIN * (k + 1), :] = tokens
            n_ref[l, WIN * k : WIN * (k + 1), :] = norm_rows(tokens.astype(F32), gain_ref[0:1, :])
    lanes = lax.broadcasted_iota(jnp.int32, (1, WIN), 1)
    level = lanes & 1
    dh = lanes // (WW * WZ)
    rows = []
    for a in range(2):
        window = (lat + n_lat - 1 + a) % n_lat
        late = window * WH + dh >= n_lat * WH - WH // 2
        extra = jnp.where(level == WZ - 1, 2.0, 0.0) + jnp.where(late, 1.0, 0.0)
        mine = mine_ref[a, WIN : WIN + REGION_ROWS, 0:WIN].astype(F32)[0:1]
        other = other_ref[a, WIN : WIN + REGION_ROWS, 0:WIN].astype(F32)[0:1]
        west = jnp.where(me == 0, mine, other)
        east = jnp.where(me == 0, other, mine)
        rows += [4.0 * west + extra, 4.0 * east + extra]
    tags = jnp.concatenate(rows + rows, axis=0)
    row_ref[...] = tags
    to = lax.broadcasted_iota(jnp.int32, (WIN, WIN), 0)
    frm = lax.broadcasted_iota(jnp.int32, (WIN, WIN), 1)
    col_ref[...] = nt_dot(jnp.where(to == frm, 1.0, 0.0).astype(BF16), tags.astype(BF16))


def enter_call(mine, other, gain):
    return pl.pallas_call(
        enter_kernel,
        out_shape=(
            jax.ShapeDtypeStruct((PAIR, TALL, D), BF16),
            jax.ShapeDtypeStruct((PAIR, TALL, D), BF16),
            jax.ShapeDtypeStruct((8, WIN), F32),
            jax.ShapeDtypeStruct((WIN, 8), F32),
        ),
        cost_estimate=pl.CostEstimate(flops=10**8, bytes_accessed=2 * 10**6, transcendentals=0),
        name="enter",
    )(mine, other, gain)


def join_kernel(n_fsdp, n_lat, own_ref, *refs):
    far, near = refs[: n_fsdp - 1], refs[n_fsdp - 1 : n_fsdp + n_lat - 2]
    qkv_ref, out_ref = refs[-2:]
    z = lax.axis_index("fsdp")
    lat = lax.axis_index("lat")
    depth = own_ref.shape[0]
    part = depth // n_lat

    def put(first, size, piece):
        rows = pl.ds(pl.multiple_of(first, part), size)
        qkv_ref[rows, :] = piece[:, 0:QKV]
        out_ref[rows, :] = piece[:, QKV:COLS]

    put(z * depth, depth, own_ref[...])
    for k in range(1, n_fsdp):
        base = ((z + n_fsdp - k) % n_fsdp) * depth
        put(base + lat * part, part, far[k - 1][...])
        for j in range(1, n_lat):
            giver = (lat + n_lat - j) % n_lat
            put(base + giver * part, part, near[j - 1][part * (k - 1) : part * k, :])


def join_call(own, far, near):
    n_fsdp, n_lat = len(far) + 1, len(near) + 1
    rows = own.shape[0] * n_fsdp
    return pl.pallas_call(
        functools.partial(join_kernel, n_fsdp, n_lat),
        out_shape=(
            jax.ShapeDtypeStruct((rows, QKV), BF16),
            jax.ShapeDtypeStruct((rows, D // PAIR), BF16),
        ),
        cost_estimate=pl.CostEstimate(flops=10**6, bytes_accessed=2 * 10**6, transcendentals=0),
        name="join",
    )(own, *far, *near)


def window_attend(q, k, v, bias_at, allowed, put):
    n = q.shape[0]
    lanes = lax.broadcasted_iota(jnp.int32, (n, 128), 1)
    owns = [(lanes >= HEAD_DIM * j) & (lanes < HEAD_DIM * (j + 1)) for j in range(GROUP)]
    ones = jnp.ones((WIN, 128), BF16)
    for g in range(MINE // 128):
        cols = slice(128 * g, 128 * (g + 1))
        q_g = q[:, cols]
        k_g = k[:, cols]
        v_g = jnp.concatenate([v[:, cols], ones], axis=1)
        q_all = jnp.concatenate([jnp.where(o, q_g, jnp.zeros_like(q_g)) for o in owns], axis=0)
        scores = nt_dot(q_all, k_g)
        probs = []
        for j in range(GROUP):
            s = scores[n * j : n * (j + 1)] * SCALE2 + bias_at(GROUP * g + j)
            if allowed is not None:
                s = jnp.where(allowed, s, NEG)
            peak = jnp.max(s, axis=-1, keepdims=True)
            probs.append(jnp.exp2(s - peak).astype(BF16))
        mixed = nn_dot(jnp.concatenate(probs, axis=0), v_g)
        acc = None
        for j in range(GROUP):
            m = mixed[n * j : n * (j + 1)]
            value = m[:, 0:128] / m[:, 128:256]
            acc = value if acc is None else jnp.where(owns[j], value, acc)
        put(128 * g, acc.astype(BF16))


def project(n, w_ref, q_s, k_s, v_s):
    both = nn_dot(n, w_ref[...]).astype(BF16)
    q_s[...] = both[:, 0:MINE]
    k_s[...] = both[:, MINE : 2 * MINE]
    v_s[...] = both[:, 2 * MINE : 3 * MINE]


def first_kernel(n_ref, w_ref, bias_ref, o_ref, q_s, k_s, v_s):
    project(n_ref[...].reshape(PAIR * TALL, D), w_ref, q_s, k_s, v_s)
    for l in range(PAIR):
        for part, (q0, q1, o0) in enumerate(
            ((KEEP0, WIN, 0), (0, WIN, PART), (0, PART, PART + WIN))
        ):
            t = TALL * l + WIN * part

            def put(col, value, l=l, o0=o0, q0=q0, q1=q1):
                o_ref[l, o0 : o0 + q1 - q0, col : col + 128] = value

            window_attend(
                q_s[t + q0 : t + q1, :],
                k_s[t : t + WIN, :],
                v_s[t : t + WIN, :],
                lambda h, q0=q0, q1=q1: bias_ref[h, q0:q1, :],
                None,
                put,
            )


def first_call(normed, weight, bias):
    scratch = pltpu.VMEM((PAIR * TALL, MINE), BF16)
    return pl.pallas_call(
        first_kernel,
        out_shape=jax.ShapeDtypeStruct((PAIR, KEPT, MINE), BF16),
        scratch_shapes=[scratch, scratch, scratch],
        cost_estimate=pl.CostEstimate(flops=2 * 10**9, bytes_accessed=4 * 10**6, transcendentals=10**6),
        name="first",
    )(normed, weight, bias)


def pair_columns(me, ref, mine, other):
    width = mine.shape[-1]
    ref[:, pl.ds(pl.multiple_of(width * me, width), width)] = mine
    ref[:, pl.ds(pl.multiple_of(width * (1 - me), width), width)] = other


def second_kernel(
    mine_ref, other_ref, wo_mine_ref, wo_other_ref, x_ref, gain_ref, src_ref, w_ref, bias_ref,
    row_ref, col_ref, back_ref, mid_ref, keep_ref, send_ref, o_s, wo_s, m_s, n_s, q_s, k_s, v_s, a_s, t_s,
):
    me = lax.axis_index("lon")
    tokens = PAIR * KEPT
    pair_columns(me, o_s, mine_ref[...].reshape(tokens, MINE), other_ref[...].reshape(tokens, MINE))
    pair_columns(me, wo_s, wo_mine_ref[...], wo_other_ref[...])
    for l in range(PAIR):
        rows = slice(KEPT * l, KEPT * (l + 1))
        value = x_ref[l, KEEP0:KEEP1, :].astype(F32) + nn_dot(o_s[rows, :], wo_s[...])
        value = value.astype(BF16)
        m_s[l] = value
        n_s[rows, :] = norm_rows(value.astype(F32), gain_ref[1:2, :])
    mid_ref[...] = m_s[me, PART : PART + WIN, :]
    windows = nn_dot(one_hot(src_ref[...], tokens), n_s[...]).astype(BF16)
    project(windows, w_ref, q_s, k_s, v_s)
    for w in range(4):
        q0, q1 = (KEEP0, WIN) if w < 2 else (0, PART)
        t = WIN * w
        allowed = col_ref[q0:q1, w : w + 1] == row_ref[w : w + 1, :]

        def put(col, value, w=w):
            a_s[PART * w : PART * (w + 1), col : col + 128] = value

        window_attend(
            q_s[t + q0 : t + q1, :],
            k_s[t : t + WIN, :],
            v_s[t : t + WIN, :],
            lambda h, q0=q0, q1=q1: bias_ref[h, q0:q1, :],
            allowed,
            put,
        )
    tiles = nn_dot(one_hot(back_ref[...], 4 * PART), a_s[...]).astype(BF16)
    t_s[0] = tiles[0:WIN]
    t_s[1] = tiles[WIN : 2 * WIN]
    keep_ref[...] = t_s[me]
    send_ref[...] = t_s[1 - me]


def second_call(mine, other, wo_mine, wo_other, x, gain, weight, bias, row, col):
    tokens = PAIR * KEPT
    qkv = pltpu.VMEM((4 * WIN, MINE), BF16)
    return pl.pallas_call(
        second_kernel,
        out_shape=(
            jax.ShapeDtypeStruct((WIN, D), BF16),
            jax.ShapeDtypeStruct((WIN, MINE), BF16),
            jax.ShapeDtypeStruct((WIN, MINE), BF16),
        ),
        scratch_shapes=[
            pltpu.VMEM((tokens, D), BF16),
            pltpu.VMEM((D, D), BF16),
            pltpu.VMEM((PAIR, KEPT, D), BF16),
            pltpu.VMEM((tokens, D), BF16),
            qkv,
            qkv,
            qkv,
            pltpu.VMEM((4 * PART, MINE), BF16),
            pltpu.VMEM((PAIR, WIN, MINE), BF16),
        ],
        cost_estimate=pl.CostEstimate(flops=2 * 10**9, bytes_accessed=4 * 10**6, transcendentals=10**6),
        name="second",
    )(
        mine, other, wo_mine, wo_other, x, gain, jnp.asarray(window_sources()), weight, bias,
        row, col, jnp.asarray(tile_sources()),
    )


def last_kernel(mid_ref, keep_ref, got_ref, wo_mine_ref, wo_other_ref, out_ref, o_s, wo_s):
    me = lax.axis_index("lon")
    pair_columns(me, o_s, keep_ref[...], got_ref[...])
    pair_columns(me, wo_s, wo_mine_ref[...], wo_other_ref[...])
    value = mid_ref[...].astype(F32) + nn_dot(o_s[...], wo_s[...])
    out_ref[...] = value.astype(BF16)


def last_call(mid, keep, got, wo_mine, wo_other):
    return pl.pallas_call(
        last_kernel,
        out_shape=jax.ShapeDtypeStruct((WIN, D), BF16),
        scratch_shapes=[pltpu.VMEM((WIN, D), BF16), pltpu.VMEM((D, D), BF16)],
        cost_estimate=pl.CostEstimate(flops=10**8, bytes_accessed=10**6, transcendentals=0),
        name="last",
    )(mid, keep, got, wo_mine, wo_other)


def paired(latent, norm_gain, qkv_weight, out_weight, rel_bias, bias_index, region_ids):
    me = lax.axis_index("lon")
    lat = lax.axis_index("lat")
    n_fsdp, n_lat = lax.axis_size("fsdp"), lax.axis_size("lat")
    depth = qkv_weight.shape[1]
    part = depth // n_lat

    def mine_of(w, groups):
        w = w.reshape(2, depth, groups, PAIR, w.shape[2] // groups // PAIR)
        return lax.dynamic_index_in_dim(w, me, 3, keepdims=False).reshape(2, depth, -1)

    own = jnp.concatenate([mine_of(qkv_weight, 3), mine_of(out_weight, 1)], axis=2)
    slices = lax.dynamic_slice_in_dim(own, lat * part, part, 1)

    swap = functools.partial(passed_along, axis="lon", distance=1)
    far = [[passed_along(slices[b], "fsdp", k) for k in range(1, n_fsdp)] for b in range(2)]

    tokens = jnp.transpose(latent[0], (1, 2, 0, 3)).reshape(WIN, D)
    regions = jnp.transpose(region_ids, (1, 2, 0)).reshape(1, WIN).astype(BF16)
    tile = jnp.concatenate(
        [tokens, jnp.pad(regions, ((0, REGION_ROWS - 1), (0, D - WIN)))], axis=0
    )
    tall = jnp.stack([passed_along(tile, "lat", 1), tile, passed_along(tile, "lat", -1)])
    x, normed, tag_row, tag_col = enter_call(tall, swap(tall), norm_gain)
    bias = bias_call(jnp.transpose(rel_bias, (0, 2, 1)), bias_index)

    weights = []
    for b in range(2):
        given = jnp.concatenate(far[b], axis=0)
        near = [passed_along(given, "lat", j) for j in range(1, n_lat)]
        weights.append(join_call(own[b], far[b], near))
    (w0, wo0), (w1, wo1) = weights
    o0 = first_call(normed, w0, bias[0])
    mid, keep, send = second_call(
        o0, swap(o0), wo0, swap(wo0), x, norm_gain, w1, bias[1], tag_row, tag_col
    )
    out = last_call(mid, keep, swap(send), wo1, swap(wo1))
    return jnp.transpose(out.reshape(WH, WW, WZ, D), (2, 0, 1, 3))[None]


def solution(mesh):
    def local(latent, norm_gain, qkv_weight, out_weight, *rest):
        one_window = latent.shape[:4] == (1, WZ, WH, WW)
        even = qkv_weight.shape[1] % (16 * mesh.shape["lat"]) == 0
        pays = mesh.shape["lon"] == PAIR and one_window and even
        program = paired if pays else any_mesh
        return program(latent, norm_gain, qkv_weight, out_weight, *rest)

    return jax.shard_map(
        local,
        mesh=mesh,
        in_specs=(
            P("fsdp", None, "lat", "lon", None),
            P(),
            P(None, "fsdp", None),
            P(None, "fsdp", None),
            P(),
            P(),
            P(None, "lat", "lon"),
        ),
        out_specs=P("fsdp", None, "lat", "lon", None),
        check_vma=False,
    )
```

```python
import functools

import jax
import jax.numpy as jnp
import numpy as np
from jax import lax
from jax.experimental import pallas as pl
from jax.experimental.pallas import tpu as pltpu
from jax.sharding import PartitionSpec as P


D = 512
HEADS = 16
HEAD_DIM = 32
WZ = 2
WH = 6
WW = 12
WIN = 144
BIAS_ROWS = 759
HALF = WIN // 2
LOG2E = 1.4426950408889634
SCALE2 = HEAD_DIM ** (-0.5) * LOG2E
NEG = -1e30


def passed_along(block, axis, distance):
    devices = range(lax.axis_size(axis))
    route = [((i - distance) % len(devices), i) for i in devices]
    return lax.ppermute(block, axis, route)


def layer_norm(hidden, gain_row):
    values = hidden.astype(jnp.float32)
    centre = jnp.mean(values, axis=-1, keepdims=True)
    shifted = values - centre
    variance = jnp.mean(shifted * shifted, axis=-1, keepdims=True)
    return (shifted * lax.rsqrt(variance + 1e-05) * gain_row).astype(jnp.bfloat16)


def bias_table(rel_bias, bias_index, block_index):
    return jnp.take(jnp.transpose(rel_bias[block_index]), bias_index, axis=1)


def split_tile(field_tile):
    sample_count, level_count, row_count, col_count, feature_width = field_tile.shape
    pieces = field_tile.reshape(
        sample_count, level_count // WZ, WZ, row_count // WH, WH, col_count // WW, WW, feature_width
    )
    pieces = jnp.transpose(pieces, (0, 1, 3, 5, 2, 4, 6, 7))
    return pieces.reshape(-1, WIN, feature_width)


def merge_tile(windows, tile_shape):
    sample_count, level_count, row_count, col_count, feature_width = tile_shape
    pieces = windows.reshape(
        sample_count, level_count // WZ, row_count // WH, col_count // WW, WZ, WH, WW, feature_width
    )
    pieces = jnp.transpose(pieces, (0, 1, 4, 2, 5, 3, 6, 7))
    return pieces.reshape(tile_shape)


def attend(normed, weight, bias_heads, region_tags):
    packed = jnp.dot(normed.reshape(-1, D), weight, preferred_element_type=jnp.float32).astype(
        jnp.bfloat16
    )
    packed = split_tile(packed.reshape(normed.shape[:-1] + (3 * D,)))
    packed = packed.reshape(-1, WIN, 3, HEADS, HEAD_DIM)
    scores = jnp.einsum(
        "gqhd,gkhd->ghqk", packed[:, :, 0], packed[:, :, 1], preferred_element_type=jnp.float32
    )
    scores = scores * HEAD_DIM ** (-0.5) + bias_heads[None]
    if region_tags is not None:
        window_tags = split_tile(region_tags[..., None])[..., 0]
        allowed = window_tags[:, :, None] == window_tags[:, None, :]
        blocked = jnp.where(allowed, jnp.float32(0.0), -jnp.inf)
        scores = scores + blocked[:, None]
    row_peak = jnp.max(scores, axis=-1, keepdims=True)
    exponent = jnp.exp(scores - row_peak)
    row_total = jnp.sum(exponent, axis=-1, keepdims=True)
    attn_probs = (exponent / row_total).astype(jnp.bfloat16)
    mixed_out = jnp.einsum(
        "ghqk,gkhd->gqhd", attn_probs, packed[:, :, 2], preferred_element_type=jnp.float32
    )
    return merge_tile(mixed_out.astype(jnp.bfloat16).reshape(-1, WIN, D), normed.shape)


def any_mesh(latent, norm_gain, qkv_weight, out_weight, rel_bias, bias_index, region_ids):
    half_rows = WH // 2
    half_cols = WW // 2
    row_count = latent.shape[2]
    col_count = latent.shape[3]
    gathered_qkv, gathered_out = (
        lax.all_gather(qkv_weight, "fsdp", axis=1, tiled=True),
        lax.all_gather(out_weight, "fsdp", axis=1, tiled=True),
    )

    def fetch_weights(block_index):
        return (gathered_qkv[block_index], gathered_out[block_index])

    first_qkv, first_out = fetch_weights(0)
    normed = layer_norm(latent, norm_gain[0])
    mixed_out = attend(normed, first_qkv, bias_table(rel_bias, bias_index, 0), None)
    projected = jnp.dot(mixed_out.reshape(-1, D), first_out, preferred_element_type=jnp.float32)
    middle = (latent.astype(jnp.float32) + projected.reshape(latent.shape)).astype(jnp.bfloat16)
    second_qkv, second_out = fetch_weights(1)
    normed = jnp.roll(layer_norm(middle, norm_gain[1]), -1, axis=1)
    east_strip = passed_along(normed[:, :, :, :half_cols], "lon", -1)
    widened = jnp.concatenate([normed[:, :, :, half_cols:], east_strip], axis=3)
    north_strip = passed_along(widened[:, :, :half_rows], "lat", -1)
    rolled = jnp.concatenate([widened[:, :, half_rows:], north_strip], axis=2)
    level_pos = lax.broadcasted_iota(jnp.int32, region_ids.shape, 0)
    row_pos = (
        lax.broadcasted_iota(jnp.int32, region_ids.shape, 1) + lax.axis_index("lat") * row_count
    )
    region_tags = region_ids * 4 + (level_pos == region_ids.shape[0] - 1).astype(jnp.int32) * 2
    region_tags = region_tags + (row_pos >= row_count * lax.axis_size("lat") - half_rows).astype(
        jnp.int32
    )
    region_tags = region_tags[None]
    mixed_out = attend(rolled, second_qkv, bias_table(rel_bias, bias_index, 1), region_tags)
    south_strip = passed_along(mixed_out[:, :, row_count - half_rows :], "lat", 1)
    widened = jnp.concatenate([south_strip, mixed_out[:, :, : row_count - half_rows]], axis=2)
    west_strip = passed_along(widened[:, :, :, col_count - half_cols :], "lon", 1)
    mixed_out = jnp.concatenate([west_strip, widened[:, :, :, : col_count - half_cols]], axis=3)
    mixed_out = jnp.roll(mixed_out, 1, axis=1)
    projected = jnp.dot(mixed_out.reshape(-1, D), second_out, preferred_element_type=jnp.float32)
    return (middle.astype(jnp.float32) + projected.reshape(latent.shape)).astype(jnp.bfloat16)


PAIR = 2
MY_HEADS = HEADS // PAIR
MINE = MY_HEADS * HEAD_DIM
QKV = 3 * MINE
OUT = D // PAIR
REST = OUT + QKV + OUT
TALL = 3 * WIN
KEEP0 = 64
KEEP1 = TALL - 64
KEPT = KEEP1 - KEEP0
PART = WIN - KEEP0
REGION_ROWS = 8
GROUP = 128 // HEAD_DIM
F32 = jnp.float32
BF16 = jnp.bfloat16


def vmem(mib):
    return pltpu.CompilerParams(vmem_limit_bytes=mib * 2**20)


def partner(index, step, size):
    if size & (size - 1) == 0:
        return index ^ step
    return (index + size - step) % size


def heard_from(block, axis, step):
    size = lax.axis_size(axis)
    return lax.ppermute(block, axis, [(partner(i, step, size), i) for i in range(size)])


def window_sources():
    src = np.zeros((2, 2, WH, WW, WZ), np.int32)
    for a in range(2):
        for v in range(2):
            for dh in range(WH):
                for dw in range(WW):
                    for dz in range(WZ):
                        row = dh + (WH // 2 if a else -(WH // 2))
                        col = (WW // 2 + WW * v + dw) % (2 * WW)
                        level = (dz + 1) % WZ
                        t = (row + WH) * WW * WZ + (col % WW) * WZ + level
                        src[a, v, dh, dw, dz] = (col // WW) * KEPT + t - KEEP0
    return src.reshape(-1, 1)


def tile_sources():
    src = np.zeros((2, WH, WW, WZ), np.int32)
    for l in range(2):
        for row in range(WH):
            for cw in range(WW):
                for level in range(WZ):
                    a = 0 if row < WH // 2 else 1
                    dh = (row + WH // 2) % WH
                    col = (WW * l + cw - WW // 2) % (2 * WW)
                    dz = (level - 1) % WZ
                    t = dh * WW * WZ + (col % WW) * WZ + dz - (0 if a else KEEP0)
                    src[l, row, cw, level] = (a * 2 + col // WW) * PART + t
    return src.reshape(-1, 1)


def one_hot(sources, width):
    lanes = lax.broadcasted_iota(jnp.int32, (sources.shape[0], width), 1)
    return jnp.where(lanes == sources, 1.0, 0.0).astype(BF16)


def nt_dot(a, b):
    return lax.dot_general(a, b, (((1,), (1,)), ((), ())), preferred_element_type=F32)


def nn_dot(a, b):
    return jnp.dot(a, b, preferred_element_type=F32)


def norm_rows(values, gain_row):
    centre = jnp.mean(values, axis=-1, keepdims=True)
    shifted = values - centre
    variance = jnp.mean(shifted * shifted, axis=-1, keepdims=True)
    return (shifted * lax.rsqrt(variance + 1e-05) * gain_row).astype(BF16)


def bias_kernel(table_ref, index_ref, first_ref, second_ref, table, index):
    me = lax.axis_index("lon")
    for b in range(2):
        heads = table_ref[b, pl.ds(pl.multiple_of(MY_HEADS * me, MY_HEADS), MY_HEADS), :]
        table[b, :, 0:BIAS_ROWS] = heads * LOG2E
    to = lax.broadcasted_iota(jnp.int32, (WIN, WIN), 0)
    frm = lax.broadcasted_iota(jnp.int32, (WIN, WIN), 1)
    move = jnp.where((to & 1) * HALF + (to >> 1) == frm, 1.0, 0.0).astype(BF16)

    def moved(a):
        a = nn_dot(move, a.astype(F32).astype(BF16)).astype(BF16)
        return nt_dot(a, move).astype(jnp.int32)

    whole = index_ref[...]
    index[:, 0:WIN] = moved(whole >> 8) * 256 + moved(whole & 255)
    outs = (first_ref, second_ref)
    chunks = (BIAS_ROWS + 127) // 128

    def step(g, carry):
        rows = pl.ds(pl.multiple_of(g * 8, 8), 8)
        for lo, hi in ((0, 128), (128, WIN)):
            at = index[rows, lo : lo + 128]
            low = at & 127
            chunk = at >> 7
            masks = [chunk == k for k in range(chunks)]
            for b in range(2):
                for h in range(MY_HEADS):
                    acc = None
                    for k in range(chunks):
                        row = jnp.broadcast_to(
                            table[b, h : h + 1, 128 * k : 128 * k + 128], (8, 128)
                        )
                        got = jnp.take_along_axis(row, low, axis=1, mode="promise_in_bounds")
                        acc = got if acc is None else jnp.where(masks[k], got, acc)
                    outs[b][h, rows, lo:hi] = acc[:, : hi - lo]
        return carry

    lax.fori_loop(0, WIN // 8, step, 0)


def bias_call(table, index):
    out = jax.ShapeDtypeStruct((MY_HEADS, WIN, WIN), F32)
    return pl.pallas_call(
        bias_kernel,
        out_shape=(out, out),
        scratch_shapes=[
            pltpu.VMEM((2, MY_HEADS, (BIAS_ROWS + 127) // 128 * 128), F32),
            pltpu.VMEM((WIN, 256), jnp.int32),
        ],
        compiler_params=vmem(8),
        cost_estimate=pl.CostEstimate(flops=10**9, bytes_accessed=2 * 10**6, transcendentals=0),
        name="bias",
    )(table, index)


def tile_kernel(latent_ref, region_ref, tile_ref):
    tile_ref[0:WIN, :] = latent_ref[...].reshape(WIN, D)
    col = lax.broadcasted_iota(jnp.int32, (WW, WIN), 0)
    token = lax.broadcasted_iota(jnp.int32, (WW, WIN), 1)
    spread = jnp.where(token % (WW * WZ) // WZ == col, 1.0, 0.0).astype(BF16)
    level = lax.broadcasted_iota(jnp.int32, (WZ, WIN), 0)
    token = lax.broadcasted_iota(jnp.int32, (WZ, WIN), 1)
    total = jnp.zeros((WZ, WIN), F32)
    for dh in range(WH):
        here = (token // (WW * WZ) == dh) & (token % WZ == level)
        total += jnp.where(here, nn_dot(region_ref[dh].astype(F32).astype(BF16), spread), 0.0)
    regions = jnp.sum(total, axis=0, keepdims=True)
    tile_ref[WIN : WIN + REGION_ROWS, 0:WIN] = jnp.broadcast_to(regions, (REGION_ROWS, WIN)).astype(BF16)
    tile_ref[WIN : WIN + REGION_ROWS, WIN:D] = jnp.zeros((REGION_ROWS, D - WIN), BF16)


def tile_call(latent, regions):
    return pl.pallas_call(
        tile_kernel,
        out_shape=jax.ShapeDtypeStruct((WIN + REGION_ROWS, D), BF16),
        compiler_params=vmem(4),
        cost_estimate=pl.CostEstimate(flops=10**6, bytes_accessed=3 * 10**5, transcendentals=0),
        name="tile",
    )(latent, regions)


def fetch(copies):
    for copy in copies:
        copy.start()
    for copy in copies:
        copy.wait()


def first_columns(qkv_ref, rows, me, dst, sems):
    return [
        pltpu.make_async_copy(
            qkv_ref.at[0, rows, pl.ds(pl.multiple_of(D * k + MINE * me, MINE), MINE)],
            dst.at[:, pl.ds(MINE * k, MINE)],
            sems.at[k],
        )
        for k in range(3)
    ]


def rest_columns(qkv_ref, out_ref, rows, me, dst, sems):
    mine = pl.ds(pl.multiple_of(MINE * me, MINE), MINE)
    outs = [
        pltpu.make_async_copy(out_ref.at[b, rows, mine], dst.at[:, pl.ds(at, OUT)], sems.at[b])
        for b, at in ((0, 0), (1, OUT + QKV))
    ]
    return outs + [
        pltpu.make_async_copy(
            qkv_ref.at[1, rows, pl.ds(pl.multiple_of(D * k + MINE * me, MINE), MINE)],
            dst.at[:, pl.ds(OUT + MINE * k, MINE)],
            sems.at[2 + k],
        )
        for k in range(3)
    ]


def cut_first_kernel(qkv_ref, part_ref, sems):
    part = part_ref.shape[0]
    rows = pl.ds(pl.multiple_of(lax.axis_index("lat") * part, part), part)
    fetch(first_columns(qkv_ref, rows, lax.axis_index("lon"), part_ref, sems))


def cut_rest_kernel(qkv_ref, out_ref, part_ref, own0_ref, own1_ref, sems):
    part, depth = part_ref.shape[0], own0_ref.shape[0]
    me = lax.axis_index("lon")
    rows = pl.ds(pl.multiple_of(lax.axis_index("lat") * part, part), part)
    every = pl.ds(0, depth)
    fetch(
        rest_columns(qkv_ref, out_ref, rows, me, part_ref, sems.at[0])
        + rest_columns(qkv_ref, out_ref, every, me, own1_ref, sems.at[1])
        + first_columns(qkv_ref, every, me, own0_ref, sems.at[2])
    )


ANYWHERE = pl.BlockSpec(memory_space=pl.ANY)


def cut_first_call(qkv, part):
    return pl.pallas_call(
        cut_first_kernel,
        out_shape=jax.ShapeDtypeStruct((part, QKV), BF16),
        in_specs=[ANYWHERE],
        scratch_shapes=[pltpu.SemaphoreType.DMA((3,))],
        compiler_params=vmem(4),
        cost_estimate=pl.CostEstimate(flops=0, bytes_accessed=10**5, transcendentals=0),
        name="cut_first",
    )(qkv)


def cut_rest_call(qkv, out, part):
    depth = qkv.shape[1]
    return pl.pallas_call(
        cut_rest_kernel,
        out_shape=(
            jax.ShapeDtypeStruct((part, REST), BF16),
            jax.ShapeDtypeStruct((depth, QKV), BF16),
            jax.ShapeDtypeStruct((depth, REST), BF16),
        ),
        in_specs=[ANYWHERE, ANYWHERE],
        scratch_shapes=[pltpu.SemaphoreType.DMA((3, 5))],
        compiler_params=vmem(4),
        cost_estimate=pl.CostEstimate(flops=0, bytes_accessed=10**6, transcendentals=0),
        name="cut_rest",
    )(qkv, out)


def enter_kernel(mine_ref, other_ref, gain_ref, x_ref, n_ref, row_ref, col_ref):
    me = lax.axis_index("lon")
    n_lat = lax.axis_size("lat")
    lat = lax.axis_index("lat")
    for k in range(3):
        for ref, l in ((mine_ref, me), (other_ref, 1 - me)):
            tokens = ref[k, 0:WIN, :]
            x_ref[l, WIN * k : WIN * (k + 1), :] = tokens
            n_ref[l, WIN * k : WIN * (k + 1), :] = norm_rows(tokens.astype(F32), gain_ref[0:1, :])
    lanes = lax.broadcasted_iota(jnp.int32, (1, WIN), 1)
    level = lanes & 1
    dh = lanes // (WW * WZ)
    rows = []
    for a in range(2):
        window = (lat + n_lat - 1 + a) % n_lat
        late = window * WH + dh >= n_lat * WH - WH // 2
        extra = jnp.where(level == WZ - 1, 2.0, 0.0) + jnp.where(late, 1.0, 0.0)
        mine = mine_ref[a, WIN : WIN + REGION_ROWS, 0:WIN].astype(F32)[0:1]
        other = other_ref[a, WIN : WIN + REGION_ROWS, 0:WIN].astype(F32)[0:1]
        west = jnp.where(me == 0, mine, other)
        east = jnp.where(me == 0, other, mine)
        rows += [4.0 * west + extra, 4.0 * east + extra]
    tags = jnp.concatenate(rows + rows, axis=0)
    row_ref[...] = tags
    to = lax.broadcasted_iota(jnp.int32, (WIN, WIN), 0)
    frm = lax.broadcasted_iota(jnp.int32, (WIN, WIN), 1)
    col_ref[...] = nt_dot(jnp.where(to == frm, 1.0, 0.0).astype(BF16), tags.astype(BF16))


def enter_call(mine, other, gain):
    return pl.pallas_call(
        enter_kernel,
        out_shape=(
            jax.ShapeDtypeStruct((PAIR, TALL, D), BF16),
            jax.ShapeDtypeStruct((PAIR, TALL, D), BF16),
            jax.ShapeDtypeStruct((8, WIN), F32),
            jax.ShapeDtypeStruct((WIN, 8), F32),
        ),
        compiler_params=vmem(16),
        cost_estimate=pl.CostEstimate(flops=10**8, bytes_accessed=2 * 10**6, transcendentals=0),
        name="enter",
    )(mine, other, gain)


def place(put, own, far, near):
    n_fsdp, n_lat = len(far) + 1, len(near) + 1
    z, lat = lax.axis_index("fsdp"), lax.axis_index("lat")
    depth = own.shape[0]
    part = depth // n_lat
    put(pl.multiple_of(z * depth, depth), depth, own[...])
    for k in range(1, n_fsdp):
        base = partner(z, k, n_fsdp) * depth
        put(pl.multiple_of(base + lat * part, part), part, far[k - 1][...])
        for j in range(1, n_lat):
            row = pl.multiple_of(base + partner(lat, j, n_lat) * part, part)
            put(row, part, near[j - 1][part * (k - 1) : part * k, :])


def join_kernel(n_far, n_near, own, *refs):
    far, near = refs[:n_far], refs[n_far : n_far + n_near]
    wo0_ref, qkv_ref, wo1_ref = refs[n_far + n_near :]

    def put(first, size, piece):
        rows = pl.ds(first, size)
        wo0_ref[rows, :] = piece[:, 0:OUT]
        qkv_ref[rows, :] = piece[:, OUT : OUT + QKV]
        wo1_ref[rows, :] = piece[:, OUT + QKV : REST]

    place(put, own, far, near)


def join_call(own, far, near):
    rows = own.shape[0] * (len(far) + 1)
    half = jax.ShapeDtypeStruct((rows, OUT), BF16)
    return pl.pallas_call(
        functools.partial(join_kernel, len(far), len(near)),
        out_shape=(half, jax.ShapeDtypeStruct((rows, QKV), BF16), half),
        compiler_params=vmem(8),
        cost_estimate=pl.CostEstimate(flops=10**6, bytes_accessed=2 * 10**6, transcendentals=0),
        name="join",
    )(own, *far, *near)


def window_attend(q, k, v, bias_at, allowed, put):
    n = q.shape[0]
    lanes = lax.broadcasted_iota(jnp.int32, (n, 128), 1)
    owns = [(lanes >= HEAD_DIM * j) & (lanes < HEAD_DIM * (j + 1)) for j in range(GROUP)]
    ones = jnp.ones((WIN, 128), BF16)
    for g in range(MINE // 128):
        cols = slice(128 * g, 128 * (g + 1))
        q_g = q[:, cols]
        k_g = k[:, cols]
        v_g = jnp.concatenate([v[:, cols], ones], axis=1)
        q_all = jnp.concatenate([jnp.where(o, q_g, jnp.zeros_like(q_g)) for o in owns], axis=0)
        scores = nt_dot(q_all, k_g)
        probs = []
        for j in range(GROUP):
            s = scores[n * j : n * (j + 1)] * SCALE2 + bias_at(GROUP * g + j)
            if allowed is not None:
                s = jnp.where(allowed, s, NEG)
            peak = jnp.max(s, axis=-1, keepdims=True)
            probs.append(jnp.exp2(s - peak).astype(BF16))
        mixed = nn_dot(jnp.concatenate(probs, axis=0), v_g)
        acc = None
        for j in range(GROUP):
            m = mixed[n * j : n * (j + 1)]
            value = m[:, 0:128] / m[:, 128:256]
            acc = value if acc is None else jnp.where(owns[j], value, acc)
        put(128 * g, acc.astype(BF16))


def project(n, w_ref, q_s, k_s, v_s):
    both = nn_dot(n, w_ref[...]).astype(BF16)
    q_s[...] = both[:, 0:MINE]
    k_s[...] = both[:, MINE : 2 * MINE]
    v_s[...] = both[:, 2 * MINE : 3 * MINE]


def first_kernel(n_far, n_near, n_ref, bias_ref, own, *refs):
    far, near = refs[:n_far], refs[n_far : n_far + n_near]
    o_ref, w_s, q_s, k_s, v_s = refs[n_far + n_near :]

    def join(first, size, piece):
        w_s[pl.ds(first, size), :] = piece

    place(join, own, far, near)
    project(n_ref[...].reshape(PAIR * TALL, D), w_s, q_s, k_s, v_s)
    for l in range(PAIR):
        for part, (q0, q1, o0) in enumerate(
            ((KEEP0, WIN, 0), (0, WIN, PART), (0, PART, PART + WIN))
        ):
            t = TALL * l + WIN * part

            def put(col, value, l=l, o0=o0, q0=q0, q1=q1):
                o_ref[l, o0 : o0 + q1 - q0, col : col + 128] = value

            window_attend(
                q_s[t + q0 : t + q1, :],
                k_s[t : t + WIN, :],
                v_s[t : t + WIN, :],
                lambda h, q0=q0, q1=q1: bias_ref[h, q0:q1, :],
                None,
                put,
            )


def first_call(normed, bias, own, far, near):
    scratch = pltpu.VMEM((PAIR * TALL, MINE), BF16)
    return pl.pallas_call(
        functools.partial(first_kernel, len(far), len(near)),
        out_shape=jax.ShapeDtypeStruct((PAIR, KEPT, MINE), BF16),
        scratch_shapes=[pltpu.VMEM((D, QKV), BF16), scratch, scratch, scratch],
        compiler_params=vmem(24),
        cost_estimate=pl.CostEstimate(flops=2 * 10**9, bytes_accessed=4 * 10**6, transcendentals=10**6),
        name="first",
    )(normed, bias, own, *far, *near)


def pair_columns(me, ref, mine, other):
    width = mine.shape[-1]
    ref[:, pl.ds(pl.multiple_of(width * me, width), width)] = mine
    ref[:, pl.ds(pl.multiple_of(width * (1 - me), width), width)] = other


def second_kernel(
    mine_ref, other_ref, wo_mine_ref, wo_other_ref, x_ref, gain_ref, src_ref, w_ref, bias_ref,
    row_ref, col_ref, back_ref, mid_ref, keep_ref, send_ref, o_s, wo_s, m_s, n_s, q_s, k_s, v_s, a_s, t_s,
):
    me = lax.axis_index("lon")
    tokens = PAIR * KEPT
    pair_columns(me, o_s, mine_ref[...].reshape(tokens, MINE), other_ref[...].reshape(tokens, MINE))
    pair_columns(me, wo_s, wo_mine_ref[...], wo_other_ref[...])
    for l in range(PAIR):
        rows = slice(KEPT * l, KEPT * (l + 1))
        value = x_ref[l, KEEP0:KEEP1, :].astype(F32) + nn_dot(o_s[rows, :], wo_s[...])
        value = value.astype(BF16)
        m_s[l] = value
        n_s[rows, :] = norm_rows(value.astype(F32), gain_ref[1:2, :])
    mid_ref[...] = m_s[me, PART : PART + WIN, :]
    windows = nn_dot(one_hot(src_ref[...], tokens), n_s[...]).astype(BF16)
    project(windows, w_ref, q_s, k_s, v_s)
    for w in range(4):
        q0, q1 = (KEEP0, WIN) if w < 2 else (0, PART)
        t = WIN * w
        allowed = col_ref[q0:q1, w : w + 1] == row_ref[w : w + 1, :]

        def put(col, value, w=w):
            a_s[PART * w : PART * (w + 1), col : col + 128] = value

        window_attend(
            q_s[t + q0 : t + q1, :],
            k_s[t : t + WIN, :],
            v_s[t : t + WIN, :],
            lambda h, q0=q0, q1=q1: bias_ref[h, q0:q1, :],
            allowed,
            put,
        )
    tiles = nn_dot(one_hot(back_ref[...], 4 * PART), a_s[...]).astype(BF16)
    t_s[0] = tiles[0:WIN]
    t_s[1] = tiles[WIN : 2 * WIN]
    keep_ref[...] = t_s[me]
    send_ref[...] = t_s[1 - me]


def second_call(mine, other, wo_mine, wo_other, x, gain, weight, bias, row, col):
    tokens = PAIR * KEPT
    qkv = pltpu.VMEM((4 * WIN, MINE), BF16)
    return pl.pallas_call(
        second_kernel,
        out_shape=(
            jax.ShapeDtypeStruct((WIN, D), BF16),
            jax.ShapeDtypeStruct((WIN, MINE), BF16),
            jax.ShapeDtypeStruct((WIN, MINE), BF16),
        ),
        scratch_shapes=[
            pltpu.VMEM((tokens, D), BF16),
            pltpu.VMEM((D, D), BF16),
            pltpu.VMEM((PAIR, KEPT, D), BF16),
            pltpu.VMEM((tokens, D), BF16),
            qkv,
            qkv,
            qkv,
            pltpu.VMEM((4 * PART, MINE), BF16),
            pltpu.VMEM((PAIR, WIN, MINE), BF16),
        ],
        compiler_params=vmem(24),
        cost_estimate=pl.CostEstimate(flops=2 * 10**9, bytes_accessed=4 * 10**6, transcendentals=10**6),
        name="second",
    )(
        mine, other, wo_mine, wo_other, x, gain, jnp.asarray(window_sources()), weight, bias,
        row, col, jnp.asarray(tile_sources()),
    )


def last_kernel(mid_ref, keep_ref, got_ref, wo_mine_ref, wo_other_ref, out_ref, o_s, wo_s):
    me = lax.axis_index("lon")
    pair_columns(me, o_s, keep_ref[...], got_ref[...])
    pair_columns(me, wo_s, wo_mine_ref[...], wo_other_ref[...])
    value = mid_ref[...].astype(F32) + nn_dot(o_s[...], wo_s[...])
    out_ref[...] = value.reshape(WIN // WZ, WZ, D).astype(BF16)


def last_call(mid, keep, got, wo_mine, wo_other):
    return pl.pallas_call(
        last_kernel,
        out_shape=jax.ShapeDtypeStruct((WIN // WZ, WZ, D), BF16),
        scratch_shapes=[pltpu.VMEM((WIN, D), BF16), pltpu.VMEM((D, D), BF16)],
        compiler_params=vmem(8),
        cost_estimate=pl.CostEstimate(flops=10**8, bytes_accessed=10**6, transcendentals=0),
        name="last",
    )(mid, keep, got, wo_mine, wo_other)


def paired(latent, norm_gain, qkv_weight, out_weight, rel_bias, bias_index, region_ids):
    n_lat = lax.axis_size("lat")
    part = qkv_weight.shape[1] // n_lat

    def swap(block):
        return passed_along(block, "lon", 1)

    def spread(block, axis):
        got = []
        for k in range(1, lax.axis_size(axis)):
            got.append(heard_from(block, axis, k))
        return got

    far0 = spread(cut_first_call(qkv_weight, part), "fsdp")
    tile = tile_call(
        jnp.transpose(latent[0], (1, 2, 0, 3)).reshape(WIN // WZ, WZ, D),
        jnp.transpose(region_ids, (1, 0, 2)),
    )
    before = passed_along(tile, "lat", 1)
    after = passed_along(tile, "lat", -1)
    cut, own0, own1 = cut_rest_call(qkv_weight, out_weight, part)
    far1 = spread(cut, "fsdp")
    near0 = spread(jnp.concatenate(far0, axis=0), "lat")
    near1 = spread(jnp.concatenate(far1, axis=0), "lat")
    tall = jnp.stack([before, tile, after])
    x, normed, tag_row, tag_col = enter_call(tall, swap(tall), norm_gain)
    bias = bias_call(jnp.transpose(rel_bias, (0, 2, 1)), bias_index)
    o0 = first_call(normed, bias[0], own0, far0, near0)
    wo0, w1, wo1 = join_call(own1, far1, near1)
    mid, keep, send = second_call(
        o0, swap(o0), wo0, swap(wo0), x, norm_gain, w1, bias[1], tag_row, tag_col
    )
    out = last_call(mid, keep, swap(send), wo1, swap(wo1))
    return jnp.transpose(out.reshape(WH, WW, WZ, D), (2, 0, 1, 3))[None]


def solution(mesh):
    pair = mesh.shape["lon"] == PAIR

    def local(latent, norm_gain, qkv_weight, out_weight, *rest):
        one_window = latent.shape[:4] == (1, WZ, WH, WW)
        even = qkv_weight.shape[1] % (16 * mesh.shape["lat"]) == 0
        program = paired if pair and one_window and even else any_mesh
        return program(latent, norm_gain, qkv_weight, out_weight, *rest)

    return jax.shard_map(
        local,
        mesh=mesh,
        in_specs=(
            P("fsdp", None, "lat", "lon", None),
            P(),
            P(None, "fsdp", None),
            P(None, "fsdp", None),
            P(),
            P(),
            P(None, "lat", "lon"),
        ),
        out_specs=P("fsdp", None, "lat", "lon", None),
        check_vma=False,
    )
```

```python
import functools

import jax
import jax.numpy as jnp
import numpy as np
from jax import lax
from jax.experimental import pallas as pl
from jax.experimental.pallas import tpu as pltpu
from jax.sharding import PartitionSpec as P


D = 512
HEADS = 16
HEAD_DIM = 32
WZ = 2
WH = 6
WW = 12
WIN = 144
BIAS_ROWS = 759
HALF = WIN // 2
LOG2E = 1.4426950408889634
SCALE2 = HEAD_DIM ** (-0.5) * LOG2E
NEG = -1e30


def passed_along(block, axis, distance):
    devices = range(lax.axis_size(axis))
    route = [((i - distance) % len(devices), i) for i in devices]
    return lax.ppermute(block, axis, route)


def layer_norm(hidden, gain_row):
    values = hidden.astype(jnp.float32)
    centre = jnp.mean(values, axis=-1, keepdims=True)
    shifted = values - centre
    variance = jnp.mean(shifted * shifted, axis=-1, keepdims=True)
    return (shifted * lax.rsqrt(variance + 1e-05) * gain_row).astype(jnp.bfloat16)


def bias_table(rel_bias, bias_index, block_index):
    return jnp.take(jnp.transpose(rel_bias[block_index]), bias_index, axis=1)


def split_tile(field_tile):
    sample_count, level_count, row_count, col_count, feature_width = field_tile.shape
    pieces = field_tile.reshape(
        sample_count, level_count // WZ, WZ, row_count // WH, WH, col_count // WW, WW, feature_width
    )
    pieces = jnp.transpose(pieces, (0, 1, 3, 5, 2, 4, 6, 7))
    return pieces.reshape(-1, WIN, feature_width)


def merge_tile(windows, tile_shape):
    sample_count, level_count, row_count, col_count, feature_width = tile_shape
    pieces = windows.reshape(
        sample_count, level_count // WZ, row_count // WH, col_count // WW, WZ, WH, WW, feature_width
    )
    pieces = jnp.transpose(pieces, (0, 1, 4, 2, 5, 3, 6, 7))
    return pieces.reshape(tile_shape)


def attend(normed, weight, bias_heads, region_tags):
    packed = jnp.dot(normed.reshape(-1, D), weight, preferred_element_type=jnp.float32).astype(
        jnp.bfloat16
    )
    packed = split_tile(packed.reshape(normed.shape[:-1] + (3 * D,)))
    packed = packed.reshape(-1, WIN, 3, HEADS, HEAD_DIM)
    scores = jnp.einsum(
        "gqhd,gkhd->ghqk", packed[:, :, 0], packed[:, :, 1], preferred_element_type=jnp.float32
    )
    scores = scores * HEAD_DIM ** (-0.5) + bias_heads[None]
    if region_tags is not None:
        window_tags = split_tile(region_tags[..., None])[..., 0]
        allowed = window_tags[:, :, None] == window_tags[:, None, :]
        blocked = jnp.where(allowed, jnp.float32(0.0), -jnp.inf)
        scores = scores + blocked[:, None]
    row_peak = jnp.max(scores, axis=-1, keepdims=True)
    exponent = jnp.exp(scores - row_peak)
    row_total = jnp.sum(exponent, axis=-1, keepdims=True)
    attn_probs = (exponent / row_total).astype(jnp.bfloat16)
    mixed_out = jnp.einsum(
        "ghqk,gkhd->gqhd", attn_probs, packed[:, :, 2], preferred_element_type=jnp.float32
    )
    return merge_tile(mixed_out.astype(jnp.bfloat16).reshape(-1, WIN, D), normed.shape)


def any_mesh(latent, norm_gain, qkv_weight, out_weight, rel_bias, bias_index, region_ids):
    half_rows = WH // 2
    half_cols = WW // 2
    row_count = latent.shape[2]
    col_count = latent.shape[3]
    gathered_qkv, gathered_out = (
        lax.all_gather(qkv_weight, "fsdp", axis=1, tiled=True),
        lax.all_gather(out_weight, "fsdp", axis=1, tiled=True),
    )

    def fetch_weights(block_index):
        return (gathered_qkv[block_index], gathered_out[block_index])

    first_qkv, first_out = fetch_weights(0)
    normed = layer_norm(latent, norm_gain[0])
    mixed_out = attend(normed, first_qkv, bias_table(rel_bias, bias_index, 0), None)
    projected = jnp.dot(mixed_out.reshape(-1, D), first_out, preferred_element_type=jnp.float32)
    middle = (latent.astype(jnp.float32) + projected.reshape(latent.shape)).astype(jnp.bfloat16)
    second_qkv, second_out = fetch_weights(1)
    normed = jnp.roll(layer_norm(middle, norm_gain[1]), -1, axis=1)
    east_strip = passed_along(normed[:, :, :, :half_cols], "lon", -1)
    widened = jnp.concatenate([normed[:, :, :, half_cols:], east_strip], axis=3)
    north_strip = passed_along(widened[:, :, :half_rows], "lat", -1)
    rolled = jnp.concatenate([widened[:, :, half_rows:], north_strip], axis=2)
    level_pos = lax.broadcasted_iota(jnp.int32, region_ids.shape, 0)
    row_pos = (
        lax.broadcasted_iota(jnp.int32, region_ids.shape, 1) + lax.axis_index("lat") * row_count
    )
    region_tags = region_ids * 4 + (level_pos == region_ids.shape[0] - 1).astype(jnp.int32) * 2
    region_tags = region_tags + (row_pos >= row_count * lax.axis_size("lat") - half_rows).astype(
        jnp.int32
    )
    region_tags = region_tags[None]
    mixed_out = attend(rolled, second_qkv, bias_table(rel_bias, bias_index, 1), region_tags)
    south_strip = passed_along(mixed_out[:, :, row_count - half_rows :], "lat", 1)
    widened = jnp.concatenate([south_strip, mixed_out[:, :, : row_count - half_rows]], axis=2)
    west_strip = passed_along(widened[:, :, :, col_count - half_cols :], "lon", 1)
    mixed_out = jnp.concatenate([west_strip, widened[:, :, :, : col_count - half_cols]], axis=3)
    mixed_out = jnp.roll(mixed_out, 1, axis=1)
    projected = jnp.dot(mixed_out.reshape(-1, D), second_out, preferred_element_type=jnp.float32)
    return (middle.astype(jnp.float32) + projected.reshape(latent.shape)).astype(jnp.bfloat16)


PAIR = 2
MY_HEADS = HEADS // PAIR
MINE = MY_HEADS * HEAD_DIM
QKV = 3 * MINE
OUT = D // PAIR
COLS = QKV + OUT
TALL = 3 * WIN
KEEP0 = 64
KEEP1 = TALL - 64
KEPT = KEEP1 - KEEP0
PART = WIN - KEEP0
REGION_ROWS = 8
GROUP = 128 // HEAD_DIM
F32 = jnp.float32
BF16 = jnp.bfloat16


def vmem(mib):
    return pltpu.CompilerParams(vmem_limit_bytes=mib * 2**20)


def partner(index, step, size):
    if size & (size - 1) == 0:
        return index ^ step
    return (index + size - step) % size


def heard_from(block, axis, step):
    size = lax.axis_size(axis)
    return lax.ppermute(block, axis, [(partner(i, step, size), i) for i in range(size)])


def window_sources():
    src = np.zeros((2, 2, WH, WW, WZ), np.int32)
    for a in range(2):
        for v in range(2):
            for dh in range(WH):
                for dw in range(WW):
                    for dz in range(WZ):
                        row = dh + (WH // 2 if a else -(WH // 2))
                        col = (WW // 2 + WW * v + dw) % (2 * WW)
                        level = (dz + 1) % WZ
                        t = (row + WH) * WW * WZ + (col % WW) * WZ + level
                        src[a, v, dh, dw, dz] = (col // WW) * KEPT + t - KEEP0
    return src.reshape(-1, 1)


def tile_sources():
    src = np.zeros((2, WH, WW, WZ), np.int32)
    for l in range(2):
        for row in range(WH):
            for cw in range(WW):
                for level in range(WZ):
                    a = 0 if row < WH // 2 else 1
                    dh = (row + WH // 2) % WH
                    col = (WW * l + cw - WW // 2) % (2 * WW)
                    dz = (level - 1) % WZ
                    t = dh * WW * WZ + (col % WW) * WZ + dz - (0 if a else KEEP0)
                    src[l, row, cw, level] = (a * 2 + col // WW) * PART + t
    return src.reshape(-1, 1)


def one_hot(sources, width):
    lanes = lax.broadcasted_iota(jnp.int32, (sources.shape[0], width), 1)
    return jnp.where(lanes == sources, 1.0, 0.0).astype(BF16)


def nt_dot(a, b):
    return lax.dot_general(a, b, (((1,), (1,)), ((), ())), preferred_element_type=F32)


def nn_dot(a, b):
    return jnp.dot(a, b, preferred_element_type=F32)


def norm_rows(values, gain_row):
    centre = jnp.mean(values, axis=-1, keepdims=True)
    shifted = values - centre
    variance = jnp.mean(shifted * shifted, axis=-1, keepdims=True)
    return (shifted * lax.rsqrt(variance + 1e-05) * gain_row).astype(BF16)


def bias_kernel(b, table_ref, index_ref, bias_ref, table, index):
    me = lax.axis_index("lon")
    heads = table_ref[b, pl.ds(pl.multiple_of(MY_HEADS * me, MY_HEADS), MY_HEADS), :]
    table[:, 0:BIAS_ROWS] = heads * LOG2E
    to = lax.broadcasted_iota(jnp.int32, (WIN, WIN), 0)
    frm = lax.broadcasted_iota(jnp.int32, (WIN, WIN), 1)
    move = jnp.where((to & 1) * HALF + (to >> 1) == frm, 1.0, 0.0).astype(BF16)

    def moved(a):
        a = nn_dot(move, a.astype(F32).astype(BF16)).astype(BF16)
        return nt_dot(a, move).astype(jnp.int32)

    whole = index_ref[...]
    index[:, 0:WIN] = moved(whole >> 8) * 256 + moved(whole & 255)
    index[:, WIN:256] = jnp.zeros((WIN, 256 - WIN), jnp.int32)
    chunks = (BIAS_ROWS + 127) // 128

    def step(g, carry):
        rows = pl.ds(pl.multiple_of(g * 8, 8), 8)
        for lo, hi in ((0, 128), (128, WIN)):
            at = index[rows, lo : lo + 128]
            low = at & 127
            chunk = at >> 7
            masks = [chunk == k for k in range(chunks)]
            for h in range(MY_HEADS):
                acc = None
                for k in range(chunks):
                    row = jnp.broadcast_to(table[h : h + 1, 128 * k : 128 * k + 128], (8, 128))
                    got = jnp.take_along_axis(row, low, axis=1, mode="promise_in_bounds")
                    acc = got if acc is None else jnp.where(masks[k], got, acc)
                bias_ref[h, rows, lo:hi] = acc[:, : hi - lo]
        return carry

    lax.fori_loop(0, WIN // 8, step, 0)


def bias_call(b, table, index):
    return pl.pallas_call(
        functools.partial(bias_kernel, b),
        out_shape=jax.ShapeDtypeStruct((MY_HEADS, WIN, WIN), F32),
        scratch_shapes=[
            pltpu.VMEM((MY_HEADS, (BIAS_ROWS + 127) // 128 * 128), F32),
            pltpu.VMEM((WIN, 256), jnp.int32),
        ],
        compiler_params=vmem(8),
        cost_estimate=pl.CostEstimate(flops=10**9, bytes_accessed=10**6, transcendentals=0),
    )(table, index)


def columns(qkv_ref, out_ref, b, rows, me, dst, at, sems):
    mine = pl.ds(pl.multiple_of(MINE * me, MINE), MINE)
    sources = [
        qkv_ref.at[b, rows, pl.ds(pl.multiple_of(D * k + MINE * me, MINE), MINE)] for k in range(3)
    ]
    sources += [out_ref.at[b, rows, mine]]
    to = pl.ds(at, rows.size)
    return [
        pltpu.make_async_copy(source, dst.at[to, pl.ds(MINE * k, MINE)], sems.at[k])
        for k, source in enumerate(sources)
    ]


def open_kernel(
    wide, latent_ref, region_ref, qkv_ref, out_ref, part0_ref, part1_ref, tile_ref,
    latent, regions, sems, own_sems,
):
    part = part0_ref.shape[0]
    me, lat = lax.axis_index("lon"), lax.axis_index("lat")

    def cut(b, dst, step, at, n):
        rows = pl.ds(pl.multiple_of((lat ^ step) * part, part), part)
        return columns(qkv_ref, out_ref, b, rows, me, dst, at, sems.at[n])

    copies = cut(0, part0_ref, 0, 0, 0)
    for i, step in enumerate(wide):
        copies += cut(1, part1_ref, step, part * i, 1 + i)
    inputs = [
        pltpu.make_async_copy(latent_ref, latent, own_sems.at[0]),
        pltpu.make_async_copy(region_ref, regions, own_sems.at[1]),
    ]
    for copy in copies + inputs:
        copy.start()
    for copy in inputs:
        copy.wait()
    tile_ref[0:WIN, :] = latent[...].reshape(WIN, D)
    col = lax.broadcasted_iota(jnp.int32, (WW, WIN), 0)
    token = lax.broadcasted_iota(jnp.int32, (WW, WIN), 1)
    spread = jnp.where(token % (WW * WZ) // WZ == col, 1.0, 0.0).astype(BF16)
    level = lax.broadcasted_iota(jnp.int32, (WZ, WIN), 0)
    token = lax.broadcasted_iota(jnp.int32, (WZ, WIN), 1)
    total = jnp.zeros((WZ, WIN), F32)
    for dh in range(WH):
        here = (token // (WW * WZ) == dh) & (token % WZ == level)
        total += jnp.where(here, nn_dot(regions[dh].astype(F32).astype(BF16), spread), 0.0)
    row = jnp.sum(total, axis=0, keepdims=True)
    tile_ref[WIN : WIN + REGION_ROWS, 0:WIN] = jnp.broadcast_to(row, (REGION_ROWS, WIN)).astype(BF16)
    tile_ref[WIN : WIN + REGION_ROWS, WIN:D] = jnp.zeros((REGION_ROWS, D - WIN), BF16)
    for copy in copies:
        copy.wait()


STAY = pl.BlockSpec(memory_space=pltpu.HBM)


def open_call(latent, regions, qkv, out, part, wide):
    return pl.pallas_call(
        functools.partial(open_kernel, wide),
        out_shape=(
            jax.ShapeDtypeStruct((part, COLS), BF16),
            jax.ShapeDtypeStruct((part * len(wide), COLS), BF16),
            jax.ShapeDtypeStruct((WIN + REGION_ROWS, D), BF16),
        ),
        in_specs=[STAY] * 4,
        scratch_shapes=[
            pltpu.VMEM(latent.shape, BF16),
            pltpu.VMEM(regions.shape, jnp.int32),
            pltpu.SemaphoreType.DMA((1 + len(wide), 4)),
            pltpu.SemaphoreType.DMA((2,)),
        ],
        compiler_params=pltpu.CompilerParams(vmem_limit_bytes=67043328-400*1024),
        cost_estimate=pl.CostEstimate(flops=10**6, bytes_accessed=10**6, transcendentals=0),
        name="open",
    )(latent, regions, qkv, out)


def own_kernel(qkv_ref, out_ref, own0_ref, own1_ref, sems):
    me = lax.axis_index("lon")
    copies = []
    for b, ref in enumerate((own0_ref, own1_ref)):
        copies += columns(qkv_ref, out_ref, b, pl.ds(0, ref.shape[0]), me, ref, 0, sems.at[b])
    for copy in copies:
        copy.start()
    for copy in copies:
        copy.wait()


def own_call(qkv, out):
    own = jax.ShapeDtypeStruct((qkv.shape[1], COLS), BF16)
    return pl.pallas_call(
        own_kernel,
        out_shape=(own, own),
        in_specs=[STAY] * 2,
        scratch_shapes=[pltpu.SemaphoreType.DMA((2, 4))],
        compiler_params=pltpu.CompilerParams(vmem_limit_bytes=67043328-2**20*6),
        cost_estimate=pl.CostEstimate(flops=0, bytes_accessed=10**6, transcendentals=0),
        name="own",
    )(qkv, out)


def enter_kernel(mine_ref, other_ref, gain_ref, x_ref, n_ref, row_ref, col_ref):
    me = lax.axis_index("lon")
    n_lat = lax.axis_size("lat")
    lat = lax.axis_index("lat")
    for k in range(3):
        for ref, l in ((mine_ref, me), (other_ref, 1 - me)):
            tokens = ref[k, 0:WIN, :]
            x_ref[l, WIN * k : WIN * (k + 1), :] = tokens
            n_ref[l, WIN * k : WIN * (k + 1), :] = norm_rows(tokens.astype(F32), gain_ref[0:1, :])
    lanes = lax.broadcasted_iota(jnp.int32, (1, WIN), 1)
    level = lanes & 1
    dh = lanes // (WW * WZ)
    rows = []
    for a in range(2):
        window = (lat + n_lat - 1 + a) % n_lat
        late = window * WH + dh >= n_lat * WH - WH // 2
        extra = jnp.where(level == WZ - 1, 2.0, 0.0) + jnp.where(late, 1.0, 0.0)
        mine = mine_ref[a, WIN : WIN + REGION_ROWS, 0:WIN].astype(F32)[0:1]
        other = other_ref[a, WIN : WIN + REGION_ROWS, 0:WIN].astype(F32)[0:1]
        west = jnp.where(me == 0, mine, other)
        east = jnp.where(me == 0, other, mine)
        rows += [4.0 * west + extra, 4.0 * east + extra]
    tags = jnp.concatenate(rows + rows, axis=0)
    row_ref[...] = tags
    to = lax.broadcasted_iota(jnp.int32, (WIN, WIN), 0)
    frm = lax.broadcasted_iota(jnp.int32, (WIN, WIN), 1)
    col_ref[...] = nt_dot(jnp.where(to == frm, 1.0, 0.0).astype(BF16), tags.astype(BF16))


def enter_call(mine, other, gain):
    return pl.pallas_call(
        enter_kernel,
        out_shape=(
            jax.ShapeDtypeStruct((PAIR, TALL, D), BF16),
            jax.ShapeDtypeStruct((PAIR, TALL, D), BF16),
            jax.ShapeDtypeStruct((8, WIN), F32),
            jax.ShapeDtypeStruct((WIN, 8), F32),
        ),
        compiler_params=vmem(16),
        cost_estimate=pl.CostEstimate(flops=10**8, bytes_accessed=2 * 10**6, transcendentals=0),
        name="enter",
    )(mine, other, gain)


def join_kernel(n_fsdp, n_lat, steps, wide, own_ref, *refs):
    far, near = refs[: n_fsdp - 1], refs[n_fsdp - 1 : n_fsdp - 1 + len(steps)]
    qkv_ref, out_ref = refs[-2:]
    z, lat = lax.axis_index("fsdp"), lax.axis_index("lat")
    depth = own_ref.shape[0]
    part = depth // n_lat

    def put(first, size, piece):
        rows = pl.ds(pl.multiple_of(first, size), size)
        qkv_ref[rows, :] = piece[:, 0:QKV]
        out_ref[rows, :] = piece[:, QKV:COLS]

    put(z * depth, depth, own_ref[...])
    for k in range(1, n_fsdp):
        base = partner(z, k, n_fsdp) * depth
        for i, step in enumerate(wide):
            put(base + (lat ^ step) * part, part, far[k - 1][part * i : part * (i + 1), :])
        for j, step in enumerate(steps):
            row = base + partner(lat, step, n_lat) * part
            put(row, part, near[j][part * (k - 1) : part * k, :])


def join_call(n_lat, steps, wide, own, far, near):
    rows = own.shape[0] * (len(far) + 1)
    return pl.pallas_call(
        functools.partial(join_kernel, len(far) + 1, n_lat, steps, wide),
        out_shape=(
            jax.ShapeDtypeStruct((rows, QKV), BF16),
            jax.ShapeDtypeStruct((rows, OUT), BF16),
        ),
        compiler_params=vmem(8),
        cost_estimate=pl.CostEstimate(flops=10**6, bytes_accessed=2 * 10**6, transcendentals=0),
    )(own, *far, *near)


def window_attend(q, k, v, bias_at, allowed, put):
    n = q.shape[0]
    lanes = lax.broadcasted_iota(jnp.int32, (n, 128), 1)
    owns = [(lanes >= HEAD_DIM * j) & (lanes < HEAD_DIM * (j + 1)) for j in range(GROUP)]
    ones = jnp.ones((WIN, 128), BF16)
    for g in range(MINE // 128):
        cols = slice(128 * g, 128 * (g + 1))
        q_g = q[:, cols]
        k_g = k[:, cols]
        v_g = jnp.concatenate([v[:, cols], ones], axis=1)
        q_all = jnp.concatenate([jnp.where(o, q_g, jnp.zeros_like(q_g)) for o in owns], axis=0)
        scores = nt_dot(q_all, k_g)
        probs = []
        for j in range(GROUP):
            s = scores[n * j : n * (j + 1)] * SCALE2 + bias_at(GROUP * g + j)
            if allowed is not None:
                s = jnp.where(allowed, s, NEG)
            peak = jnp.max(s, axis=-1, keepdims=True)
            probs.append(jnp.exp2(s - peak).astype(BF16))
        mixed = nn_dot(jnp.concatenate(probs, axis=0), v_g)
        acc = None
        for j in range(GROUP):
            m = mixed[n * j : n * (j + 1)]
            value = m[:, 0:128] / m[:, 128:256]
            acc = value if acc is None else jnp.where(owns[j], value, acc)
        put(128 * g, acc.astype(BF16))


def project(n, w_ref, q_s, k_s, v_s):
    both = nn_dot(n, w_ref[...]).astype(BF16)
    q_s[...] = both[:, 0:MINE]
    k_s[...] = both[:, MINE : 2 * MINE]
    v_s[...] = both[:, 2 * MINE : 3 * MINE]


def first_kernel(n_ref, w_ref, bias_ref, o_ref, q_s, k_s, v_s):
    project(n_ref[...].reshape(PAIR * TALL, D), w_ref, q_s, k_s, v_s)
    for l in range(PAIR):
        for part, (q0, q1, o0) in enumerate(
            ((KEEP0, WIN, 0), (0, WIN, PART), (0, PART, PART + WIN))
        ):
            t = TALL * l + WIN * part

            def put(col, value, l=l, o0=o0, q0=q0, q1=q1):
                o_ref[l, o0 : o0 + q1 - q0, col : col + 128] = value

            window_attend(
                q_s[t + q0 : t + q1, :],
                k_s[t : t + WIN, :],
                v_s[t : t + WIN, :],
                lambda h, q0=q0, q1=q1: bias_ref[h, q0:q1, :],
                None,
                put,
            )


def first_call(normed, weight, bias):
    scratch = pltpu.VMEM((PAIR * TALL, MINE), BF16)
    return pl.pallas_call(
        first_kernel,
        out_shape=jax.ShapeDtypeStruct((PAIR, KEPT, MINE), BF16),
        scratch_shapes=[scratch, scratch, scratch],
        compiler_params=vmem(24),
        cost_estimate=pl.CostEstimate(flops=2 * 10**9, bytes_accessed=4 * 10**6, transcendentals=10**6),
        name="first",
    )(normed, weight, bias)


def pair_columns(me, ref, mine, other):
    width = mine.shape[-1]
    ref[:, pl.ds(pl.multiple_of(width * me, width), width)] = mine
    ref[:, pl.ds(pl.multiple_of(width * (1 - me), width), width)] = other


def second_kernel(
    mine_ref, other_ref, wo_mine_ref, wo_other_ref, x_ref, gain_ref, src_ref, w_ref, bias_ref,
    row_ref, col_ref, back_ref, mid_ref, keep_ref, send_ref, o_s, wo_s, m_s, n_s, q_s, k_s, v_s, a_s, t_s,
):
    me = lax.axis_index("lon")
    tokens = PAIR * KEPT
    pair_columns(me, o_s, mine_ref[...].reshape(tokens, MINE), other_ref[...].reshape(tokens, MINE))
    pair_columns(me, wo_s, wo_mine_ref[...], wo_other_ref[...])
    for l in range(PAIR):
        rows = slice(KEPT * l, KEPT * (l + 1))
        value = x_ref[l, KEEP0:KEEP1, :].astype(F32) + nn_dot(o_s[rows, :], wo_s[...])
        value = value.astype(BF16)
        m_s[l] = value
        n_s[rows, :] = norm_rows(value.astype(F32), gain_ref[1:2, :])
    mid_ref[...] = m_s[me, PART : PART + WIN, :]
    windows = nn_dot(one_hot(src_ref[...], tokens), n_s[...]).astype(BF16)
    project(windows, w_ref, q_s, k_s, v_s)
    for w in range(4):
        q0, q1 = (KEEP0, WIN) if w < 2 else (0, PART)
        t = WIN * w
        allowed = col_ref[q0:q1, w : w + 1] == row_ref[w : w + 1, :]

        def put(col, value, w=w):
            a_s[PART * w : PART * (w + 1), col : col + 128] = value

        window_attend(
            q_s[t + q0 : t + q1, :],
            k_s[t : t + WIN, :],
            v_s[t : t + WIN, :],
            lambda h, q0=q0, q1=q1: bias_ref[h, q0:q1, :],
            allowed,
            put,
        )
    tiles = nn_dot(one_hot(back_ref[...], 4 * PART), a_s[...]).astype(BF16)
    t_s[0] = tiles[0:WIN]
    t_s[1] = tiles[WIN : 2 * WIN]
    keep_ref[...] = t_s[me]
    send_ref[...] = t_s[1 - me]


def second_call(mine, other, wo_mine, wo_other, x, gain, weight, bias, row, col):
    tokens = PAIR * KEPT
    qkv = pltpu.VMEM((4 * WIN, MINE), BF16)
    return pl.pallas_call(
        second_kernel,
        out_shape=(
            jax.ShapeDtypeStruct((WIN, D), BF16),
            jax.ShapeDtypeStruct((WIN, MINE), BF16),
            jax.ShapeDtypeStruct((WIN, MINE), BF16),
        ),
        scratch_shapes=[
            pltpu.VMEM((tokens, D), BF16),
            pltpu.VMEM((D, D), BF16),
            pltpu.VMEM((PAIR, KEPT, D), BF16),
            pltpu.VMEM((tokens, D), BF16),
            qkv,
            qkv,
            qkv,
            pltpu.VMEM((4 * PART, MINE), BF16),
            pltpu.VMEM((PAIR, WIN, MINE), BF16),
        ],
        compiler_params=vmem(24),
        cost_estimate=pl.CostEstimate(flops=2 * 10**9, bytes_accessed=4 * 10**6, transcendentals=10**6),
        name="second",
    )(
        mine, other, wo_mine, wo_other, x, gain, jnp.asarray(window_sources()), weight, bias,
        row, col, jnp.asarray(tile_sources()),
    )


def last_kernel(mid_ref, keep_ref, got_ref, wo_mine_ref, wo_other_ref, out_ref, o_s, wo_s):
    me = lax.axis_index("lon")
    pair_columns(me, o_s, keep_ref[...], got_ref[...])
    pair_columns(me, wo_s, wo_mine_ref[...], wo_other_ref[...])
    value = mid_ref[...].astype(F32) + nn_dot(o_s[...], wo_s[...])
    out_ref[...] = value.reshape(WIN // WZ, WZ, D).astype(BF16)


def last_call(mid, keep, got, wo_mine, wo_other):
    return pl.pallas_call(
        last_kernel,
        out_shape=jax.ShapeDtypeStruct((WIN // WZ, WZ, D), BF16),
        scratch_shapes=[pltpu.VMEM((WIN, D), BF16), pltpu.VMEM((D, D), BF16)],
        compiler_params=vmem(8),
        cost_estimate=pl.CostEstimate(flops=10**8, bytes_accessed=10**6, transcendentals=0),
        name="last",
    )(mid, keep, got, wo_mine, wo_other)


def sharing(n_lat):
    every = tuple(range(1, n_lat))
    if n_lat == 4:
        return (((0,), every), ((0, 3), (1, 2)))
    return (((0,), every), ((0,), every))


def paired(latent, norm_gain, qkv_weight, out_weight, rel_bias, bias_index, region_ids):
    n_fsdp, n_lat = lax.axis_size("fsdp"), lax.axis_size("lat")
    part = qkv_weight.shape[1] // n_lat
    plan = sharing(n_lat)

    def swap(block):
        return passed_along(block, "lon", 1)

    def spread(block, axis, steps):
        got = []
        for k in steps:
            got.append(heard_from(block, axis, k))
        return got

    part0, part1, tile = open_call(
        jnp.transpose(latent[0], (1, 2, 0, 3)).reshape(WIN // WZ, WZ, D),
        jnp.transpose(region_ids, (1, 0, 2)),
        qkv_weight,
        out_weight,
        part,
        plan[1][0],
    )
    far0 = spread(part0, "fsdp", range(1, n_fsdp))
    before = passed_along(tile, "lat", 1)
    after = passed_along(tile, "lat", -1)
    far1 = spread(part1, "fsdp", range(1, n_fsdp))
    near0 = spread(jnp.concatenate(far0, axis=0), "lat", plan[0][1])
    near1 = spread(jnp.concatenate([f[:part] for f in far1], axis=0), "lat", plan[1][1])
    own0, own1 = own_call(qkv_weight, out_weight)
    tall = jnp.stack([before, tile, after])
    x, normed, tag_row, tag_col = enter_call(tall, swap(tall), norm_gain)
    table = jnp.transpose(rel_bias, (0, 2, 1))
    w0, wo0 = join_call(n_lat, plan[0][1], plan[0][0], own0, far0, near0)
    o0 = first_call(normed, w0, bias_call(0, table, bias_index))
    w1, wo1 = join_call(n_lat, plan[1][1], plan[1][0], own1, far1, near1)
    mid, keep, send = second_call(
        o0, swap(o0), wo0, swap(wo0), x, norm_gain, w1,
        bias_call(1, table, bias_index), tag_row, tag_col,
    )
    out = last_call(mid, keep, swap(send), wo1, swap(wo1))
    return jnp.transpose(out.reshape(WH, WW, WZ, D), (2, 0, 1, 3))[None]


def solution(mesh):
    pair = mesh.shape["lon"] == PAIR

    def local(latent, norm_gain, qkv_weight, out_weight, *rest):
        one_window = latent.shape[:4] == (1, WZ, WH, WW)
        even = qkv_weight.shape[1] % (16 * mesh.shape["lat"]) == 0
        program = paired if pair and one_window and even else any_mesh
        return program(latent, norm_gain, qkv_weight, out_weight, *rest)

    return jax.shard_map(
        local,
        mesh=mesh,
        in_specs=(
            P("fsdp", None, "lat", "lon", None),
            P(),
            P(None, "fsdp", None),
            P(None, "fsdp", None),
            P(),
            P(),
            P(None, "lat", "lon"),
        ),
        out_specs=P("fsdp", None, "lat", "lon", None),
        check_vma=False,
    )
```

```python
import functools

import jax
import jax.numpy as jnp
import numpy as np
from jax import lax
from jax.experimental import pallas as pl
from jax.experimental.pallas import tpu as pltpu
from jax.sharding import PartitionSpec as P


D = 512
HEADS = 16
HEAD_DIM = 32
WZ = 2
WH = 6
WW = 12
WIN = 144
BIAS_ROWS = 759
HALF = WIN // 2
LOG2E = 1.4426950408889634
SCALE2 = HEAD_DIM ** (-0.5) * LOG2E
NEG = -1e30


def passed_along(block, axis, distance):
    devices = range(lax.axis_size(axis))
    route = [((i - distance) % len(devices), i) for i in devices]
    return lax.ppermute(block, axis, route)


def layer_norm(hidden, gain_row):
    values = hidden.astype(jnp.float32)
    centre = jnp.mean(values, axis=-1, keepdims=True)
    shifted = values - centre
    variance = jnp.mean(shifted * shifted, axis=-1, keepdims=True)
    return (shifted * lax.rsqrt(variance + 1e-05) * gain_row).astype(jnp.bfloat16)


def bias_table(rel_bias, bias_index, block_index):
    return jnp.take(jnp.transpose(rel_bias[block_index]), bias_index, axis=1)


def split_tile(field_tile):
    sample_count, level_count, row_count, col_count, feature_width = field_tile.shape
    pieces = field_tile.reshape(
        sample_count, level_count // WZ, WZ, row_count // WH, WH, col_count // WW, WW, feature_width
    )
    pieces = jnp.transpose(pieces, (0, 1, 3, 5, 2, 4, 6, 7))
    return pieces.reshape(-1, WIN, feature_width)


def merge_tile(windows, tile_shape):
    sample_count, level_count, row_count, col_count, feature_width = tile_shape
    pieces = windows.reshape(
        sample_count, level_count // WZ, row_count // WH, col_count // WW, WZ, WH, WW, feature_width
    )
    pieces = jnp.transpose(pieces, (0, 1, 4, 2, 5, 3, 6, 7))
    return pieces.reshape(tile_shape)


def attend(normed, weight, bias_heads, region_tags):
    packed = jnp.dot(normed.reshape(-1, D), weight, preferred_element_type=jnp.float32).astype(
        jnp.bfloat16
    )
    packed = split_tile(packed.reshape(normed.shape[:-1] + (3 * D,)))
    packed = packed.reshape(-1, WIN, 3, HEADS, HEAD_DIM)
    scores = jnp.einsum(
        "gqhd,gkhd->ghqk", packed[:, :, 0], packed[:, :, 1], preferred_element_type=jnp.float32
    )
    scores = scores * HEAD_DIM ** (-0.5) + bias_heads[None]
    if region_tags is not None:
        window_tags = split_tile(region_tags[..., None])[..., 0]
        allowed = window_tags[:, :, None] == window_tags[:, None, :]
        blocked = jnp.where(allowed, jnp.float32(0.0), -jnp.inf)
        scores = scores + blocked[:, None]
    row_peak = jnp.max(scores, axis=-1, keepdims=True)
    exponent = jnp.exp(scores - row_peak)
    row_total = jnp.sum(exponent, axis=-1, keepdims=True)
    attn_probs = (exponent / row_total).astype(jnp.bfloat16)
    mixed_out = jnp.einsum(
        "ghqk,gkhd->gqhd", attn_probs, packed[:, :, 2], preferred_element_type=jnp.float32
    )
    return merge_tile(mixed_out.astype(jnp.bfloat16).reshape(-1, WIN, D), normed.shape)


def any_mesh(latent, norm_gain, qkv_weight, out_weight, rel_bias, bias_index, region_ids):
    half_rows = WH // 2
    half_cols = WW // 2
    row_count = latent.shape[2]
    col_count = latent.shape[3]
    gathered_qkv, gathered_out = (
        lax.all_gather(qkv_weight, "fsdp", axis=1, tiled=True),
        lax.all_gather(out_weight, "fsdp", axis=1, tiled=True),
    )

    def fetch_weights(block_index):
        return (gathered_qkv[block_index], gathered_out[block_index])

    first_qkv, first_out = fetch_weights(0)
    normed = layer_norm(latent, norm_gain[0])
    mixed_out = attend(normed, first_qkv, bias_table(rel_bias, bias_index, 0), None)
    projected = jnp.dot(mixed_out.reshape(-1, D), first_out, preferred_element_type=jnp.float32)
    middle = (latent.astype(jnp.float32) + projected.reshape(latent.shape)).astype(jnp.bfloat16)
    second_qkv, second_out = fetch_weights(1)
    normed = jnp.roll(layer_norm(middle, norm_gain[1]), -1, axis=1)
    east_strip = passed_along(normed[:, :, :, :half_cols], "lon", -1)
    widened = jnp.concatenate([normed[:, :, :, half_cols:], east_strip], axis=3)
    north_strip = passed_along(widened[:, :, :half_rows], "lat", -1)
    rolled = jnp.concatenate([widened[:, :, half_rows:], north_strip], axis=2)
    level_pos = lax.broadcasted_iota(jnp.int32, region_ids.shape, 0)
    row_pos = (
        lax.broadcasted_iota(jnp.int32, region_ids.shape, 1) + lax.axis_index("lat") * row_count
    )
    region_tags = region_ids * 4 + (level_pos == region_ids.shape[0] - 1).astype(jnp.int32) * 2
    region_tags = region_tags + (row_pos >= row_count * lax.axis_size("lat") - half_rows).astype(
        jnp.int32
    )
    region_tags = region_tags[None]
    mixed_out = attend(rolled, second_qkv, bias_table(rel_bias, bias_index, 1), region_tags)
    south_strip = passed_along(mixed_out[:, :, row_count - half_rows :], "lat", 1)
    widened = jnp.concatenate([south_strip, mixed_out[:, :, : row_count - half_rows]], axis=2)
    west_strip = passed_along(widened[:, :, :, col_count - half_cols :], "lon", 1)
    mixed_out = jnp.concatenate([west_strip, widened[:, :, :, : col_count - half_cols]], axis=3)
    mixed_out = jnp.roll(mixed_out, 1, axis=1)
    projected = jnp.dot(mixed_out.reshape(-1, D), second_out, preferred_element_type=jnp.float32)
    return (middle.astype(jnp.float32) + projected.reshape(latent.shape)).astype(jnp.bfloat16)


PAIR = 2
MY_HEADS = HEADS // PAIR
MINE = MY_HEADS * HEAD_DIM
QKV = 3 * MINE
OUT = D // PAIR
COLS = QKV + OUT
TALL = 3 * WIN
KEEP0 = 64
KEEP1 = TALL - 64
KEPT = KEEP1 - KEEP0
PART = WIN - KEEP0
REGION_ROWS = 8
GROUP = 128 // HEAD_DIM
F32 = jnp.float32
BF16 = jnp.bfloat16


def vmem(mib):
    return pltpu.CompilerParams(vmem_limit_bytes=mib * 2**20)


def partner(index, step, size):
    if size & (size - 1) == 0:
        return index ^ step
    return (index + size - step) % size


def heard_from(block, axis, step):
    size = lax.axis_size(axis)
    return lax.ppermute(block, axis, [(partner(i, step, size), i) for i in range(size)])


def window_sources():
    src = np.zeros((2, 2, WH, WW, WZ), np.int32)
    for a in range(2):
        for v in range(2):
            for dh in range(WH):
                for dw in range(WW):
                    for dz in range(WZ):
                        row = dh + (WH // 2 if a else -(WH // 2))
                        col = (WW // 2 + WW * v + dw) % (2 * WW)
                        level = (dz + 1) % WZ
                        t = (row + WH) * WW * WZ + (col % WW) * WZ + level
                        src[a, v, dh, dw, dz] = (col // WW) * KEPT + t - KEEP0
    return src.reshape(-1, 1)


def tile_sources():
    src = np.zeros((2, WH, WW, WZ), np.int32)
    for l in range(2):
        for row in range(WH):
            for cw in range(WW):
                for level in range(WZ):
                    a = 0 if row < WH // 2 else 1
                    dh = (row + WH // 2) % WH
                    col = (WW * l + cw - WW // 2) % (2 * WW)
                    dz = (level - 1) % WZ
                    t = dh * WW * WZ + (col % WW) * WZ + dz - (0 if a else KEEP0)
                    src[l, row, cw, level] = (a * 2 + col // WW) * PART + t
    return src.reshape(-1, 1)


def one_hot(sources, width):
    lanes = lax.broadcasted_iota(jnp.int32, (sources.shape[0], width), 1)
    return jnp.where(lanes == sources, 1.0, 0.0).astype(BF16)


def nt_dot(a, b):
    return lax.dot_general(a, b, (((1,), (1,)), ((), ())), preferred_element_type=F32)


def nn_dot(a, b):
    return jnp.dot(a, b, preferred_element_type=F32)


def norm_rows(values, gain_row):
    centre = jnp.mean(values, axis=-1, keepdims=True)
    shifted = values - centre
    variance = jnp.mean(shifted * shifted, axis=-1, keepdims=True)
    return (shifted * lax.rsqrt(variance + 1e-05) * gain_row).astype(BF16)


def gather_heads(b, table_ref, index, table, bias_ref):
    me = lax.axis_index("lon")
    heads = table_ref[b, pl.ds(pl.multiple_of(MY_HEADS * me, MY_HEADS), MY_HEADS), :]
    table[:, 0:BIAS_ROWS] = heads * LOG2E
    chunks = (BIAS_ROWS + 127) // 128

    def look_up(at, put):
        low = at & 127
        chunk = at >> 7
        masks = [chunk == k for k in range(chunks)]
        for h in range(MY_HEADS):
            acc = None
            for k in range(chunks):
                row = jnp.broadcast_to(table[h : h + 1, 128 * k : 128 * k + 128], (8, 128))
                got = jnp.take_along_axis(row, low, axis=1, mode="promise_in_bounds")
                acc = got if acc is None else jnp.where(masks[k], got, acc)
            put(h, acc)

    def step(g, carry):
        rows = pl.ds(pl.multiple_of(g * 8, 8), 8)

        def put(h, value):
            bias_ref[h, rows, 0:128] = value

        look_up(index[rows, 0:128], put)
        return carry

    lax.fori_loop(0, WIN // 8, step, 0)
    rest = WIN - 128
    each = 128 // rest
    groups = WIN // 8
    for first in range(0, groups, each):
        here = range(first, min(first + each, groups))
        pieces = [index[8 * g : 8 * g + 8, 128:WIN] for g in here]
        pieces += [jnp.zeros((8, rest), jnp.int32)] * (each - len(pieces))

        def put(h, value, here=here):
            for r, g in enumerate(here):
                bias_ref[h, 8 * g : 8 * g + 8, 128:WIN] = value[:, rest * r : rest * (r + 1)]

        look_up(jnp.concatenate(pieces, axis=1), put)


def bias0_kernel(table_ref, index_ref, bias_ref, moved_ref, table):
    to = lax.broadcasted_iota(jnp.int32, (WIN, WIN), 0)
    frm = lax.broadcasted_iota(jnp.int32, (WIN, WIN), 1)
    move = jnp.where((to & 1) * HALF + (to >> 1) == frm, 1.0, 0.0).astype(BF16)
    whole = index_ref[...]
    parts = jnp.concatenate([whole >> 8, whole & 255], axis=0).astype(F32).astype(BF16)
    parts = nt_dot(parts, move).astype(BF16)
    moved_ref[...] = (
        nn_dot(move, parts[0:WIN]) * 256.0 + nn_dot(move, parts[WIN : 2 * WIN])
    ).astype(jnp.int32)
    gather_heads(0, table_ref, moved_ref, table, bias_ref)


def bias1_kernel(table_ref, index_ref, bias_ref, table):
    gather_heads(1, table_ref, index_ref, table, bias_ref)


def bias_call(b, table, index):
    bias = jax.ShapeDtypeStruct((MY_HEADS, WIN, WIN), F32)
    moved = jax.ShapeDtypeStruct((WIN, WIN), jnp.int32)
    return pl.pallas_call(
        bias1_kernel if b else bias0_kernel,
        out_shape=bias if b else (bias, moved),
        scratch_shapes=[pltpu.VMEM((MY_HEADS, (BIAS_ROWS + 127) // 128 * 128), F32)],
        compiler_params=vmem(8),
        cost_estimate=pl.CostEstimate(flops=10**9, bytes_accessed=10**6, transcendentals=0),
    )(table, index)


def columns(qkv_ref, out_ref, b, rows, me, dst, at, sems):
    mine = pl.ds(pl.multiple_of(MINE * me, MINE), MINE)
    sources = [
        qkv_ref.at[b, rows, pl.ds(pl.multiple_of(D * k + MINE * me, MINE), MINE)] for k in range(3)
    ]
    sources += [out_ref.at[b, rows, mine]]
    to = pl.ds(at, rows.size)
    return [
        pltpu.make_async_copy(source, dst.at[to, pl.ds(MINE * k, MINE)], sems.at[k])
        for k, source in enumerate(sources)
    ]


def open_kernel(
    wide, latent_ref, region_ref, qkv_ref, out_ref, part0_ref, part1_ref, tile_ref,
    latent, regions, sems, own_sems,
):
    part = part0_ref.shape[0]
    me, lat = lax.axis_index("lon"), lax.axis_index("lat")

    def cut(b, dst, step, at, n):
        rows = pl.ds(pl.multiple_of((lat ^ step) * part, part), part)
        return columns(qkv_ref, out_ref, b, rows, me, dst, at, sems.at[n])

    copies = cut(0, part0_ref, 0, 0, 0)
    for i, step in enumerate(wide):
        copies += cut(1, part1_ref, step, part * i, 1 + i)
    inputs = [
        pltpu.make_async_copy(latent_ref, latent, own_sems.at[0]),
        pltpu.make_async_copy(region_ref, regions, own_sems.at[1]),
    ]
    for copy in copies + inputs:
        copy.start()
    for copy in inputs:
        copy.wait()
    tile_ref[0:WIN, :] = latent[...].reshape(WIN, D)
    col = lax.broadcasted_iota(jnp.int32, (WW, WIN), 0)
    token = lax.broadcasted_iota(jnp.int32, (WW, WIN), 1)
    spread = jnp.where(token % (WW * WZ) // WZ == col, 1.0, 0.0).astype(BF16)
    level = lax.broadcasted_iota(jnp.int32, (WZ, WIN), 0)
    token = lax.broadcasted_iota(jnp.int32, (WZ, WIN), 1)
    total = jnp.zeros((WZ, WIN), F32)
    for dh in range(WH):
        here = (token // (WW * WZ) == dh) & (token % WZ == level)
        total += jnp.where(here, nn_dot(regions[dh].astype(F32).astype(BF16), spread), 0.0)
    row = jnp.sum(total, axis=0, keepdims=True)
    tile_ref[WIN : WIN + REGION_ROWS, 0:WIN] = jnp.broadcast_to(row, (REGION_ROWS, WIN)).astype(BF16)
    tile_ref[WIN : WIN + REGION_ROWS, WIN:D] = jnp.zeros((REGION_ROWS, D - WIN), BF16)
    for copy in copies:
        copy.wait()


STAY = pl.BlockSpec(memory_space=pltpu.HBM)


def open_call(latent, regions, qkv, out, part, wide):
    return pl.pallas_call(
        functools.partial(open_kernel, wide),
        out_shape=(
            jax.ShapeDtypeStruct((part, COLS), BF16),
            jax.ShapeDtypeStruct((part * len(wide), COLS), BF16),
            jax.ShapeDtypeStruct((WIN + REGION_ROWS, D), BF16),
        ),
        in_specs=[STAY] * 4,
        scratch_shapes=[
            pltpu.VMEM(latent.shape, BF16),
            pltpu.VMEM(regions.shape, jnp.int32),
            pltpu.SemaphoreType.DMA((1 + len(wide), 4)),
            pltpu.SemaphoreType.DMA((2,)),
        ],
        compiler_params=pltpu.CompilerParams(vmem_limit_bytes=67043328-400*1024),
        cost_estimate=pl.CostEstimate(flops=10**6, bytes_accessed=10**6, transcendentals=0),
        name="open",
    )(latent, regions, qkv, out)


def stack_kernel(before_ref, tile_ref, after_ref, tall_ref):
    tall_ref[0] = before_ref[...]
    tall_ref[1] = tile_ref[...]
    tall_ref[2] = after_ref[...]


def stack_call(before, tile, after):
    return pl.pallas_call(
        stack_kernel,
        out_shape=jax.ShapeDtypeStruct((3,) + tile.shape, BF16),
        compiler_params=vmem(4),
        cost_estimate=pl.CostEstimate(flops=0, bytes_accessed=10**6, transcendentals=0),
        name="stack",
    )(before, tile, after)


def enter_kernel(mine_ref, other_ref, gain_ref, x_ref, n_ref, row_ref, col_ref):
    me = lax.axis_index("lon")
    n_lat = lax.axis_size("lat")
    lat = lax.axis_index("lat")
    for k in range(3):
        for ref, l in ((mine_ref, me), (other_ref, 1 - me)):
            tokens = ref[k, 0:WIN, :]
            x_ref[l, WIN * k : WIN * (k + 1), :] = tokens
            n_ref[l, WIN * k : WIN * (k + 1), :] = norm_rows(tokens.astype(F32), gain_ref[0:1, :])
    lanes = lax.broadcasted_iota(jnp.int32, (1, WIN), 1)
    level = lanes & 1
    dh = lanes // (WW * WZ)
    rows = []
    for a in range(2):
        window = (lat + n_lat - 1 + a) % n_lat
        late = window * WH + dh >= n_lat * WH - WH // 2
        extra = jnp.where(level == WZ - 1, 2.0, 0.0) + jnp.where(late, 1.0, 0.0)
        mine = mine_ref[a, WIN : WIN + REGION_ROWS, 0:WIN].astype(F32)[0:1]
        other = other_ref[a, WIN : WIN + REGION_ROWS, 0:WIN].astype(F32)[0:1]
        west = jnp.where(me == 0, mine, other)
        east = jnp.where(me == 0, other, mine)
        rows += [4.0 * west + extra, 4.0 * east + extra]
    tags = jnp.concatenate(rows + rows, axis=0)
    row_ref[...] = tags
    to = lax.broadcasted_iota(jnp.int32, (WIN, WIN), 0)
    frm = lax.broadcasted_iota(jnp.int32, (WIN, WIN), 1)
    col_ref[...] = nt_dot(jnp.where(to == frm, 1.0, 0.0).astype(BF16), tags.astype(BF16))


def enter_call(mine, other, gain):
    return pl.pallas_call(
        enter_kernel,
        out_shape=(
            jax.ShapeDtypeStruct((PAIR, TALL, D), BF16),
            jax.ShapeDtypeStruct((PAIR, TALL, D), BF16),
            jax.ShapeDtypeStruct((8, WIN), F32),
            jax.ShapeDtypeStruct((WIN, 8), F32),
        ),
        compiler_params=vmem(16),
        cost_estimate=pl.CostEstimate(flops=10**8, bytes_accessed=2 * 10**6, transcendentals=0),
        name="enter",
    )(mine, other, gain)


def join_kernel(b, n_fsdp, n_lat, steps, wide, own_qkv_ref, own_out_ref, *refs):
    far, near = refs[: n_fsdp - 1], refs[n_fsdp - 1 : n_fsdp - 1 + len(steps)]
    qkv_ref, out_ref = refs[-2:]
    z, lat = lax.axis_index("fsdp"), lax.axis_index("lat")
    depth = own_qkv_ref.shape[1]
    part = depth // n_lat
    me = lax.axis_index("lon")

    def put(first, size, piece):
        rows = pl.ds(pl.multiple_of(first, size), size)
        qkv_ref[rows, :] = piece[:, 0:QKV]
        out_ref[rows, :] = piece[:, QKV:COLS]

    own = pl.ds(pl.multiple_of(z * depth, depth), depth)
    for k in range(3):
        mine = pl.ds(pl.multiple_of(D * k + MINE * me, MINE), MINE)
        qkv_ref[own, MINE * k : MINE * (k + 1)] = own_qkv_ref[b, :, mine]
    out_ref[own, :] = own_out_ref[b, :, pl.ds(pl.multiple_of(OUT * me, OUT), OUT)]
    for k in range(1, n_fsdp):
        base = partner(z, k, n_fsdp) * depth
        for i, step in enumerate(wide):
            put(base + (lat ^ step) * part, part, far[k - 1][part * i : part * (i + 1), :])
        for j, step in enumerate(steps):
            row = base + partner(lat, step, n_lat) * part
            put(row, part, near[j][part * (k - 1) : part * k, :])


def join_call(b, n_lat, steps, wide, qkv, out, far, near):
    rows = qkv.shape[1] * (len(far) + 1)
    return pl.pallas_call(
        functools.partial(join_kernel, b, len(far) + 1, n_lat, steps, wide),
        out_shape=(
            jax.ShapeDtypeStruct((rows, QKV), BF16),
            jax.ShapeDtypeStruct((rows, OUT), BF16),
        ),
        compiler_params=vmem(8),
        cost_estimate=pl.CostEstimate(flops=10**6, bytes_accessed=2 * 10**6, transcendentals=0),
    )(qkv, out, *far, *near)


def window_attend(q, k, v, bias_at, allowed, put):
    n = q.shape[0]
    lanes = lax.broadcasted_iota(jnp.int32, (n, 128), 1)
    owns = [(lanes >= HEAD_DIM * j) & (lanes < HEAD_DIM * (j + 1)) for j in range(GROUP)]
    ones = jnp.ones((WIN, 128), BF16)
    for g in range(MINE // 128):
        cols = slice(128 * g, 128 * (g + 1))
        q_g = q[:, cols]
        k_g = k[:, cols]
        v_g = jnp.concatenate([v[:, cols], ones], axis=1)
        q_all = jnp.concatenate([jnp.where(o, q_g, jnp.zeros_like(q_g)) for o in owns], axis=0)
        scores = nt_dot(q_all, k_g)
        probs = []
        for j in range(GROUP):
            s = scores[n * j : n * (j + 1)] * SCALE2 + bias_at(GROUP * g + j)
            if allowed is not None:
                s = jnp.where(allowed, s, NEG)
            peak = jnp.max(s, axis=-1, keepdims=True)
            probs.append(jnp.exp2(s - peak).astype(BF16))
        mixed = nn_dot(jnp.concatenate(probs, axis=0), v_g)
        acc = None
        for j in range(GROUP):
            m = mixed[n * j : n * (j + 1)]
            value = m[:, 0:128] / m[:, 128:256]
            acc = value if acc is None else jnp.where(owns[j], value, acc)
        put(128 * g, acc.astype(BF16))


def project(n, w_ref, q_s, k_s, v_s):
    both = nn_dot(n, w_ref[...]).astype(BF16)
    q_s[...] = both[:, 0:MINE]
    k_s[...] = both[:, MINE : 2 * MINE]
    v_s[...] = both[:, 2 * MINE : 3 * MINE]


def first_kernel(n_ref, w_ref, bias_ref, wo_ref, o_ref, q_s, k_s, v_s):
    o_ref[PAIR * KEPT :, :] = wo_ref[...]
    project(n_ref[...].reshape(PAIR * TALL, D), w_ref, q_s, k_s, v_s)
    for l in range(PAIR):
        for part, (q0, q1, o0) in enumerate(
            ((KEEP0, WIN, 0), (0, WIN, PART), (0, PART, PART + WIN))
        ):
            t = TALL * l + WIN * part

            def put(col, value, l=l, o0=o0, q0=q0, q1=q1):
                o_ref[KEPT * l + o0 : KEPT * l + o0 + q1 - q0, col : col + 128] = value

            window_attend(
                q_s[t + q0 : t + q1, :],
                k_s[t : t + WIN, :],
                v_s[t : t + WIN, :],
                lambda h, q0=q0, q1=q1: bias_ref[h, q0:q1, :],
                None,
                put,
            )


def first_call(normed, weight, bias, wo):
    scratch = pltpu.VMEM((PAIR * TALL, MINE), BF16)
    return pl.pallas_call(
        first_kernel,
        out_shape=jax.ShapeDtypeStruct((PAIR * KEPT + D, MINE), BF16),
        scratch_shapes=[scratch, scratch, scratch],
        compiler_params=vmem(24),
        cost_estimate=pl.CostEstimate(flops=2 * 10**9, bytes_accessed=4 * 10**6, transcendentals=10**6),
        name="first",
    )(normed, weight, bias, wo)


def pair_columns(me, ref, mine, other):
    width = mine.shape[-1]
    ref[:, pl.ds(pl.multiple_of(width * me, width), width)] = mine
    ref[:, pl.ds(pl.multiple_of(width * (1 - me), width), width)] = other


def second_kernel(
    mine_ref, other_ref, x_ref, gain_ref, src_ref, w_ref, bias_ref,
    row_ref, col_ref, back_ref, mid_ref, keep_ref, send_ref, o_s, wo_s, m_s, n_s, q_s, k_s, v_s, a_s, t_s,
):
    me = lax.axis_index("lon")
    tokens = PAIR * KEPT
    pair_columns(me, o_s, mine_ref[0:tokens, :], other_ref[0:tokens, :])
    pair_columns(me, wo_s, mine_ref[tokens:, :], other_ref[tokens:, :])
    for l in range(PAIR):
        rows = slice(KEPT * l, KEPT * (l + 1))
        value = x_ref[l, KEEP0:KEEP1, :].astype(F32) + nn_dot(o_s[rows, :], wo_s[...])
        value = value.astype(BF16)
        m_s[l] = value
        n_s[rows, :] = norm_rows(value.astype(F32), gain_ref[1:2, :])
    mid_ref[...] = m_s[me, PART : PART + WIN, :]
    windows = nn_dot(one_hot(src_ref[...], tokens), n_s[...]).astype(BF16)
    project(windows, w_ref, q_s, k_s, v_s)
    for w in range(4):
        q0, q1 = (KEEP0, WIN) if w < 2 else (0, PART)
        t = WIN * w
        allowed = col_ref[q0:q1, w : w + 1] == row_ref[w : w + 1, :]

        def put(col, value, w=w):
            a_s[PART * w : PART * (w + 1), col : col + 128] = value

        window_attend(
            q_s[t + q0 : t + q1, :],
            k_s[t : t + WIN, :],
            v_s[t : t + WIN, :],
            lambda h, q0=q0, q1=q1: bias_ref[h, q0:q1, :],
            allowed,
            put,
        )
    tiles = nn_dot(one_hot(back_ref[...], 4 * PART), a_s[...]).astype(BF16)
    t_s[0] = tiles[0:WIN]
    t_s[1] = tiles[WIN : 2 * WIN]
    keep_ref[...] = t_s[me]
    send_ref[...] = t_s[1 - me]


def second_call(mine, other, x, gain, weight, bias, row, col):
    tokens = PAIR * KEPT
    qkv = pltpu.VMEM((4 * WIN, MINE), BF16)
    return pl.pallas_call(
        second_kernel,
        out_shape=(
            jax.ShapeDtypeStruct((WIN, D), BF16),
            jax.ShapeDtypeStruct((WIN, MINE), BF16),
            jax.ShapeDtypeStruct((WIN, MINE), BF16),
        ),
        scratch_shapes=[
            pltpu.VMEM((tokens, D), BF16),
            pltpu.VMEM((D, D), BF16),
            pltpu.VMEM((PAIR, KEPT, D), BF16),
            pltpu.VMEM((tokens, D), BF16),
            qkv,
            qkv,
            qkv,
            pltpu.VMEM((4 * PART, MINE), BF16),
            pltpu.VMEM((PAIR, WIN, MINE), BF16),
        ],
        compiler_params=vmem(24),
        cost_estimate=pl.CostEstimate(flops=2 * 10**9, bytes_accessed=4 * 10**6, transcendentals=10**6),
        name="second",
    )(
        mine, other, x, gain, jnp.asarray(window_sources()), weight, bias,
        row, col, jnp.asarray(tile_sources()),
    )


def most_kernel(mid_ref, keep_ref, wo_mine_ref, wo_other_ref, sum_ref, rows_ref, wo_s):
    me = lax.axis_index("lon")
    pair_columns(me, wo_s, wo_mine_ref[...], wo_other_ref[...])
    mine = pl.ds(pl.multiple_of(MINE * me, MINE), MINE)
    rows_ref[...] = wo_s[pl.ds(pl.multiple_of(MINE * (1 - me), MINE), MINE), :]
    sum_ref[...] = mid_ref[...].astype(F32) + nn_dot(keep_ref[...], wo_s[mine, :])


def most_call(mid, keep, wo_mine, wo_other):
    return pl.pallas_call(
        most_kernel,
        out_shape=(jax.ShapeDtypeStruct((WIN, D), F32), jax.ShapeDtypeStruct((MINE, D), BF16)),
        scratch_shapes=[pltpu.VMEM((D, D), BF16)],
        compiler_params=vmem(8),
        cost_estimate=pl.CostEstimate(flops=10**8, bytes_accessed=10**6, transcendentals=0),
        name="most",
    )(mid, keep, wo_mine, wo_other)


def last_kernel(sum_ref, rows_ref, got_ref, out_ref):
    value = sum_ref[...] + nn_dot(got_ref[...], rows_ref[...])
    out_ref[...] = value.reshape(WIN // WZ, WZ, D).astype(BF16)


def last_call(total, rows, got):
    return pl.pallas_call(
        last_kernel,
        out_shape=jax.ShapeDtypeStruct((WIN // WZ, WZ, D), BF16),
        compiler_params=vmem(8),
        cost_estimate=pl.CostEstimate(flops=10**8, bytes_accessed=10**6, transcendentals=0),
        name="last",
    )(total, rows, got)


def sharing(n_lat):
    every = tuple(range(1, n_lat))
    if n_lat == 4:
        return (((0,), every), ((0, 3), (1, 2)))
    return (((0,), every), ((0,), every))


def paired(latent, norm_gain, qkv_weight, out_weight, rel_bias, bias_index, region_ids):
    n_fsdp, n_lat = lax.axis_size("fsdp"), lax.axis_size("lat")
    part = qkv_weight.shape[1] // n_lat
    plan = sharing(n_lat)

    def swap(block):
        return passed_along(block, "lon", 1)

    def spread(block, axis, steps):
        got = []
        for k in steps:
            got.append(heard_from(block, axis, k))
        return got

    part0, part1, tile = open_call(
        jnp.transpose(latent[0], (1, 2, 0, 3)).reshape(WIN // WZ, WZ, D),
        jnp.transpose(region_ids, (1, 0, 2)),
        qkv_weight,
        out_weight,
        part,
        plan[1][0],
    )
    far0 = spread(part0, "fsdp", range(1, n_fsdp))
    before = passed_along(tile, "lat", 1)
    after = passed_along(tile, "lat", -1)
    far1 = spread(part1, "fsdp", range(1, n_fsdp))
    near0 = spread(jnp.concatenate(far0, axis=0), "lat", plan[0][1])
    near1 = spread(jnp.concatenate([f[:part] for f in far1], axis=0), "lat", plan[1][1])
    tall = stack_call(before, tile, after)
    x, normed, tag_row, tag_col = enter_call(tall, swap(tall), norm_gain)
    table = jnp.transpose(rel_bias, (0, 2, 1))
    params = (qkv_weight, out_weight)
    w0, wo0 = join_call(0, n_lat, plan[0][1], plan[0][0], *params, far0, near0)
    bias0, index = bias_call(0, table, bias_index)
    o0 = first_call(normed, w0, bias0, wo0)
    w1, wo1 = join_call(1, n_lat, plan[1][1], plan[1][0], *params, far1, near1)
    bias1 = bias_call(1, table, index)
    mid, keep, send = second_call(o0, swap(o0), x, norm_gain, w1, bias1, tag_row, tag_col)
    total, rows = most_call(mid, keep, wo1, swap(wo1))
    out = last_call(total, rows, swap(send))
    return jnp.transpose(out.reshape(WH, WW, WZ, D), (2, 0, 1, 3))[None]


def solution(mesh):
    pair = mesh.shape["lon"] == PAIR

    def local(latent, norm_gain, qkv_weight, out_weight, *rest):
        one_window = latent.shape[:4] == (1, WZ, WH, WW)
        even = qkv_weight.shape[1] % (16 * mesh.shape["lat"]) == 0
        program = paired if pair and one_window and even else any_mesh
        return program(latent, norm_gain, qkv_weight, out_weight, *rest)

    return jax.shard_map(
        local,
        mesh=mesh,
        in_specs=(
            P("fsdp", None, "lat", "lon", None),
            P(),
            P(None, "fsdp", None),
            P(None, "fsdp", None),
            P(),
            P(),
            P(None, "lat", "lon"),
        ),
        out_specs=P("fsdp", None, "lat", "lon", None),
        check_vma=False,
    )
```

```python
import functools

import jax
import jax.numpy as jnp
import numpy as np
from jax import lax
from jax.experimental import pallas as pl
from jax.experimental.pallas import tpu as pltpu
from jax.sharding import PartitionSpec as P


D = 512
HEADS = 16
HEAD_DIM = 32
WZ = 2
WH = 6
WW = 12
WIN = 144
BIAS_ROWS = 759
HALF = WIN // 2
LOG2E = 1.4426950408889634
SCALE2 = HEAD_DIM ** (-0.5) * LOG2E
NEG = -1e30


def passed_along(block, axis, distance):
    devices = range(lax.axis_size(axis))
    route = [((i - distance) % len(devices), i) for i in devices]
    return lax.ppermute(block, axis, route)


def layer_norm(hidden, gain_row):
    values = hidden.astype(jnp.float32)
    centre = jnp.mean(values, axis=-1, keepdims=True)
    shifted = values - centre
    variance = jnp.mean(shifted * shifted, axis=-1, keepdims=True)
    return (shifted * lax.rsqrt(variance + 1e-05) * gain_row).astype(jnp.bfloat16)


def bias_table(rel_bias, bias_index, block_index):
    return jnp.take(jnp.transpose(rel_bias[block_index]), bias_index, axis=1)


def split_tile(field_tile):
    sample_count, level_count, row_count, col_count, feature_width = field_tile.shape
    pieces = field_tile.reshape(
        sample_count, level_count // WZ, WZ, row_count // WH, WH, col_count // WW, WW, feature_width
    )
    pieces = jnp.transpose(pieces, (0, 1, 3, 5, 2, 4, 6, 7))
    return pieces.reshape(-1, WIN, feature_width)


def merge_tile(windows, tile_shape):
    sample_count, level_count, row_count, col_count, feature_width = tile_shape
    pieces = windows.reshape(
        sample_count, level_count // WZ, row_count // WH, col_count // WW, WZ, WH, WW, feature_width
    )
    pieces = jnp.transpose(pieces, (0, 1, 4, 2, 5, 3, 6, 7))
    return pieces.reshape(tile_shape)


def attend(normed, weight, bias_heads, region_tags):
    packed = jnp.dot(normed.reshape(-1, D), weight, preferred_element_type=jnp.float32).astype(
        jnp.bfloat16
    )
    packed = split_tile(packed.reshape(normed.shape[:-1] + (3 * D,)))
    packed = packed.reshape(-1, WIN, 3, HEADS, HEAD_DIM)
    scores = jnp.einsum(
        "gqhd,gkhd->ghqk", packed[:, :, 0], packed[:, :, 1], preferred_element_type=jnp.float32
    )
    scores = scores * HEAD_DIM ** (-0.5) + bias_heads[None]
    if region_tags is not None:
        window_tags = split_tile(region_tags[..., None])[..., 0]
        allowed = window_tags[:, :, None] == window_tags[:, None, :]
        blocked = jnp.where(allowed, jnp.float32(0.0), -jnp.inf)
        scores = scores + blocked[:, None]
    row_peak = jnp.max(scores, axis=-1, keepdims=True)
    exponent = jnp.exp(scores - row_peak)
    row_total = jnp.sum(exponent, axis=-1, keepdims=True)
    attn_probs = (exponent / row_total).astype(jnp.bfloat16)
    mixed_out = jnp.einsum(
        "ghqk,gkhd->gqhd", attn_probs, packed[:, :, 2], preferred_element_type=jnp.float32
    )
    return merge_tile(mixed_out.astype(jnp.bfloat16).reshape(-1, WIN, D), normed.shape)


def any_mesh(latent, norm_gain, qkv_weight, out_weight, rel_bias, bias_index, region_ids):
    half_rows = WH // 2
    half_cols = WW // 2
    row_count = latent.shape[2]
    col_count = latent.shape[3]
    gathered_qkv, gathered_out = (
        lax.all_gather(qkv_weight, "fsdp", axis=1, tiled=True),
        lax.all_gather(out_weight, "fsdp", axis=1, tiled=True),
    )

    def fetch_weights(block_index):
        return (gathered_qkv[block_index], gathered_out[block_index])

    first_qkv, first_out = fetch_weights(0)
    normed = layer_norm(latent, norm_gain[0])
    mixed_out = attend(normed, first_qkv, bias_table(rel_bias, bias_index, 0), None)
    projected = jnp.dot(mixed_out.reshape(-1, D), first_out, preferred_element_type=jnp.float32)
    middle = (latent.astype(jnp.float32) + projected.reshape(latent.shape)).astype(jnp.bfloat16)
    second_qkv, second_out = fetch_weights(1)
    normed = jnp.roll(layer_norm(middle, norm_gain[1]), -1, axis=1)
    east_strip = passed_along(normed[:, :, :, :half_cols], "lon", -1)
    widened = jnp.concatenate([normed[:, :, :, half_cols:], east_strip], axis=3)
    north_strip = passed_along(widened[:, :, :half_rows], "lat", -1)
    rolled = jnp.concatenate([widened[:, :, half_rows:], north_strip], axis=2)
    level_pos = lax.broadcasted_iota(jnp.int32, region_ids.shape, 0)
    row_pos = (
        lax.broadcasted_iota(jnp.int32, region_ids.shape, 1) + lax.axis_index("lat") * row_count
    )
    region_tags = region_ids * 4 + (level_pos == region_ids.shape[0] - 1).astype(jnp.int32) * 2
    region_tags = region_tags + (row_pos >= row_count * lax.axis_size("lat") - half_rows).astype(
        jnp.int32
    )
    region_tags = region_tags[None]
    mixed_out = attend(rolled, second_qkv, bias_table(rel_bias, bias_index, 1), region_tags)
    south_strip = passed_along(mixed_out[:, :, row_count - half_rows :], "lat", 1)
    widened = jnp.concatenate([south_strip, mixed_out[:, :, : row_count - half_rows]], axis=2)
    west_strip = passed_along(widened[:, :, :, col_count - half_cols :], "lon", 1)
    mixed_out = jnp.concatenate([west_strip, widened[:, :, :, : col_count - half_cols]], axis=3)
    mixed_out = jnp.roll(mixed_out, 1, axis=1)
    projected = jnp.dot(mixed_out.reshape(-1, D), second_out, preferred_element_type=jnp.float32)
    return (middle.astype(jnp.float32) + projected.reshape(latent.shape)).astype(jnp.bfloat16)


PAIR = 2
MY_HEADS = HEADS // PAIR
MINE = MY_HEADS * HEAD_DIM
QKV = 3 * MINE
OUT = D // PAIR
COLS = QKV + OUT
TALL = 3 * WIN
KEEP0 = 64
KEEP1 = TALL - 64
KEPT = KEEP1 - KEEP0
PART = WIN - KEEP0
REGION_ROWS = 8
GROUP = 128 // HEAD_DIM
F32 = jnp.float32
BF16 = jnp.bfloat16


def vmem(mib):
    return pltpu.CompilerParams(vmem_limit_bytes=mib * 2**20)


def partner(index, step, size):
    if size & (size - 1) == 0:
        return index ^ step
    return (index + size - step) % size


def heard_from(block, axis, step):
    size = lax.axis_size(axis)
    return lax.ppermute(block, axis, [(partner(i, step, size), i) for i in range(size)])


def window_sources():
    src = np.zeros((2, 2, WH, WW, WZ), np.int32)
    for a in range(2):
        for v in range(2):
            for dh in range(WH):
                for dw in range(WW):
                    for dz in range(WZ):
                        row = dh + (WH // 2 if a else -(WH // 2))
                        col = (WW // 2 + WW * v + dw) % (2 * WW)
                        level = (dz + 1) % WZ
                        t = (row + WH) * WW * WZ + (col % WW) * WZ + level
                        src[a, v, dh, dw, dz] = (col // WW) * KEPT + t - KEEP0
    return src.reshape(-1, 1)


def tile_sources():
    src = np.zeros((2, WH, WW, WZ), np.int32)
    for l in range(2):
        for row in range(WH):
            for cw in range(WW):
                for level in range(WZ):
                    a = 0 if row < WH // 2 else 1
                    dh = (row + WH // 2) % WH
                    col = (WW * l + cw - WW // 2) % (2 * WW)
                    dz = (level - 1) % WZ
                    t = dh * WW * WZ + (col % WW) * WZ + dz - (0 if a else KEEP0)
                    src[l, row, cw, level] = (a * 2 + col // WW) * PART + t
    return src.reshape(-1, 1)


def one_hot(sources, width):
    lanes = lax.broadcasted_iota(jnp.int32, (sources.shape[0], width), 1)
    return jnp.where(lanes == sources, 1.0, 0.0).astype(BF16)


def nt_dot(a, b):
    return lax.dot_general(a, b, (((1,), (1,)), ((), ())), preferred_element_type=F32)


def nn_dot(a, b):
    return jnp.dot(a, b, preferred_element_type=F32)


def norm_rows(values, gain_row):
    centre = jnp.mean(values, axis=-1, keepdims=True)
    shifted = values - centre
    variance = jnp.mean(shifted * shifted, axis=-1, keepdims=True)
    return (shifted * lax.rsqrt(variance + 1e-05) * gain_row).astype(BF16)


def gather_heads(b, table_ref, index, table, bias_ref):
    me = lax.axis_index("lon")
    heads = table_ref[b, pl.ds(pl.multiple_of(MY_HEADS * me, MY_HEADS), MY_HEADS), :]
    table[:, 0:BIAS_ROWS] = heads * LOG2E
    chunks = (BIAS_ROWS + 127) // 128

    def look_up(at, put):
        low = at & 127
        chunk = at >> 7
        masks = [chunk == k for k in range(chunks)]
        for h in range(MY_HEADS):
            acc = None
            for k in range(chunks):
                row = jnp.broadcast_to(table[h : h + 1, 128 * k : 128 * k + 128], (8, 128))
                got = jnp.take_along_axis(row, low, axis=1, mode="promise_in_bounds")
                acc = got if acc is None else jnp.where(masks[k], got, acc)
            put(h, acc)

    def step(g, carry):
        rows = pl.ds(pl.multiple_of(g * 8, 8), 8)

        def put(h, value):
            bias_ref[h, rows, 0:128] = value

        look_up(index[rows, 0:128], put)
        return carry

    lax.fori_loop(0, WIN // 8, step, 0, unroll=9)
    rest = WIN - 128
    each = 128 // rest
    groups = WIN // 8
    for first in range(0, groups, each):
        here = range(first, min(first + each, groups))
        pieces = [index[8 * g : 8 * g + 8, 128:WIN] for g in here]
        pieces += [jnp.zeros((8, rest), jnp.int32)] * (each - len(pieces))

        def put(h, value, here=here):
            for r, g in enumerate(here):
                bias_ref[h, 8 * g : 8 * g + 8, 128:WIN] = value[:, rest * r : rest * (r + 1)]

        look_up(jnp.concatenate(pieces, axis=1), put)


def bias0_kernel(table_ref, index_ref, bias_ref, moved_ref, table):
    to = lax.broadcasted_iota(jnp.int32, (WIN, WIN), 0)
    frm = lax.broadcasted_iota(jnp.int32, (WIN, WIN), 1)
    move = jnp.where((to & 1) * HALF + (to >> 1) == frm, 1.0, 0.0).astype(BF16)
    whole = index_ref[...]
    parts = jnp.concatenate([whole >> 8, whole & 255], axis=0).astype(F32).astype(BF16)
    parts = nt_dot(parts, move).astype(BF16)
    moved_ref[...] = (
        nn_dot(move, parts[0:WIN]) * 256.0 + nn_dot(move, parts[WIN : 2 * WIN])
    ).astype(jnp.int32)
    gather_heads(0, table_ref, moved_ref, table, bias_ref)


def bias1_kernel(table_ref, index_ref, bias_ref, table):
    gather_heads(1, table_ref, index_ref, table, bias_ref)


def bias_call(b, table, index):
    bias = jax.ShapeDtypeStruct((MY_HEADS, WIN, WIN), F32)
    moved = jax.ShapeDtypeStruct((WIN, WIN), jnp.int32)
    return pl.pallas_call(
        bias1_kernel if b else bias0_kernel,
        out_shape=bias if b else (bias, moved),
        scratch_shapes=[pltpu.VMEM((MY_HEADS, (BIAS_ROWS + 127) // 128 * 128), F32)],
        compiler_params=vmem(8),
        cost_estimate=pl.CostEstimate(flops=10**9, bytes_accessed=10**6, transcendentals=0),
    )(table, index)


def columns(qkv_ref, out_ref, b, rows, me, dst, at, sems):
    mine = pl.ds(pl.multiple_of(MINE * me, MINE), MINE)
    sources = [
        qkv_ref.at[b, rows, pl.ds(pl.multiple_of(D * k + MINE * me, MINE), MINE)] for k in range(3)
    ]
    sources += [out_ref.at[b, rows, mine]]
    to = pl.ds(at, rows.size)
    return [
        pltpu.make_async_copy(source, dst.at[to, pl.ds(MINE * k, MINE)], sems.at[k])
        for k, source in enumerate(sources)
    ]


def open_kernel(
    wide, latent_ref, region_ref, qkv_ref, out_ref, part0_ref, part1_ref, tile_ref,
    latent, regions, sems, own_sems,
):
    part = part0_ref.shape[0]
    me, lat = lax.axis_index("lon"), lax.axis_index("lat")

    def cut(b, dst, step, at, n):
        rows = pl.ds(pl.multiple_of((lat ^ step) * part, part), part)
        return columns(qkv_ref, out_ref, b, rows, me, dst, at, sems.at[n])

    copies = cut(0, part0_ref, 0, 0, 0)
    for i, step in enumerate(wide):
        copies += cut(1, part1_ref, step, part * i, 1 + i)
    inputs = [
        pltpu.make_async_copy(latent_ref, latent, own_sems.at[0]),
        pltpu.make_async_copy(region_ref, regions, own_sems.at[1]),
    ]
    for copy in copies + inputs:
        copy.start()
    for copy in inputs:
        copy.wait()
    tile_ref[0:WIN, :] = latent[...].reshape(WIN, D)
    col = lax.broadcasted_iota(jnp.int32, (WW, WIN), 0)
    token = lax.broadcasted_iota(jnp.int32, (WW, WIN), 1)
    spread = jnp.where(token % (WW * WZ) // WZ == col, 1.0, 0.0).astype(BF16)
    level = lax.broadcasted_iota(jnp.int32, (WZ, WIN), 0)
    token = lax.broadcasted_iota(jnp.int32, (WZ, WIN), 1)
    total = jnp.zeros((WZ, WIN), F32)
    for dh in range(WH):
        here = (token // (WW * WZ) == dh) & (token % WZ == level)
        total += jnp.where(here, nn_dot(regions[dh].astype(F32).astype(BF16), spread), 0.0)
    row = jnp.sum(total, axis=0, keepdims=True)
    tile_ref[WIN : WIN + REGION_ROWS, 0:WIN] = jnp.broadcast_to(row, (REGION_ROWS, WIN)).astype(BF16)
    tile_ref[WIN : WIN + REGION_ROWS, WIN:D] = jnp.zeros((REGION_ROWS, D - WIN), BF16)
    for copy in copies:
        copy.wait()


STAY = pl.BlockSpec(memory_space=pltpu.HBM)


def open_call(latent, regions, qkv, out, part, wide):
    return pl.pallas_call(
        functools.partial(open_kernel, wide),
        out_shape=(
            jax.ShapeDtypeStruct((part, COLS), BF16),
            jax.ShapeDtypeStruct((part * len(wide), COLS), BF16),
            jax.ShapeDtypeStruct((WIN + REGION_ROWS, D), BF16),
        ),
        in_specs=[STAY] * 4,
        scratch_shapes=[
            pltpu.VMEM(latent.shape, BF16),
            pltpu.VMEM(regions.shape, jnp.int32),
            pltpu.SemaphoreType.DMA((1 + len(wide), 4)),
            pltpu.SemaphoreType.DMA((2,)),
        ],
        compiler_params=pltpu.CompilerParams(vmem_limit_bytes=67043328-400*1024),
        cost_estimate=pl.CostEstimate(flops=10**6, bytes_accessed=10**6, transcendentals=0),
        name="open",
    )(latent, regions, qkv, out)


def enter_kernel(mirrored, *refs):
    mine, other = refs[0:3], refs[3:6]
    gain_ref, x_ref, n_ref, row_ref, col_ref = refs[6:]
    me = lax.axis_index("lon")
    n_lat = lax.axis_size("lat")
    lat = lax.axis_index("lat")
    odd = lat & 1 if mirrored else 1
    places = (2 - 2 * odd, 1, 2 * odd)
    for k, place in enumerate(places):
        rows = pl.ds(pl.multiple_of(WIN * place, WIN), WIN)
        for ref, l in ((mine[k], me), (other[k], 1 - me)):
            tokens = ref[0:WIN, :]
            x_ref[l, rows, :] = tokens
            n_ref[l, rows, :] = norm_rows(tokens.astype(F32), gain_ref[0:1, :])
    lanes = lax.broadcasted_iota(jnp.int32, (1, WIN), 1)
    level = lanes & 1
    dh = lanes // (WW * WZ)

    def regions(three):
        found = [ref[WIN : WIN + REGION_ROWS, 0:WIN].astype(F32)[0:1] for ref in three]
        return jnp.where(odd == 1, found[0], found[2]), found[1]

    rows = []
    for a, (own, pair) in enumerate(zip(regions(mine), regions(other))):
        window = (lat + n_lat - 1 + a) % n_lat
        late = window * WH + dh >= n_lat * WH - WH // 2
        extra = jnp.where(level == WZ - 1, 2.0, 0.0) + jnp.where(late, 1.0, 0.0)
        west = jnp.where(me == 0, own, pair)
        east = jnp.where(me == 0, pair, own)
        rows += [4.0 * west + extra, 4.0 * east + extra]
    tags = jnp.concatenate(rows + rows, axis=0)
    row_ref[...] = tags
    to = lax.broadcasted_iota(jnp.int32, (WIN, WIN), 0)
    frm = lax.broadcasted_iota(jnp.int32, (WIN, WIN), 1)
    col_ref[...] = nt_dot(jnp.where(to == frm, 1.0, 0.0).astype(BF16), tags.astype(BF16))


def enter_call(mirrored, mine, other, gain):
    return pl.pallas_call(
        functools.partial(enter_kernel, mirrored),
        out_shape=(
            jax.ShapeDtypeStruct((PAIR, TALL, D), BF16),
            jax.ShapeDtypeStruct((PAIR, TALL, D), BF16),
            jax.ShapeDtypeStruct((8, WIN), F32),
            jax.ShapeDtypeStruct((WIN, 8), F32),
        ),
        compiler_params=vmem(16),
        cost_estimate=pl.CostEstimate(flops=10**8, bytes_accessed=2 * 10**6, transcendentals=0),
        name="enter",
    )(*mine, *other, gain)


def join_kernel(b, n_fsdp, n_lat, steps, wide, own_qkv_ref, own_out_ref, *refs):
    far, near = refs[: n_fsdp - 1], refs[n_fsdp - 1 : n_fsdp - 1 + len(steps)]
    qkv_ref, out_ref = refs[-2:]
    z, lat = lax.axis_index("fsdp"), lax.axis_index("lat")
    depth = own_qkv_ref.shape[1]
    part = depth // n_lat
    me = lax.axis_index("lon")

    def put(first, size, piece):
        rows = pl.ds(pl.multiple_of(first, size), size)
        qkv_ref[rows, :] = piece[:, 0:QKV]
        out_ref[rows, :] = piece[:, QKV:COLS]

    own = pl.ds(pl.multiple_of(z * depth, depth), depth)
    for k in range(3):
        mine = pl.ds(pl.multiple_of(D * k + MINE * me, MINE), MINE)
        qkv_ref[own, MINE * k : MINE * (k + 1)] = own_qkv_ref[b, :, mine]
    out_ref[own, :] = own_out_ref[b, :, pl.ds(pl.multiple_of(OUT * me, OUT), OUT)]
    for k in range(1, n_fsdp):
        base = partner(z, k, n_fsdp) * depth
        for i, step in enumerate(wide):
            put(base + (lat ^ step) * part, part, far[k - 1][part * i : part * (i + 1), :])
        for j, step in enumerate(steps):
            row = base + partner(lat, step, n_lat) * part
            put(row, part, near[j][part * (k - 1) : part * k, :])


def join_call(b, n_lat, steps, wide, qkv, out, far, near):
    rows = qkv.shape[1] * (len(far) + 1)
    return pl.pallas_call(
        functools.partial(join_kernel, b, len(far) + 1, n_lat, steps, wide),
        out_shape=(
            jax.ShapeDtypeStruct((rows, QKV), BF16),
            jax.ShapeDtypeStruct((rows, OUT), BF16),
        ),
        compiler_params=vmem(8),
        cost_estimate=pl.CostEstimate(flops=10**6, bytes_accessed=2 * 10**6, transcendentals=0),
    )(qkv, out, *far, *near)


def window_attend(q, k, v, bias_at, allowed, put):
    n = q.shape[0]
    lanes = lax.broadcasted_iota(jnp.int32, (n, 128), 1)
    owns = [(lanes >= HEAD_DIM * j) & (lanes < HEAD_DIM * (j + 1)) for j in range(GROUP)]
    ones = jnp.ones((WIN, 128), BF16)
    for g in range(MINE // 128):
        cols = slice(128 * g, 128 * (g + 1))
        q_g = q[:, cols]
        k_g = k[:, cols]
        v_g = jnp.concatenate([v[:, cols], ones], axis=1)
        q_all = jnp.concatenate([jnp.where(o, q_g, jnp.zeros_like(q_g)) for o in owns], axis=0)
        scores = nt_dot(q_all, k_g)
        probs = []
        for j in range(GROUP):
            s = scores[n * j : n * (j + 1)] * SCALE2 + bias_at(GROUP * g + j)
            if allowed is not None:
                s = jnp.where(allowed, s, NEG)
            peak = jnp.max(s, axis=-1, keepdims=True)
            probs.append(jnp.exp2(s - peak).astype(BF16))
        mixed = nn_dot(jnp.concatenate(probs, axis=0), v_g)
        acc = None
        for j in range(GROUP):
            m = mixed[n * j : n * (j + 1)]
            value = m[:, 0:128] / m[:, 128:256]
            acc = value if acc is None else jnp.where(owns[j], value, acc)
        put(128 * g, acc.astype(BF16))


def project(n, w_ref, q_s, k_s, v_s):
    both = nn_dot(n, w_ref[...]).astype(BF16)
    q_s[...] = both[:, 0:MINE]
    k_s[...] = both[:, MINE : 2 * MINE]
    v_s[...] = both[:, 2 * MINE : 3 * MINE]


def first_kernel(n_ref, w_ref, bias_ref, wo_ref, o_ref, q_s, k_s, v_s):
    o_ref[PAIR * KEPT :, :] = wo_ref[...]
    project(n_ref[...].reshape(PAIR * TALL, D), w_ref, q_s, k_s, v_s)
    for l in range(PAIR):
        for part, (q0, q1, o0) in enumerate(
            ((KEEP0, WIN, 0), (0, WIN, PART), (0, PART, PART + WIN))
        ):
            t = TALL * l + WIN * part

            def put(col, value, l=l, o0=o0, q0=q0, q1=q1):
                o_ref[KEPT * l + o0 : KEPT * l + o0 + q1 - q0, col : col + 128] = value

            window_attend(
                q_s[t + q0 : t + q1, :],
                k_s[t : t + WIN, :],
                v_s[t : t + WIN, :],
                lambda h, q0=q0, q1=q1: bias_ref[h, q0:q1, :],
                None,
                put,
            )


def first_call(normed, weight, bias, wo):
    scratch = pltpu.VMEM((PAIR * TALL, MINE), BF16)
    return pl.pallas_call(
        first_kernel,
        out_shape=jax.ShapeDtypeStruct((PAIR * KEPT + D, MINE), BF16),
        scratch_shapes=[scratch, scratch, scratch],
        compiler_params=vmem(24),
        cost_estimate=pl.CostEstimate(flops=2 * 10**9, bytes_accessed=4 * 10**6, transcendentals=10**6),
        name="first",
    )(normed, weight, bias, wo)


def pair_columns(me, ref, mine, other):
    width = mine.shape[-1]
    ref[:, pl.ds(pl.multiple_of(width * me, width), width)] = mine
    ref[:, pl.ds(pl.multiple_of(width * (1 - me), width), width)] = other


def second_kernel(
    mine_ref, other_ref, x_ref, gain_ref, src_ref, w_ref, bias_ref,
    row_ref, col_ref, back_ref, mid_ref, keep_ref, send_ref, o_s, wo_s, m_s, n_s, q_s, k_s, v_s, a_s, t_s,
):
    me = lax.axis_index("lon")
    tokens = PAIR * KEPT
    pair_columns(me, o_s, mine_ref[0:tokens, :], other_ref[0:tokens, :])
    pair_columns(me, wo_s, mine_ref[tokens:, :], other_ref[tokens:, :])
    for l in range(PAIR):
        rows = slice(KEPT * l, KEPT * (l + 1))
        value = x_ref[l, KEEP0:KEEP1, :].astype(F32) + nn_dot(o_s[rows, :], wo_s[...])
        value = value.astype(BF16)
        m_s[l] = value
        n_s[rows, :] = norm_rows(value.astype(F32), gain_ref[1:2, :])
    mid_ref[...] = m_s[me, PART : PART + WIN, :]
    windows = nn_dot(one_hot(src_ref[...], tokens), n_s[...]).astype(BF16)
    project(windows, w_ref, q_s, k_s, v_s)
    for w in range(4):
        q0, q1 = (KEEP0, WIN) if w < 2 else (0, PART)
        t = WIN * w
        allowed = col_ref[q0:q1, w : w + 1] == row_ref[w : w + 1, :]

        def put(col, value, w=w):
            a_s[PART * w : PART * (w + 1), col : col + 128] = value

        window_attend(
            q_s[t + q0 : t + q1, :],
            k_s[t : t + WIN, :],
            v_s[t : t + WIN, :],
            lambda h, q0=q0, q1=q1: bias_ref[h, q0:q1, :],
            allowed,
            put,
        )
    tiles = nn_dot(one_hot(back_ref[...], 4 * PART), a_s[...]).astype(BF16)
    t_s[0] = tiles[0:WIN]
    t_s[1] = tiles[WIN : 2 * WIN]
    keep_ref[...] = t_s[me]
    send_ref[...] = t_s[1 - me]


def second_call(mine, other, x, gain, weight, bias, row, col):
    tokens = PAIR * KEPT
    qkv = pltpu.VMEM((4 * WIN, MINE), BF16)
    return pl.pallas_call(
        second_kernel,
        out_shape=(
            jax.ShapeDtypeStruct((WIN, D), BF16),
            jax.ShapeDtypeStruct((WIN, MINE), BF16),
            jax.ShapeDtypeStruct((WIN, MINE), BF16),
        ),
        scratch_shapes=[
            pltpu.VMEM((tokens, D), BF16),
            pltpu.VMEM((D, D), BF16),
            pltpu.VMEM((PAIR, KEPT, D), BF16),
            pltpu.VMEM((tokens, D), BF16),
            qkv,
            qkv,
            qkv,
            pltpu.VMEM((4 * PART, MINE), BF16),
            pltpu.VMEM((PAIR, WIN, MINE), BF16),
        ],
        compiler_params=vmem(24),
        cost_estimate=pl.CostEstimate(flops=2 * 10**9, bytes_accessed=4 * 10**6, transcendentals=10**6),
        name="second",
    )(
        mine, other, x, gain, jnp.asarray(window_sources()), weight, bias,
        row, col, jnp.asarray(tile_sources()),
    )


def most_kernel(mid_ref, keep_ref, wo_mine_ref, wo_other_ref, sum_ref, rows_ref, wo_s):
    me = lax.axis_index("lon")
    pair_columns(me, wo_s, wo_mine_ref[...], wo_other_ref[...])
    mine = pl.ds(pl.multiple_of(MINE * me, MINE), MINE)
    rows_ref[...] = wo_s[pl.ds(pl.multiple_of(MINE * (1 - me), MINE), MINE), :]
    sum_ref[...] = mid_ref[...].astype(F32) + nn_dot(keep_ref[...], wo_s[mine, :])


def most_call(mid, keep, wo_mine, wo_other):
    return pl.pallas_call(
        most_kernel,
        out_shape=(jax.ShapeDtypeStruct((WIN, D), F32), jax.ShapeDtypeStruct((MINE, D), BF16)),
        scratch_shapes=[pltpu.VMEM((D, D), BF16)],
        compiler_params=vmem(8),
        cost_estimate=pl.CostEstimate(flops=10**8, bytes_accessed=10**6, transcendentals=0),
        name="most",
    )(mid, keep, wo_mine, wo_other)


def last_kernel(sum_ref, rows_ref, got_ref, out_ref):
    value = sum_ref[...] + nn_dot(got_ref[...], rows_ref[...])
    out_ref[...] = value.reshape(WIN // WZ, WZ, D).astype(BF16)


def last_call(total, rows, got):
    return pl.pallas_call(
        last_kernel,
        out_shape=jax.ShapeDtypeStruct((WIN // WZ, WZ, D), BF16),
        compiler_params=vmem(8),
        cost_estimate=pl.CostEstimate(flops=10**8, bytes_accessed=10**6, transcendentals=0),
        name="last",
    )(total, rows, got)


def sharing(n_lat):
    every = tuple(range(1, n_lat))
    if n_lat == 4:
        return (((0,), every), ((0, 3), (1, 2)))
    return (((0,), every), ((0,), every))


def paired(latent, norm_gain, qkv_weight, out_weight, rel_bias, bias_index, region_ids):
    n_fsdp, n_lat = lax.axis_size("fsdp"), lax.axis_size("lat")
    part = qkv_weight.shape[1] // n_lat
    plan = sharing(n_lat)

    def swap(block):
        return passed_along(block, "lon", 1)

    def spread(block, axis, steps):
        got = []
        for k in steps:
            got.append(heard_from(block, axis, k))
        return got

    part0, part1, tile = open_call(
        jnp.transpose(latent[0], (1, 2, 0, 3)).reshape(WIN // WZ, WZ, D),
        jnp.transpose(region_ids, (1, 0, 2)),
        qkv_weight,
        out_weight,
        part,
        plan[1][0],
    )
    far0 = spread(part0, "fsdp", range(1, n_fsdp))
    mirrored = n_lat == 4
    side = heard_from(tile, "lat", 1) if mirrored else passed_along(tile, "lat", 1)
    cross = heard_from(side, "lat", 2) if mirrored else passed_along(tile, "lat", -1)
    far1 = spread(part1, "fsdp", range(1, n_fsdp))
    near0 = spread(jnp.concatenate(far0, axis=0), "lat", plan[0][1])
    near1 = spread(jnp.concatenate([f[:part] for f in far1], axis=0), "lat", plan[1][1])
    three = (side, tile, cross)
    pair = [swap(t) for t in three]
    x, normed, tag_row, tag_col = enter_call(mirrored, three, pair, norm_gain)
    table = jnp.transpose(rel_bias, (0, 2, 1))
    params = (qkv_weight, out_weight)
    w0, wo0 = join_call(0, n_lat, plan[0][1], plan[0][0], *params, far0, near0)
    bias0, index = bias_call(0, table, bias_index)
    o0 = first_call(normed, w0, bias0, wo0)
    w1, wo1 = join_call(1, n_lat, plan[1][1], plan[1][0], *params, far1, near1)
    bias1 = bias_call(1, table, index)
    mid, keep, send = second_call(o0, swap(o0), x, norm_gain, w1, bias1, tag_row, tag_col)
    total, rows = most_call(mid, keep, wo1, swap(wo1))
    out = last_call(total, rows, swap(send))
    return jnp.transpose(out.reshape(WH, WW, WZ, D), (2, 0, 1, 3))[None]


def solution(mesh):
    pair = mesh.shape["lon"] == PAIR

    def local(latent, norm_gain, qkv_weight, out_weight, *rest):
        one_window = latent.shape[:4] == (1, WZ, WH, WW)
        even = qkv_weight.shape[1] % (16 * mesh.shape["lat"]) == 0
        program = paired if pair and one_window and even else any_mesh
        return program(latent, norm_gain, qkv_weight, out_weight, *rest)

    return jax.shard_map(
        local,
        mesh=mesh,
        in_specs=(
            P("fsdp", None, "lat", "lon", None),
            P(),
            P(None, "fsdp", None),
            P(None, "fsdp", None),
            P(),
            P(),
            P(None, "lat", "lon"),
        ),
        out_specs=P("fsdp", None, "lat", "lon", None),
        check_vma=False,
    )
```

```python
import functools

import jax
import jax.numpy as jnp
from jax import lax
from jax.experimental import pallas as pl
from jax.experimental.pallas import tpu as pltpu
from jax.sharding import PartitionSpec as P


D = 512
HEADS = 16
HEAD_DIM = 32
WZ = 2
WH = 6
WW = 12
WIN = 144
BIAS_ROWS = 759
HALF = WIN // 2
LOG2E = 1.4426950408889634
SCALE2 = HEAD_DIM ** (-0.5) * LOG2E
NEG = -1e30


def passed_along(block, axis, distance):
    devices = range(lax.axis_size(axis))
    route = [((i - distance) % len(devices), i) for i in devices]
    return lax.ppermute(block, axis, route)


def layer_norm(hidden, gain_row):
    values = hidden.astype(jnp.float32)
    centre = jnp.mean(values, axis=-1, keepdims=True)
    shifted = values - centre
    variance = jnp.mean(shifted * shifted, axis=-1, keepdims=True)
    return (shifted * lax.rsqrt(variance + 1e-05) * gain_row).astype(jnp.bfloat16)


def bias_table(rel_bias, bias_index, block_index):
    return jnp.take(jnp.transpose(rel_bias[block_index]), bias_index, axis=1)


def split_tile(field_tile):
    sample_count, level_count, row_count, col_count, feature_width = field_tile.shape
    pieces = field_tile.reshape(
        sample_count, level_count // WZ, WZ, row_count // WH, WH, col_count // WW, WW, feature_width
    )
    pieces = jnp.transpose(pieces, (0, 1, 3, 5, 2, 4, 6, 7))
    return pieces.reshape(-1, WIN, feature_width)


def merge_tile(windows, tile_shape):
    sample_count, level_count, row_count, col_count, feature_width = tile_shape
    pieces = windows.reshape(
        sample_count, level_count // WZ, row_count // WH, col_count // WW, WZ, WH, WW, feature_width
    )
    pieces = jnp.transpose(pieces, (0, 1, 4, 2, 5, 3, 6, 7))
    return pieces.reshape(tile_shape)


def attend(normed, weight, bias_heads, region_tags):
    packed = jnp.dot(normed.reshape(-1, D), weight, preferred_element_type=jnp.float32).astype(
        jnp.bfloat16
    )
    packed = split_tile(packed.reshape(normed.shape[:-1] + (3 * D,)))
    packed = packed.reshape(-1, WIN, 3, HEADS, HEAD_DIM)
    scores = jnp.einsum(
        "gqhd,gkhd->ghqk", packed[:, :, 0], packed[:, :, 1], preferred_element_type=jnp.float32
    )
    scores = scores * HEAD_DIM ** (-0.5) + bias_heads[None]
    if region_tags is not None:
        window_tags = split_tile(region_tags[..., None])[..., 0]
        allowed = window_tags[:, :, None] == window_tags[:, None, :]
        blocked = jnp.where(allowed, jnp.float32(0.0), -jnp.inf)
        scores = scores + blocked[:, None]
    row_peak = jnp.max(scores, axis=-1, keepdims=True)
    exponent = jnp.exp(scores - row_peak)
    row_total = jnp.sum(exponent, axis=-1, keepdims=True)
    attn_probs = (exponent / row_total).astype(jnp.bfloat16)
    mixed_out = jnp.einsum(
        "ghqk,gkhd->gqhd", attn_probs, packed[:, :, 2], preferred_element_type=jnp.float32
    )
    return merge_tile(mixed_out.astype(jnp.bfloat16).reshape(-1, WIN, D), normed.shape)


def any_mesh(latent, norm_gain, qkv_weight, out_weight, rel_bias, bias_index, region_ids):
    half_rows = WH // 2
    half_cols = WW // 2
    row_count = latent.shape[2]
    col_count = latent.shape[3]
    gathered_qkv, gathered_out = (
        lax.all_gather(qkv_weight, "fsdp", axis=1, tiled=True),
        lax.all_gather(out_weight, "fsdp", axis=1, tiled=True),
    )

    def fetch_weights(block_index):
        return (gathered_qkv[block_index], gathered_out[block_index])

    first_qkv, first_out = fetch_weights(0)
    normed = layer_norm(latent, norm_gain[0])
    mixed_out = attend(normed, first_qkv, bias_table(rel_bias, bias_index, 0), None)
    projected = jnp.dot(mixed_out.reshape(-1, D), first_out, preferred_element_type=jnp.float32)
    middle = (latent.astype(jnp.float32) + projected.reshape(latent.shape)).astype(jnp.bfloat16)
    second_qkv, second_out = fetch_weights(1)
    normed = jnp.roll(layer_norm(middle, norm_gain[1]), -1, axis=1)
    east_strip = passed_along(normed[:, :, :, :half_cols], "lon", -1)
    widened = jnp.concatenate([normed[:, :, :, half_cols:], east_strip], axis=3)
    north_strip = passed_along(widened[:, :, :half_rows], "lat", -1)
    rolled = jnp.concatenate([widened[:, :, half_rows:], north_strip], axis=2)
    level_pos = lax.broadcasted_iota(jnp.int32, region_ids.shape, 0)
    row_pos = (
        lax.broadcasted_iota(jnp.int32, region_ids.shape, 1) + lax.axis_index("lat") * row_count
    )
    region_tags = region_ids * 4 + (level_pos == region_ids.shape[0] - 1).astype(jnp.int32) * 2
    region_tags = region_tags + (row_pos >= row_count * lax.axis_size("lat") - half_rows).astype(
        jnp.int32
    )
    region_tags = region_tags[None]
    mixed_out = attend(rolled, second_qkv, bias_table(rel_bias, bias_index, 1), region_tags)
    south_strip = passed_along(mixed_out[:, :, row_count - half_rows :], "lat", 1)
    widened = jnp.concatenate([south_strip, mixed_out[:, :, : row_count - half_rows]], axis=2)
    west_strip = passed_along(widened[:, :, :, col_count - half_cols :], "lon", 1)
    mixed_out = jnp.concatenate([west_strip, widened[:, :, :, : col_count - half_cols]], axis=3)
    mixed_out = jnp.roll(mixed_out, 1, axis=1)
    projected = jnp.dot(mixed_out.reshape(-1, D), second_out, preferred_element_type=jnp.float32)
    return (middle.astype(jnp.float32) + projected.reshape(latent.shape)).astype(jnp.bfloat16)


PAIR = 2
MY_HEADS = HEADS // PAIR
MINE = MY_HEADS * HEAD_DIM
QKV = 3 * MINE
OUT = D // PAIR
COLS = QKV + OUT
TALL = 3 * WIN
KEEP0 = 64
KEEP1 = TALL - 64
KEPT = KEEP1 - KEEP0
PART = WIN - KEEP0
REGION_ROWS = 8
GROUP = 128 // HEAD_DIM
F32 = jnp.float32
BF16 = jnp.bfloat16


def vmem(mib):
    return pltpu.CompilerParams(vmem_limit_bytes=mib * 2**20)


def partner(index, step, size):
    if size & (size - 1) == 0:
        return index ^ step
    return (index + size - step) % size


def heard_from(block, axis, step):
    size = lax.axis_size(axis)
    return lax.ppermute(block, axis, [(partner(i, step, size), i) for i in range(size)])


def as_column(lanes, size):
    return jnp.transpose(lanes.astype(F32))[0:size, 0:1].astype(jnp.int32)


def window_sources():
    token = lax.broadcasted_iota(jnp.int32, (8, 5 * 128), 1)
    a, v = token // (2 * WIN), token // WIN % 2
    dh, dw, dz = token % WIN // (WW * WZ), token % (WW * WZ) // WZ, token % WZ
    row = dh + WH * a - WH // 2
    col = (WW // 2 + WW * v + dw) % (2 * WW)
    level = (dz + 1) % WZ
    return as_column(col // WW * KEPT + (row + WH) * WW * WZ + col % WW * WZ + level - KEEP0, 4 * WIN)


def tile_sources():
    token = lax.broadcasted_iota(jnp.int32, (8, 3 * 128), 1)
    tile = token // WIN
    row, cw, level = token % WIN // (WW * WZ), token % (WW * WZ) // WZ, token % WZ
    a = row // (WH // 2)
    dh = (row + WH // 2) % WH
    col = (WW * tile + cw + 2 * WW - WW // 2) % (2 * WW)
    dz = (level + WZ - 1) % WZ
    found = (a * 2 + col // WW) * PART + dh * WW * WZ + col % WW * WZ + dz - KEEP0 * (1 - a)
    return as_column(found, 2 * WIN)


def one_hot(sources, width):
    lanes = lax.broadcasted_iota(jnp.int32, (sources.shape[0], width), 1)
    return jnp.where(lanes == sources, 1.0, 0.0).astype(BF16)


def nt_dot(a, b):
    return lax.dot_general(a, b, (((1,), (1,)), ((), ())), preferred_element_type=F32)


def nn_dot(a, b):
    return jnp.dot(a, b, preferred_element_type=F32)


def norm_rows(values, gain_row):
    centre = jnp.mean(values, axis=-1, keepdims=True)
    shifted = values - centre
    variance = jnp.mean(shifted * shifted, axis=-1, keepdims=True)
    return (shifted * lax.rsqrt(variance + 1e-05) * gain_row).astype(BF16)


def gather_heads(b, start, table_ref, index, table, bias_ref):
    me = lax.axis_index("lon")
    heads = table_ref[b, pl.ds(pl.multiple_of(MY_HEADS * me, MY_HEADS), MY_HEADS), :]
    table[:, 0:BIAS_ROWS] = heads * LOG2E
    chunks = (BIAS_ROWS + 127) // 128

    def look_up(at, put):
        low = at & 127
        chunk = at >> 7
        masks = [chunk == k for k in range(chunks)]
        for h in range(bias_ref.shape[0]):
            acc = None
            at_h = slice(start + h, start + h + 1)
            for k in range(chunks):
                row = jnp.broadcast_to(table[at_h, 128 * k : 128 * k + 128], (8, 128))
                got = jnp.take_along_axis(row, low, axis=1, mode="promise_in_bounds")
                acc = got if acc is None else jnp.where(masks[k], got, acc)
            put(h, acc)

    def step(g, carry):
        rows = pl.ds(pl.multiple_of(g * 8, 8), 8)

        def put(h, value):
            bias_ref[h, rows, 0:128] = value

        look_up(index[rows, 0:128], put)
        return carry

    lax.fori_loop(0, WIN // 8, step, 0, unroll=9)
    rest = WIN - 128
    each = 128 // rest
    groups = WIN // 8
    for first in range(0, groups, each):
        here = range(first, min(first + each, groups))
        pieces = [index[8 * g : 8 * g + 8, 128:WIN] for g in here]
        pieces += [jnp.zeros((8, rest), jnp.int32)] * (each - len(pieces))

        def put(h, value, here=here):
            for r, g in enumerate(here):
                bias_ref[h, 8 * g : 8 * g + 8, 128:WIN] = value[:, rest * r : rest * (r + 1)]

        look_up(jnp.concatenate(pieces, axis=1), put)


def bias0_kernel(table_ref, index_ref, bias_ref, moved_ref, table):
    to = lax.broadcasted_iota(jnp.int32, (WIN, WIN), 0)
    frm = lax.broadcasted_iota(jnp.int32, (WIN, WIN), 1)
    move = jnp.where((to & 1) * HALF + (to >> 1) == frm, 1.0, 0.0).astype(BF16)
    whole = index_ref[...]
    parts = jnp.concatenate([whole >> 8, whole & 255], axis=0).astype(F32).astype(BF16)
    parts = nt_dot(parts, move).astype(BF16)
    moved_ref[...] = (
        nn_dot(move, parts[0:WIN]) * 256.0 + nn_dot(move, parts[WIN : 2 * WIN])
    ).astype(jnp.int32)
    gather_heads(0, 0, table_ref, moved_ref, table, bias_ref)


def bias1_kernel(start, table_ref, index_ref, bias_ref, table):
    gather_heads(1, start, table_ref, index_ref, table, bias_ref)


def bias_call(kernel, heads, more, table, index):
    bias = jax.ShapeDtypeStruct((heads, WIN, WIN), F32)
    moved = jax.ShapeDtypeStruct((WIN, WIN), jnp.int32)
    return pl.pallas_call(
        kernel,
        out_shape=(bias, moved) if more else bias,
        scratch_shapes=[pltpu.VMEM((MY_HEADS, (BIAS_ROWS + 127) // 128 * 128), F32)],
        compiler_params=vmem(8),
        cost_estimate=pl.CostEstimate(flops=10**9, bytes_accessed=10**6, transcendentals=0),
    )(table, index)


def columns(qkv_ref, out_ref, b, rows, me, dst, at, sems):
    mine = pl.ds(pl.multiple_of(MINE * me, MINE), MINE)
    sources = [
        qkv_ref.at[b, rows, pl.ds(pl.multiple_of(D * k + MINE * me, MINE), MINE)] for k in range(3)
    ]
    sources += [out_ref.at[b, rows, mine]]
    to = pl.ds(at, rows.size)
    return [
        pltpu.make_async_copy(source, dst.at[to, pl.ds(MINE * k, MINE)], sems.at[k])
        for k, source in enumerate(sources)
    ]


def open_kernel(
    wide, latent_ref, region_ref, qkv_ref, out_ref, part0_ref, part1_ref, tile_ref,
    latent, regions, sems, own_sems,
):
    part = part0_ref.shape[0]
    me, lat = lax.axis_index("lon"), lax.axis_index("lat")

    def cut(b, dst, step, at, n):
        rows = pl.ds(pl.multiple_of((lat ^ step) * part, part), part)
        return columns(qkv_ref, out_ref, b, rows, me, dst, at, sems.at[n])

    copies = cut(0, part0_ref, 0, 0, 0)
    for i, step in enumerate(wide):
        copies += cut(1, part1_ref, step, part * i, 1 + i)
    inputs = [
        pltpu.make_async_copy(latent_ref, latent, own_sems.at[0]),
        pltpu.make_async_copy(region_ref, regions, own_sems.at[1]),
    ]
    for copy in copies + inputs:
        copy.start()
    for copy in inputs:
        copy.wait()
    tile_ref[0:WIN, :] = latent[...].reshape(WIN, D)
    col = lax.broadcasted_iota(jnp.int32, (WW, WIN), 0)
    token = lax.broadcasted_iota(jnp.int32, (WW, WIN), 1)
    spread = jnp.where(token % (WW * WZ) // WZ == col, 1.0, 0.0).astype(BF16)
    level = lax.broadcasted_iota(jnp.int32, (WZ, WIN), 0)
    token = lax.broadcasted_iota(jnp.int32, (WZ, WIN), 1)
    total = jnp.zeros((WZ, WIN), F32)
    for dh in range(WH):
        here = (token // (WW * WZ) == dh) & (token % WZ == level)
        total += jnp.where(here, nn_dot(regions[dh].astype(F32).astype(BF16), spread), 0.0)
    row = jnp.sum(total, axis=0, keepdims=True)
    tile_ref[WIN : WIN + REGION_ROWS, 0:WIN] = jnp.broadcast_to(row, (REGION_ROWS, WIN)).astype(BF16)
    tile_ref[WIN : WIN + REGION_ROWS, WIN:D] = jnp.zeros((REGION_ROWS, D - WIN), BF16)
    for copy in copies:
        copy.wait()


STAY = pl.BlockSpec(memory_space=pltpu.HBM)


def open_call(latent, regions, qkv, out, part, wide):
    return pl.pallas_call(
        functools.partial(open_kernel, wide),
        out_shape=(
            jax.ShapeDtypeStruct((part, COLS), BF16),
            jax.ShapeDtypeStruct((part * len(wide), COLS), BF16),
            jax.ShapeDtypeStruct((WIN + REGION_ROWS, D), BF16),
        ),
        in_specs=[STAY] * 4,
        scratch_shapes=[
            pltpu.VMEM(latent.shape, BF16),
            pltpu.VMEM(regions.shape, jnp.int32),
            pltpu.SemaphoreType.DMA((1 + len(wide), 4)),
            pltpu.SemaphoreType.DMA((2,)),
        ],
        compiler_params=pltpu.CompilerParams(vmem_limit_bytes=67043328-400*1024),
        cost_estimate=pl.CostEstimate(flops=10**6, bytes_accessed=10**6, transcendentals=0),
        name="open",
    )(latent, regions, qkv, out)


def enter_kernel(mirrored, *refs):
    mine, other = refs[0:3], refs[3:6]
    gain_ref, x_ref, n_ref, row_ref, col_ref = refs[6:]
    me = lax.axis_index("lon")
    n_lat = lax.axis_size("lat")
    lat = lax.axis_index("lat")
    odd = lat & 1 if mirrored else 1
    places = (2 - 2 * odd, 1, 2 * odd)
    for k, place in enumerate(places):
        rows = pl.ds(pl.multiple_of(WIN * place, WIN), WIN)
        for ref, l in ((mine[k], me), (other[k], 1 - me)):
            tokens = ref[0:WIN, :]
            x_ref[l, rows, :] = tokens
            n_ref[l, rows, :] = norm_rows(tokens.astype(F32), gain_ref[0:1, :])
    lanes = lax.broadcasted_iota(jnp.int32, (1, WIN), 1)
    level = lanes & 1
    dh = lanes // (WW * WZ)

    def regions(three):
        found = [ref[WIN : WIN + REGION_ROWS, 0:WIN].astype(F32)[0:1] for ref in three]
        return jnp.where(odd == 1, found[0], found[2]), found[1]

    rows = []
    for a, (own, pair) in enumerate(zip(regions(mine), regions(other))):
        window = (lat + n_lat - 1 + a) % n_lat
        late = window * WH + dh >= n_lat * WH - WH // 2
        extra = jnp.where(level == WZ - 1, 2.0, 0.0) + jnp.where(late, 1.0, 0.0)
        west = jnp.where(me == 0, own, pair)
        east = jnp.where(me == 0, pair, own)
        rows += [4.0 * west + extra, 4.0 * east + extra]
    tags = jnp.concatenate(rows + rows, axis=0)
    row_ref[...] = tags
    to = lax.broadcasted_iota(jnp.int32, (WIN, WIN), 0)
    frm = lax.broadcasted_iota(jnp.int32, (WIN, WIN), 1)
    col_ref[...] = nt_dot(jnp.where(to == frm, 1.0, 0.0).astype(BF16), tags.astype(BF16))


def enter_call(mirrored, mine, other, gain):
    return pl.pallas_call(
        functools.partial(enter_kernel, mirrored),
        out_shape=(
            jax.ShapeDtypeStruct((PAIR, TALL, D), BF16),
            jax.ShapeDtypeStruct((PAIR, TALL, D), BF16),
            jax.ShapeDtypeStruct((8, WIN), F32),
            jax.ShapeDtypeStruct((WIN, 8), F32),
        ),
        compiler_params=vmem(16),
        cost_estimate=pl.CostEstimate(flops=10**8, bytes_accessed=2 * 10**6, transcendentals=0),
        name="enter",
    )(*mine, *other, gain)


def join_kernel(b, n_fsdp, n_lat, steps, wide, own_qkv_ref, own_out_ref, *refs):
    far, near = refs[: n_fsdp - 1], refs[n_fsdp - 1 : n_fsdp - 1 + len(steps)]
    qkv_ref, out_ref = refs[-2:]
    z, lat = lax.axis_index("fsdp"), lax.axis_index("lat")
    depth = own_qkv_ref.shape[1]
    part = depth // n_lat
    me = lax.axis_index("lon")

    def put(first, size, piece):
        rows = pl.ds(pl.multiple_of(first, size), size)
        qkv_ref[rows, :] = piece[:, 0:QKV]
        out_ref[rows, :] = piece[:, QKV:COLS]

    own = pl.ds(pl.multiple_of(z * depth, depth), depth)
    for k in range(3):
        mine = pl.ds(pl.multiple_of(D * k + MINE * me, MINE), MINE)
        qkv_ref[own, MINE * k : MINE * (k + 1)] = own_qkv_ref[b, :, mine]
    out_ref[own, :] = own_out_ref[b, :, pl.ds(pl.multiple_of(OUT * me, OUT), OUT)]
    for k in range(1, n_fsdp):
        base = partner(z, k, n_fsdp) * depth
        for i, step in enumerate(wide):
            put(base + (lat ^ step) * part, part, far[k - 1][part * i : part * (i + 1), :])
        for j, step in enumerate(steps):
            row = base + partner(lat, step, n_lat) * part
            put(row, part, near[j][part * (k - 1) : part * k, :])


def join_call(b, n_lat, steps, wide, qkv, out, far, near):
    rows = qkv.shape[1] * (len(far) + 1)
    return pl.pallas_call(
        functools.partial(join_kernel, b, len(far) + 1, n_lat, steps, wide),
        out_shape=(
            jax.ShapeDtypeStruct((rows, QKV), BF16),
            jax.ShapeDtypeStruct((rows, OUT), BF16),
        ),
        compiler_params=vmem(8),
        cost_estimate=pl.CostEstimate(flops=10**6, bytes_accessed=2 * 10**6, transcendentals=0),
    )(qkv, out, *far, *near)


def window_attend(q, k, v, bias_at, allowed, put):
    n = q.shape[0]
    lanes = lax.broadcasted_iota(jnp.int32, (n, 128), 1)
    owns = [(lanes >= HEAD_DIM * j) & (lanes < HEAD_DIM * (j + 1)) for j in range(GROUP)]
    ones = jnp.ones((WIN, 128), BF16)
    for g in range(MINE // 128):
        cols = slice(128 * g, 128 * (g + 1))
        q_g = q[:, cols]
        k_g = k[:, cols]
        v_g = jnp.concatenate([v[:, cols], ones], axis=1)
        q_all = jnp.concatenate([jnp.where(o, q_g, jnp.zeros_like(q_g)) for o in owns], axis=0)
        scores = nt_dot(q_all, k_g)
        probs = []
        for j in range(GROUP):
            s = scores[n * j : n * (j + 1)] + bias_at(GROUP * g + j)
            if allowed is not None:
                s = jnp.where(allowed, s, NEG)
            peak = jnp.max(s, axis=-1, keepdims=True)
            probs.append(jnp.exp2(s - peak).astype(BF16))
        mixed = nn_dot(jnp.concatenate(probs, axis=0), v_g)
        value, total = mixed[0:n, 0:128], mixed[0:n, 128:256]
        for j in range(1, GROUP):
            value = jnp.where(owns[j], mixed[n * j : n * (j + 1), 0:128], value)
            total = jnp.where(owns[j], mixed[n * j : n * (j + 1), 128:256], total)
        put(128 * g, (value / total).astype(BF16))


def project(n, w_ref, q_s, k_s, v_s):
    both = nn_dot(n, w_ref[...])
    q_s[...] = (both[:, 0:MINE] * SCALE2).astype(BF16)
    k_s[...] = both[:, MINE : 2 * MINE].astype(BF16)
    v_s[...] = both[:, 2 * MINE : 3 * MINE].astype(BF16)


def first_kernel(n_ref, w_ref, bias_ref, wo_ref, o_ref, q_s, k_s, v_s):
    o_ref[PAIR * KEPT :, :] = wo_ref[...]
    project(n_ref[...].reshape(PAIR * TALL, D), w_ref, q_s, k_s, v_s)
    for l in range(PAIR):
        for part, (q0, q1, o0) in enumerate(
            ((KEEP0, WIN, 0), (0, WIN, PART), (0, PART, PART + WIN))
        ):
            t = TALL * l + WIN * part

            def put(col, value, l=l, o0=o0, q0=q0, q1=q1):
                o_ref[KEPT * l + o0 : KEPT * l + o0 + q1 - q0, col : col + 128] = value

            window_attend(
                q_s[t + q0 : t + q1, :],
                k_s[t : t + WIN, :],
                v_s[t : t + WIN, :],
                lambda h, q0=q0, q1=q1: bias_ref[h, q0:q1, :],
                None,
                put,
            )


def first_call(normed, weight, bias, wo):
    scratch = pltpu.VMEM((PAIR * TALL, MINE), BF16)
    return pl.pallas_call(
        first_kernel,
        out_shape=jax.ShapeDtypeStruct((PAIR * KEPT + D, MINE), BF16),
        scratch_shapes=[scratch, scratch, scratch],
        compiler_params=vmem(24),
        cost_estimate=pl.CostEstimate(flops=2 * 10**9, bytes_accessed=4 * 10**6, transcendentals=10**6),
        name="first",
    )(normed, weight, bias, wo)


def pair_columns(me, ref, mine, other):
    width = mine.shape[-1]
    ref[:, pl.ds(pl.multiple_of(width * me, width), width)] = mine
    ref[:, pl.ds(pl.multiple_of(width * (1 - me), width), width)] = other


def middle_kernel(
    mine_ref, other_ref, x_ref, gain_ref, mid_ref, win_ref, o_s, wo_s, m_s, n_s
):
    me = lax.axis_index("lon")
    tokens = PAIR * KEPT
    pair_columns(me, o_s, mine_ref[0:tokens, :], other_ref[0:tokens, :])
    pair_columns(me, wo_s, mine_ref[tokens:, :], other_ref[tokens:, :])
    for l in range(PAIR):
        rows = slice(KEPT * l, KEPT * (l + 1))
        value = x_ref[l, KEEP0:KEEP1, :].astype(F32) + nn_dot(o_s[rows, :], wo_s[...])
        value = value.astype(BF16)
        m_s[l] = value
        n_s[rows, :] = norm_rows(value.astype(F32), gain_ref[1:2, :])
    mid_ref[...] = m_s[me, PART : PART + WIN, :]
    win_ref[...] = nn_dot(one_hot(window_sources(), tokens), n_s[...]).astype(BF16)


def middle_call(mine, other, x, gain):
    tokens = PAIR * KEPT
    return pl.pallas_call(
        middle_kernel,
        out_shape=(
            jax.ShapeDtypeStruct((WIN, D), BF16),
            jax.ShapeDtypeStruct((4 * WIN, D), BF16),
        ),
        scratch_shapes=[
            pltpu.VMEM((tokens, D), BF16),
            pltpu.VMEM((D, D), BF16),
            pltpu.VMEM((PAIR, KEPT, D), BF16),
            pltpu.VMEM((tokens, D), BF16),
        ],
        compiler_params=vmem(16),
        cost_estimate=pl.CostEstimate(flops=10**9, bytes_accessed=3 * 10**6, transcendentals=0),
        name="middle",
    )(mine, other, x, gain)


def second_kernel(
    win_ref, w_ref, bias_a, bias_b, row_ref, col_ref, keep_ref, send_ref, q_s, k_s, v_s, a_s, t_s
):
    me = lax.axis_index("lon")
    half = MY_HEADS // 2
    project(win_ref[...], w_ref, q_s, k_s, v_s)
    for w in range(4):
        q0, q1 = (KEEP0, WIN) if w < 2 else (0, PART)
        t = WIN * w
        allowed = col_ref[q0:q1, w : w + 1] == row_ref[w : w + 1, :]

        def put(col, value, w=w):
            a_s[PART * w : PART * (w + 1), col : col + 128] = value

        window_attend(
            q_s[t + q0 : t + q1, :],
            k_s[t : t + WIN, :],
            v_s[t : t + WIN, :],
            lambda h, q0=q0, q1=q1: (bias_a, bias_b)[h // half][h % half, q0:q1, :],
            allowed,
            put,
        )
    tiles = nn_dot(one_hot(tile_sources(), 4 * PART), a_s[...]).astype(BF16)
    t_s[0] = tiles[0:WIN]
    t_s[1] = tiles[WIN : 2 * WIN]
    keep_ref[...] = t_s[me]
    send_ref[...] = t_s[1 - me]


def second_call(windows, weight, bias_a, bias_b, row, col):
    qkv = pltpu.VMEM((4 * WIN, MINE), BF16)
    half = jax.ShapeDtypeStruct((WIN, MINE), BF16)
    return pl.pallas_call(
        second_kernel,
        out_shape=(half, half),
        scratch_shapes=[
            qkv,
            qkv,
            qkv,
            pltpu.VMEM((4 * PART, MINE), BF16),
            pltpu.VMEM((PAIR, WIN, MINE), BF16),
        ],
        compiler_params=vmem(24),
        cost_estimate=pl.CostEstimate(flops=2 * 10**9, bytes_accessed=4 * 10**6, transcendentals=10**6),
        name="second",
    )(windows, weight, bias_a, bias_b, row, col)


def most_kernel(mid_ref, keep_ref, wo_mine_ref, wo_other_ref, sum_ref, rows_ref, wo_s):
    me = lax.axis_index("lon")
    pair_columns(me, wo_s, wo_mine_ref[...], wo_other_ref[...])
    mine = pl.ds(pl.multiple_of(MINE * me, MINE), MINE)
    rows_ref[...] = wo_s[pl.ds(pl.multiple_of(MINE * (1 - me), MINE), MINE), :]
    sum_ref[...] = mid_ref[...].astype(F32) + nn_dot(keep_ref[...], wo_s[mine, :])


def most_call(mid, keep, wo_mine, wo_other):
    return pl.pallas_call(
        most_kernel,
        out_shape=(jax.ShapeDtypeStruct((WIN, D), F32), jax.ShapeDtypeStruct((MINE, D), BF16)),
        scratch_shapes=[pltpu.VMEM((D, D), BF16)],
        compiler_params=vmem(8),
        cost_estimate=pl.CostEstimate(flops=10**8, bytes_accessed=10**6, transcendentals=0),
        name="most",
    )(mid, keep, wo_mine, wo_other)


def last_kernel(sum_ref, rows_ref, got_ref, out_ref):
    value = sum_ref[...] + nn_dot(got_ref[...], rows_ref[...])
    out_ref[...] = value.reshape(WIN // WZ, WZ, D).astype(BF16)


def last_call(total, rows, got):
    return pl.pallas_call(
        last_kernel,
        out_shape=jax.ShapeDtypeStruct((WIN // WZ, WZ, D), BF16),
        compiler_params=vmem(8),
        cost_estimate=pl.CostEstimate(flops=10**8, bytes_accessed=10**6, transcendentals=0),
        name="last",
    )(total, rows, got)


def sharing(n_lat):
    every = tuple(range(1, n_lat))
    if n_lat == 4:
        return (((0,), every), ((0, 3), (1, 2)))
    return (((0,), every), ((0,), every))


def paired(latent, norm_gain, qkv_weight, out_weight, rel_bias, bias_index, region_ids):
    n_fsdp, n_lat = lax.axis_size("fsdp"), lax.axis_size("lat")
    part = qkv_weight.shape[1] // n_lat
    plan = sharing(n_lat)

    def swap(block):
        return passed_along(block, "lon", 1)

    def spread(block, axis, steps):
        got = []
        for k in steps:
            got.append(heard_from(block, axis, k))
        return got

    part0, part1, tile = open_call(
        jnp.transpose(latent[0], (1, 2, 0, 3)).reshape(WIN // WZ, WZ, D),
        jnp.transpose(region_ids, (1, 0, 2)),
        qkv_weight,
        out_weight,
        part,
        plan[1][0],
    )
    far0 = spread(part0, "fsdp", range(1, n_fsdp))
    mirrored = n_lat == 4
    side = heard_from(tile, "lat", 1) if mirrored else passed_along(tile, "lat", 1)
    cross = heard_from(tile, "lat", 3) if mirrored else passed_along(tile, "lat", -1)
    far1 = spread(part1, "fsdp", range(1, n_fsdp))
    near0 = spread(jnp.concatenate(far0, axis=0), "lat", plan[0][1])
    near1 = spread(jnp.concatenate([f[:part] for f in far1], axis=0), "lat", plan[1][1])
    three = (side, tile, cross)
    pair = [swap(t) for t in three]
    x, normed, tag_row, tag_col = enter_call(mirrored, three, pair, norm_gain)
    table = jnp.transpose(rel_bias, (0, 2, 1))
    params = (qkv_weight, out_weight)
    w0, wo0 = join_call(0, n_lat, plan[0][1], plan[0][0], *params, far0, near0)
    bias0, index = bias_call(bias0_kernel, MY_HEADS, True, table, bias_index)
    o0 = first_call(normed, w0, bias0, wo0)
    w1, wo1 = join_call(1, n_lat, plan[1][1], plan[1][0], *params, far1, near1)
    half = MY_HEADS // 2
    bias1 = [
        bias_call(functools.partial(bias1_kernel, half * i), half, False, table, index)
        for i in range(2)
    ]
    mid, windows = middle_call(o0, swap(o0), x, norm_gain)
    keep, send = second_call(windows, w1, *bias1, tag_row, tag_col)
    total, rows = most_call(mid, keep, wo1, swap(wo1))
    out = last_call(total, rows, swap(send))
    return jnp.transpose(out.reshape(WH, WW, WZ, D), (2, 0, 1, 3))[None]


def solution(mesh):
    pair = mesh.shape["lon"] == PAIR

    def local(latent, norm_gain, qkv_weight, out_weight, *rest):
        one_window = latent.shape[:4] == (1, WZ, WH, WW)
        even = qkv_weight.shape[1] % (16 * mesh.shape["lat"]) == 0
        program = paired if pair and one_window and even else any_mesh
        return program(latent, norm_gain, qkv_weight, out_weight, *rest)

    return jax.shard_map(
        local,
        mesh=mesh,
        in_specs=(
            P("fsdp", None, "lat", "lon", None),
            P(),
            P(None, "fsdp", None),
            P(None, "fsdp", None),
            P(),
            P(),
            P(None, "lat", "lon"),
        ),
        out_specs=P("fsdp", None, "lat", "lon", None),
        check_vma=False,
    )
```

```python
import functools

import jax
import jax.numpy as jnp
from jax import lax
from jax.experimental import pallas as pl
from jax.experimental.pallas import tpu as pltpu
from jax.sharding import PartitionSpec as P


D = 512
HEADS = 16
HEAD_DIM = 32
WZ = 2
WH = 6
WW = 12
WIN = 144
BIAS_ROWS = 759
HALF = WIN // 2
LOG2E = 1.4426950408889634
SCALE2 = HEAD_DIM ** (-0.5) * LOG2E
NEG = -1e30


def passed_along(block, axis, distance):
    devices = range(lax.axis_size(axis))
    route = [((i - distance) % len(devices), i) for i in devices]
    return lax.ppermute(block, axis, route)


def layer_norm(hidden, gain_row):
    values = hidden.astype(jnp.float32)
    centre = jnp.mean(values, axis=-1, keepdims=True)
    shifted = values - centre
    variance = jnp.mean(shifted * shifted, axis=-1, keepdims=True)
    return (shifted * lax.rsqrt(variance + 1e-05) * gain_row).astype(jnp.bfloat16)


def bias_table(rel_bias, bias_index, block_index):
    return jnp.take(jnp.transpose(rel_bias[block_index]), bias_index, axis=1)


def split_tile(field_tile):
    sample_count, level_count, row_count, col_count, feature_width = field_tile.shape
    pieces = field_tile.reshape(
        sample_count, level_count // WZ, WZ, row_count // WH, WH, col_count // WW, WW, feature_width
    )
    pieces = jnp.transpose(pieces, (0, 1, 3, 5, 2, 4, 6, 7))
    return pieces.reshape(-1, WIN, feature_width)


def merge_tile(windows, tile_shape):
    sample_count, level_count, row_count, col_count, feature_width = tile_shape
    pieces = windows.reshape(
        sample_count, level_count // WZ, row_count // WH, col_count // WW, WZ, WH, WW, feature_width
    )
    pieces = jnp.transpose(pieces, (0, 1, 4, 2, 5, 3, 6, 7))
    return pieces.reshape(tile_shape)


def attend(normed, weight, bias_heads, region_tags):
    packed = jnp.dot(normed.reshape(-1, D), weight, preferred_element_type=jnp.float32).astype(
        jnp.bfloat16
    )
    packed = split_tile(packed.reshape(normed.shape[:-1] + (3 * D,)))
    packed = packed.reshape(-1, WIN, 3, HEADS, HEAD_DIM)
    scores = jnp.einsum(
        "gqhd,gkhd->ghqk", packed[:, :, 0], packed[:, :, 1], preferred_element_type=jnp.float32
    )
    scores = scores * HEAD_DIM ** (-0.5) + bias_heads[None]
    if region_tags is not None:
        window_tags = split_tile(region_tags[..., None])[..., 0]
        allowed = window_tags[:, :, None] == window_tags[:, None, :]
        blocked = jnp.where(allowed, jnp.float32(0.0), -jnp.inf)
        scores = scores + blocked[:, None]
    row_peak = jnp.max(scores, axis=-1, keepdims=True)
    exponent = jnp.exp(scores - row_peak)
    row_total = jnp.sum(exponent, axis=-1, keepdims=True)
    attn_probs = (exponent / row_total).astype(jnp.bfloat16)
    mixed_out = jnp.einsum(
        "ghqk,gkhd->gqhd", attn_probs, packed[:, :, 2], preferred_element_type=jnp.float32
    )
    return merge_tile(mixed_out.astype(jnp.bfloat16).reshape(-1, WIN, D), normed.shape)


def any_mesh(latent, norm_gain, qkv_weight, out_weight, rel_bias, bias_index, region_ids):
    half_rows = WH // 2
    half_cols = WW // 2
    row_count = latent.shape[2]
    col_count = latent.shape[3]
    gathered_qkv, gathered_out = (
        lax.all_gather(qkv_weight, "fsdp", axis=1, tiled=True),
        lax.all_gather(out_weight, "fsdp", axis=1, tiled=True),
    )

    def fetch_weights(block_index):
        return (gathered_qkv[block_index], gathered_out[block_index])

    first_qkv, first_out = fetch_weights(0)
    normed = layer_norm(latent, norm_gain[0])
    mixed_out = attend(normed, first_qkv, bias_table(rel_bias, bias_index, 0), None)
    projected = jnp.dot(mixed_out.reshape(-1, D), first_out, preferred_element_type=jnp.float32)
    middle = (latent.astype(jnp.float32) + projected.reshape(latent.shape)).astype(jnp.bfloat16)
    second_qkv, second_out = fetch_weights(1)
    normed = jnp.roll(layer_norm(middle, norm_gain[1]), -1, axis=1)
    east_strip = passed_along(normed[:, :, :, :half_cols], "lon", -1)
    widened = jnp.concatenate([normed[:, :, :, half_cols:], east_strip], axis=3)
    north_strip = passed_along(widened[:, :, :half_rows], "lat", -1)
    rolled = jnp.concatenate([widened[:, :, half_rows:], north_strip], axis=2)
    level_pos = lax.broadcasted_iota(jnp.int32, region_ids.shape, 0)
    row_pos = (
        lax.broadcasted_iota(jnp.int32, region_ids.shape, 1) + lax.axis_index("lat") * row_count
    )
    region_tags = region_ids * 4 + (level_pos == region_ids.shape[0] - 1).astype(jnp.int32) * 2
    region_tags = region_tags + (row_pos >= row_count * lax.axis_size("lat") - half_rows).astype(
        jnp.int32
    )
    region_tags = region_tags[None]
    mixed_out = attend(rolled, second_qkv, bias_table(rel_bias, bias_index, 1), region_tags)
    south_strip = passed_along(mixed_out[:, :, row_count - half_rows :], "lat", 1)
    widened = jnp.concatenate([south_strip, mixed_out[:, :, : row_count - half_rows]], axis=2)
    west_strip = passed_along(widened[:, :, :, col_count - half_cols :], "lon", 1)
    mixed_out = jnp.concatenate([west_strip, widened[:, :, :, : col_count - half_cols]], axis=3)
    mixed_out = jnp.roll(mixed_out, 1, axis=1)
    projected = jnp.dot(mixed_out.reshape(-1, D), second_out, preferred_element_type=jnp.float32)
    return (middle.astype(jnp.float32) + projected.reshape(latent.shape)).astype(jnp.bfloat16)


PAIR = 2
MY_HEADS = HEADS // PAIR
MINE = MY_HEADS * HEAD_DIM
QKV = 3 * MINE
OUT = D // PAIR
COLS = QKV + OUT
TALL = 3 * WIN
KEEP0 = 64
KEEP1 = TALL - 64
KEPT = KEEP1 - KEEP0
PART = WIN - KEEP0
MAIN = 128
TAIL = WIN - MAIN
LAG = 1
REGION_ROWS = 8
GROUP = 128 // HEAD_DIM
F32 = jnp.float32
BF16 = jnp.bfloat16


def vmem(mib):
    return pltpu.CompilerParams(vmem_limit_bytes=mib * 2**20)


def partner(index, step, size):
    if size & (size - 1) == 0:
        return index ^ step
    return (index + size - step) % size


def heard_from(block, axis, step):
    size = lax.axis_size(axis)
    return lax.ppermute(block, axis, [(partner(i, step, size), i) for i in range(size)])


def as_column(lanes, size):
    return jnp.transpose(lanes.astype(F32))[0:size, 0:1].astype(jnp.int32)


def window_sources():
    token = lax.broadcasted_iota(jnp.int32, (8, 5 * 128), 1)
    a, v = token // (2 * WIN), token // WIN % 2
    dh, dw, dz = token % WIN // (WW * WZ), token % (WW * WZ) // WZ, token % WZ
    row = dh + WH * a - WH // 2
    col = (WW // 2 + WW * v + dw) % (2 * WW)
    level = (dz + 1) % WZ
    return as_column(col // WW * KEPT + (row + WH) * WW * WZ + col % WW * WZ + level - KEEP0, 4 * WIN)


def tile_sources():
    token = lax.broadcasted_iota(jnp.int32, (8, 3 * 128), 1)
    tile = token // WIN
    row, cw, level = token % WIN // (WW * WZ), token % (WW * WZ) // WZ, token % WZ
    a = row // (WH // 2)
    dh = (row + WH // 2) % WH
    col = (WW * tile + cw + 2 * WW - WW // 2) % (2 * WW)
    dz = (level + WZ - 1) % WZ
    found = (a * 2 + col // WW) * PART + dh * WW * WZ + col % WW * WZ + dz - KEEP0 * (1 - a)
    return as_column(found, 2 * WIN)


def one_hot(sources, width):
    lanes = lax.broadcasted_iota(jnp.int32, (sources.shape[0], width), 1)
    return jnp.where(lanes == sources, 1.0, 0.0).astype(BF16)


def nt_dot(a, b):
    return lax.dot_general(a, b, (((1,), (1,)), ((), ())), preferred_element_type=F32)


def nn_dot(a, b):
    return jnp.dot(a, b, preferred_element_type=F32)


def norm_rows(values, gain_row):
    centre = jnp.mean(values, axis=-1, keepdims=True)
    shifted = values - centre
    variance = jnp.mean(shifted * shifted, axis=-1, keepdims=True)
    return (shifted * lax.rsqrt(variance + 1e-05) * gain_row).astype(BF16)


def look_up(table, at, heads, put):
    chunks = (BIAS_ROWS + 127) // 128
    low = at & 127
    chunk = at >> 7
    masks = [chunk == k for k in range(chunks)]
    for h in heads:
        acc = None
        for k in range(chunks):
            row = jnp.broadcast_to(table[h : h + 1, 128 * k : 128 * k + 128], (8, 128))
            got = jnp.take_along_axis(row, low, axis=1, mode="promise_in_bounds")
            acc = got if acc is None else jnp.where(masks[k], got, acc)
        put(h, acc)


def load_table(b, table_ref, table):
    me = lax.axis_index("lon")
    heads = table_ref[b, pl.ds(pl.multiple_of(MY_HEADS * me, MY_HEADS), MY_HEADS), :]
    table[:, 0:BIAS_ROWS] = heads * LOG2E


def gather_main(start, index_ref, table, bias_ref):
    def step(g, carry):
        rows = pl.ds(pl.multiple_of(g * 8, 8), 8)

        def put(h, value):
            bias_ref[h - start, rows, :] = value

        look_up(table, index_ref[rows, 0:MAIN], range(start, start + bias_ref.shape[0]), put)
        return carry

    lax.fori_loop(0, WIN // 8, step, 0, unroll=9)


def gather_tail(flip_ref, table, tail_ref, flipped):
    for t in range(0, TAIL, 8):
        for lo in (0, 128):

            def put(h, value, t=t, lo=lo):
                flipped[TAIL * h + t : TAIL * h + t + 8, lo : lo + 128] = value

            look_up(table, flip_ref[t : t + 8, lo : lo + 128], range(MY_HEADS), put)
    tail_ref[...] = jnp.transpose(flipped[...])[0:WIN]


def bias0_kernel(table_ref, index_ref, bias_ref, tail_ref, moved_ref, flip_ref, table, flipped):
    to = lax.broadcasted_iota(jnp.int32, (WIN, WIN), 0)
    frm = lax.broadcasted_iota(jnp.int32, (WIN, WIN), 1)
    move = jnp.where((to & 1) * HALF + (to >> 1) == frm, 1.0, 0.0).astype(BF16)
    whole = index_ref[...]
    parts = jnp.concatenate([whole >> 8, whole & 255], axis=0).astype(F32).astype(BF16)
    parts = nt_dot(parts, move).astype(BF16)
    high, low = parts[0:WIN], parts[WIN : 2 * WIN]
    moved = nn_dot(move, high) * 256.0 + nn_dot(move, low)
    moved_ref[...] = moved.astype(jnp.int32)
    flip_ref[:, WIN:256] = jnp.zeros((TAIL, 256 - WIN), jnp.int32)
    flip_ref[:, 0:WIN] = jnp.transpose(moved[:, MAIN:WIN]).astype(jnp.int32)
    load_table(0, table_ref, table)
    gather_main(0, moved_ref, table, bias_ref)
    gather_tail(flip_ref, table, tail_ref, flipped)


def bias1_kernel(start, table_ref, index_ref, bias_ref, table, flipped):
    load_table(1, table_ref, table)
    gather_main(start, index_ref, table, bias_ref)


def bias1_tail_kernel(start, table_ref, index_ref, flip_ref, bias_ref, tail_ref, table, flipped):
    load_table(1, table_ref, table)
    gather_main(start, index_ref, table, bias_ref)
    gather_tail(flip_ref, table, tail_ref, flipped)


def bias_call(kernel, heads, tail, first, *operands):
    out = [jax.ShapeDtypeStruct((heads, WIN, MAIN), F32)]
    out += [jax.ShapeDtypeStruct((WIN, MY_HEADS * TAIL), F32)] * tail
    if first:
        out += [jax.ShapeDtypeStruct((WIN, WIN), jnp.int32), jax.ShapeDtypeStruct((TAIL, 256), jnp.int32)]
    return pl.pallas_call(
        kernel,
        out_shape=out,
        scratch_shapes=[
            pltpu.VMEM((MY_HEADS, (BIAS_ROWS + 127) // 128 * 128), F32),
            pltpu.VMEM((MY_HEADS * TAIL, 256), F32),
        ],
        compiler_params=vmem(8),
        cost_estimate=pl.CostEstimate(flops=10**9, bytes_accessed=10**6, transcendentals=0),
    )(*operands)


def columns(qkv_ref, out_ref, b, rows, me, dst, at, sems):
    mine = pl.ds(pl.multiple_of(MINE * me, MINE), MINE)
    sources = [
        qkv_ref.at[b, rows, pl.ds(pl.multiple_of(D * k + MINE * me, MINE), MINE)] for k in range(3)
    ]
    sources += [out_ref.at[b, rows, mine]]
    to = pl.ds(at, rows.size)
    return [
        pltpu.make_async_copy(source, dst.at[to, pl.ds(MINE * k, MINE)], sems.at[k])
        for k, source in enumerate(sources)
    ]


def open_kernel(
    wide, latent_ref, region_ref, qkv_ref, out_ref, part0_ref, part1_ref, tile_ref,
    latent, regions, sems, own_sems,
):
    part = part0_ref.shape[0]
    me, lat = lax.axis_index("lon"), lax.axis_index("lat")

    def cut(b, dst, step, at, n):
        rows = pl.ds(pl.multiple_of((lat ^ step) * part, part), part)
        return columns(qkv_ref, out_ref, b, rows, me, dst, at, sems.at[n])

    copies = cut(0, part0_ref, 0, 0, 0)
    for i, step in enumerate(wide):
        copies += cut(1, part1_ref, step, part * i, 1 + i)
    inputs = [
        pltpu.make_async_copy(latent_ref, latent, own_sems.at[0]),
        pltpu.make_async_copy(region_ref, regions, own_sems.at[1]),
    ]
    for copy in copies + inputs:
        copy.start()
    for copy in inputs:
        copy.wait()
    tile_ref[0:WIN, :] = latent[...].reshape(WIN, D)
    col = lax.broadcasted_iota(jnp.int32, (WW, WIN), 0)
    token = lax.broadcasted_iota(jnp.int32, (WW, WIN), 1)
    spread = jnp.where(token % (WW * WZ) // WZ == col, 1.0, 0.0).astype(BF16)
    level = lax.broadcasted_iota(jnp.int32, (WZ, WIN), 0)
    token = lax.broadcasted_iota(jnp.int32, (WZ, WIN), 1)
    total = jnp.zeros((WZ, WIN), F32)
    for dh in range(WH):
        here = (token // (WW * WZ) == dh) & (token % WZ == level)
        total += jnp.where(here, nn_dot(regions[dh].astype(F32).astype(BF16), spread), 0.0)
    row = jnp.sum(total, axis=0, keepdims=True)
    tile_ref[WIN : WIN + REGION_ROWS, 0:WIN] = jnp.broadcast_to(row, (REGION_ROWS, WIN)).astype(BF16)
    tile_ref[WIN : WIN + REGION_ROWS, WIN:D] = jnp.zeros((REGION_ROWS, D - WIN), BF16)
    for copy in copies:
        copy.wait()


STAY = pl.BlockSpec(memory_space=pltpu.HBM)


def open_call(latent, regions, qkv, out, part, wide):
    return pl.pallas_call(
        functools.partial(open_kernel, wide),
        out_shape=(
            jax.ShapeDtypeStruct((part, COLS), BF16),
            jax.ShapeDtypeStruct((part * len(wide), COLS), BF16),
            jax.ShapeDtypeStruct((WIN + REGION_ROWS, D), BF16),
        ),
        in_specs=[STAY] * 4,
        scratch_shapes=[
            pltpu.VMEM(latent.shape, BF16),
            pltpu.VMEM(regions.shape, jnp.int32),
            pltpu.SemaphoreType.DMA((1 + len(wide), 4)),
            pltpu.SemaphoreType.DMA((2,)),
        ],
        compiler_params=pltpu.CompilerParams(vmem_limit_bytes=67043328-400*1024),
        cost_estimate=pl.CostEstimate(flops=10**6, bytes_accessed=10**6, transcendentals=0),
        name="open",
    )(latent, regions, qkv, out)


def enter_kernel(mirrored, *refs):
    mine, other = refs[0:3], refs[3:6]
    gain_ref, x_ref, n_ref, row_ref, col_ref = refs[6:]
    me = lax.axis_index("lon")
    n_lat = lax.axis_size("lat")
    lat = lax.axis_index("lat")
    odd = lat & 1 if mirrored else 1
    places = (2 - 2 * odd, 1, 2 * odd)
    for k, place in enumerate(places):
        rows = pl.ds(pl.multiple_of(WIN * place, WIN), WIN)
        for ref, l in ((mine[k], me), (other[k], 1 - me)):
            tokens = ref[0:WIN, :]
            x_ref[l, rows, :] = tokens
            n_ref[l, rows, :] = norm_rows(tokens.astype(F32), gain_ref[0:1, :])
    lanes = lax.broadcasted_iota(jnp.int32, (1, WIN), 1)
    level = lanes & 1
    dh = lanes // (WW * WZ)

    def regions(three):
        found = [ref[WIN : WIN + REGION_ROWS, 0:WIN].astype(F32)[0:1] for ref in three]
        return jnp.where(odd == 1, found[0], found[2]), found[1]

    rows = []
    for a, (own, pair) in enumerate(zip(regions(mine), regions(other))):
        window = (lat + n_lat - 1 + a) % n_lat
        late = window * WH + dh >= n_lat * WH - WH // 2
        extra = jnp.where(level == WZ - 1, 2.0, 0.0) + jnp.where(late, 1.0, 0.0)
        west = jnp.where(me == 0, own, pair)
        east = jnp.where(me == 0, pair, own)
        rows += [4.0 * west + extra, 4.0 * east + extra]
    tags = jnp.concatenate(rows + rows, axis=0)
    row_ref[:, 0:MAIN] = tags[:, 0:MAIN]
    row_ref[:, MAIN:] = jnp.concatenate([tags[:, MAIN:WIN]] * MY_HEADS, axis=1)
    to = lax.broadcasted_iota(jnp.int32, (WIN, WIN), 0)
    frm = lax.broadcasted_iota(jnp.int32, (WIN, WIN), 1)
    col_ref[...] = nt_dot(jnp.where(to == frm, 1.0, 0.0).astype(BF16), tags.astype(BF16))


def enter_call(mirrored, mine, other, gain):
    return pl.pallas_call(
        functools.partial(enter_kernel, mirrored),
        out_shape=(
            jax.ShapeDtypeStruct((PAIR, TALL, D), BF16),
            jax.ShapeDtypeStruct((PAIR, TALL, D), BF16),
            jax.ShapeDtypeStruct((8, MAIN + MY_HEADS * TAIL), F32),
            jax.ShapeDtypeStruct((WIN, 8), F32),
        ),
        compiler_params=vmem(16),
        cost_estimate=pl.CostEstimate(flops=10**8, bytes_accessed=2 * 10**6, transcendentals=0),
        name="enter",
    )(*mine, *other, gain)


def give_kernel(part, *refs):
    for k, ref in enumerate(refs[:-1]):
        refs[-1][part * k : part * (k + 1), :] = ref[0:part, :]


def give_call(part, pieces):
    return pl.pallas_call(
        functools.partial(give_kernel, part),
        out_shape=jax.ShapeDtypeStruct((part * len(pieces), COLS), BF16),
        compiler_params=vmem(4),
        cost_estimate=pl.CostEstimate(flops=0, bytes_accessed=10**6, transcendentals=0),
    )(*pieces)


def join_kernel(b, n_fsdp, n_lat, steps, wide, own_qkv_ref, own_out_ref, *refs):
    far, near = refs[: n_fsdp - 1], refs[n_fsdp - 1 : n_fsdp - 1 + len(steps)]
    qkv_ref, out_ref = refs[-2:]
    z, lat = lax.axis_index("fsdp"), lax.axis_index("lat")
    depth = own_qkv_ref.shape[1]
    part = depth // n_lat
    me = lax.axis_index("lon")

    def put(first, size, piece):
        rows = pl.ds(pl.multiple_of(first, size), size)
        qkv_ref[rows, :] = piece[:, 0:QKV]
        out_ref[rows, :] = piece[:, QKV:COLS]

    own = pl.ds(pl.multiple_of(z * depth, depth), depth)
    for k in range(3):
        mine = pl.ds(pl.multiple_of(D * k + MINE * me, MINE), MINE)
        qkv_ref[own, MINE * k : MINE * (k + 1)] = own_qkv_ref[b, :, mine]
    out_ref[own, :] = own_out_ref[b, :, pl.ds(pl.multiple_of(OUT * me, OUT), OUT)]
    for k in range(1, n_fsdp):
        base = partner(z, k, n_fsdp) * depth
        for i, step in enumerate(wide):
            put(base + (lat ^ step) * part, part, far[k - 1][part * i : part * (i + 1), :])
        for j, step in enumerate(steps):
            row = base + partner(lat, step, n_lat) * part
            put(row, part, near[j][part * (k - 1) : part * k, :])


def join_call(b, n_lat, steps, wide, qkv, out, far, near):
    rows = qkv.shape[1] * (len(far) + 1)
    return pl.pallas_call(
        functools.partial(join_kernel, b, len(far) + 1, n_lat, steps, wide),
        out_shape=(
            jax.ShapeDtypeStruct((rows, QKV), BF16),
            jax.ShapeDtypeStruct((rows, OUT), BF16),
        ),
        compiler_params=vmem(8),
        cost_estimate=pl.CostEstimate(flops=10**6, bytes_accessed=2 * 10**6, transcendentals=0),
    )(qkv, out, *far, *near)


def window_attend(q, k, v, bias_at, tail_bias, allowed, tail_allowed, put):
    n = q.shape[0]
    width = MY_HEADS * TAIL
    lanes = lax.broadcasted_iota(jnp.int32, (n, 128), 1)
    owns = [lanes // HEAD_DIM == j for j in range(GROUP)]
    blocks = [lanes // TAIL == h for h in range(MY_HEADS)]
    row = lax.broadcasted_iota(jnp.int32, (width, MINE), 0)
    col = lax.broadcasted_iota(jnp.int32, (width, MINE), 1)
    same = row // TAIL == col // HEAD_DIM
    groups = range(MINE // 128)

    def spread(x):
        x = jnp.concatenate([x[MAIN:WIN]] * MY_HEADS, axis=0)
        return jnp.where(same, x, jnp.zeros_like(x))

    tail = nt_dot(q, spread(k)) + tail_bias
    scores = []
    for g in groups:
        cols = slice(128 * g, 128 * (g + 1))
        q_g = q[:, cols]
        q_all = jnp.concatenate([jnp.where(o, q_g, jnp.zeros_like(q_g)) for o in owns], axis=0)
        scores.append(nt_dot(q_all, k[0:MAIN, cols]))
    yield
    if tail_allowed is not None:
        tail = jnp.where(tail_allowed, tail, NEG)
    tail_peak = jnp.zeros_like(tail)
    probs = []
    for h in range(MY_HEADS):
        j = h % GROUP
        s = scores[h // GROUP][n * j : n * (j + 1)] + bias_at(h)
        if allowed is not None:
            s = jnp.where(allowed, s, NEG)
        peak = jnp.max(jnp.maximum(s, jnp.where(blocks[h], tail, NEG)), axis=-1, keepdims=True)
        tail_peak = jnp.where(blocks[h], peak, tail_peak)
        probs.append(jnp.exp2(s - peak).astype(BF16))
    tail = jnp.exp2(tail - tail_peak).astype(BF16)
    yield
    rest = nn_dot(tail, spread(v))
    ones = jnp.where(same, 1.0, 0.0).astype(BF16)
    rest_total = nn_dot(tail, ones)
    for g in groups:
        cols = slice(128 * g, 128 * (g + 1))
        wide = jnp.concatenate([v[0:MAIN, cols], jnp.ones((MAIN, 128), BF16)], axis=1)
        mixed = nn_dot(jnp.concatenate(probs[GROUP * g : GROUP * (g + 1)], axis=0), wide)
        value, total = mixed[0:n, 0:128], mixed[0:n, 128:256]
        for j in range(1, GROUP):
            value = jnp.where(owns[j], mixed[n * j : n * (j + 1), 0:128], value)
            total = jnp.where(owns[j], mixed[n * j : n * (j + 1), 128:256], total)
        put(128 * g, ((value + rest[:, cols]) / (total + rest_total[:, cols])).astype(BF16))
    yield


def staggered(windows, lag):
    for at in range(len(windows) + 2 * lag):
        for stage in range(3):
            if 0 <= at - stage * lag < len(windows):
                next(windows[at - stage * lag])


def project(n, w_ref, q_s, k_s, v_s):
    both = nn_dot(n, w_ref[...])
    q_s[...] = (both[:, 0:MINE] * SCALE2).astype(BF16)
    k_s[...] = both[:, MINE : 2 * MINE].astype(BF16)
    v_s[...] = both[:, 2 * MINE : 3 * MINE].astype(BF16)


def first_kernel(n_ref, w_ref, bias_ref, tail_ref, wo_ref, o_ref, q_s, k_s, v_s):
    o_ref[PAIR * KEPT :, :] = wo_ref[...]
    project(n_ref[...].reshape(PAIR * TALL, D), w_ref, q_s, k_s, v_s)
    windows = []
    for l in range(PAIR):
        for part, (q0, q1, o0) in enumerate(
            ((KEEP0, WIN, 0), (0, WIN, PART), (0, PART, PART + WIN))
        ):
            t = TALL * l + WIN * part

            def put(col, value, l=l, o0=o0, q0=q0, q1=q1):
                o_ref[KEPT * l + o0 : KEPT * l + o0 + q1 - q0, col : col + 128] = value

            windows.append(window_attend(
                q_s[t + q0 : t + q1, :],
                k_s[t : t + WIN, :],
                v_s[t : t + WIN, :],
                lambda h, q0=q0, q1=q1: bias_ref[h, q0:q1, :],
                tail_ref[q0:q1, :],
                None,
                None,
                put,
            ))
    staggered(windows, LAG)


def first_call(normed, weight, bias, tail, wo):
    scratch = pltpu.VMEM((PAIR * TALL, MINE), BF16)
    return pl.pallas_call(
        first_kernel,
        out_shape=jax.ShapeDtypeStruct((PAIR * KEPT + D, MINE), BF16),
        scratch_shapes=[scratch, scratch, scratch],
        compiler_params=vmem(24),
        cost_estimate=pl.CostEstimate(flops=2 * 10**9, bytes_accessed=4 * 10**6, transcendentals=10**6),
        name="first",
    )(normed, weight, bias, tail, wo)


def pair_columns(me, ref, mine, other):
    width = mine.shape[-1]
    ref[:, pl.ds(pl.multiple_of(width * me, width), width)] = mine
    ref[:, pl.ds(pl.multiple_of(width * (1 - me), width), width)] = other


def middle_kernel(
    mine_ref, other_ref, x_ref, gain_ref, mid_ref, win_ref, o_s, wo_s, m_s, n_s
):
    me = lax.axis_index("lon")
    tokens = PAIR * KEPT
    pair_columns(me, o_s, mine_ref[0:tokens, :], other_ref[0:tokens, :])
    pair_columns(me, wo_s, mine_ref[tokens:, :], other_ref[tokens:, :])
    for l in range(PAIR):
        rows = slice(KEPT * l, KEPT * (l + 1))
        value = x_ref[l, KEEP0:KEEP1, :].astype(F32) + nn_dot(o_s[rows, :], wo_s[...])
        value = value.astype(BF16)
        m_s[l] = value
        n_s[rows, :] = norm_rows(value.astype(F32), gain_ref[1:2, :])
    mid_ref[...] = m_s[me, PART : PART + WIN, :]
    win_ref[...] = nn_dot(one_hot(window_sources(), tokens), n_s[...]).astype(BF16)


def middle_call(mine, other, x, gain):
    tokens = PAIR * KEPT
    return pl.pallas_call(
        middle_kernel,
        out_shape=(
            jax.ShapeDtypeStruct((WIN, D), BF16),
            jax.ShapeDtypeStruct((4 * WIN, D), BF16),
        ),
        scratch_shapes=[
            pltpu.VMEM((tokens, D), BF16),
            pltpu.VMEM((D, D), BF16),
            pltpu.VMEM((PAIR, KEPT, D), BF16),
            pltpu.VMEM((tokens, D), BF16),
        ],
        compiler_params=vmem(16),
        cost_estimate=pl.CostEstimate(flops=10**9, bytes_accessed=3 * 10**6, transcendentals=0),
        name="middle",
    )(mine, other, x, gain)


def second_kernel(
    win_ref, w_ref, bias_a, bias_b, tail_ref, row_ref, col_ref, keep_ref, send_ref, q_s, k_s, v_s, a_s, t_s
):
    me = lax.axis_index("lon")
    half = MY_HEADS // 2
    project(win_ref[...], w_ref, q_s, k_s, v_s)
    windows = []
    for w in range(4):
        q0, q1 = (KEEP0, WIN) if w < 2 else (0, PART)
        t = WIN * w
        allowed = col_ref[q0:q1, w : w + 1] == row_ref[w : w + 1, :]

        def put(col, value, w=w):
            a_s[PART * w : PART * (w + 1), col : col + 128] = value

        windows.append(window_attend(
            q_s[t + q0 : t + q1, :],
            k_s[t : t + WIN, :],
            v_s[t : t + WIN, :],
            lambda h, q0=q0, q1=q1: (bias_a, bias_b)[h // half][h % half, q0:q1, :],
            tail_ref[q0:q1, :],
            allowed[:, 0:MAIN],
            allowed[:, MAIN:],
            put,
        ))
    staggered(windows, LAG)
    tiles = nn_dot(one_hot(tile_sources(), 4 * PART), a_s[...]).astype(BF16)
    t_s[0] = tiles[0:WIN]
    t_s[1] = tiles[WIN : 2 * WIN]
    keep_ref[...] = t_s[me]
    send_ref[...] = t_s[1 - me]


def second_call(windows, weight, bias_a, bias_b, tail, row, col):
    qkv = pltpu.VMEM((4 * WIN, MINE), BF16)
    half = jax.ShapeDtypeStruct((WIN, MINE), BF16)
    return pl.pallas_call(
        second_kernel,
        out_shape=(half, half),
        scratch_shapes=[
            qkv,
            qkv,
            qkv,
            pltpu.VMEM((4 * PART, MINE), BF16),
            pltpu.VMEM((PAIR, WIN, MINE), BF16),
        ],
        compiler_params=vmem(24),
        cost_estimate=pl.CostEstimate(flops=2 * 10**9, bytes_accessed=4 * 10**6, transcendentals=10**6),
        name="second",
    )(windows, weight, bias_a, bias_b, tail, row, col)


def most_kernel(mid_ref, keep_ref, wo_mine_ref, wo_other_ref, sum_ref, rows_ref, wo_s):
    me = lax.axis_index("lon")
    pair_columns(me, wo_s, wo_mine_ref[...], wo_other_ref[...])
    mine = pl.ds(pl.multiple_of(MINE * me, MINE), MINE)
    rows_ref[...] = wo_s[pl.ds(pl.multiple_of(MINE * (1 - me), MINE), MINE), :]
    sum_ref[...] = mid_ref[...].astype(F32) + nn_dot(keep_ref[...], wo_s[mine, :])


def most_call(mid, keep, wo_mine, wo_other):
    return pl.pallas_call(
        most_kernel,
        out_shape=(jax.ShapeDtypeStruct((WIN, D), F32), jax.ShapeDtypeStruct((MINE, D), BF16)),
        scratch_shapes=[pltpu.VMEM((D, D), BF16)],
        compiler_params=vmem(8),
        cost_estimate=pl.CostEstimate(flops=10**8, bytes_accessed=10**6, transcendentals=0),
        name="most",
    )(mid, keep, wo_mine, wo_other)


def last_kernel(sum_ref, rows_ref, got_ref, out_ref):
    value = sum_ref[...] + nn_dot(got_ref[...], rows_ref[...])
    out_ref[...] = value.reshape(WIN // WZ, WZ, D).astype(BF16)


def last_call(total, rows, got):
    return pl.pallas_call(
        last_kernel,
        out_shape=jax.ShapeDtypeStruct((WIN // WZ, WZ, D), BF16),
        compiler_params=vmem(8),
        cost_estimate=pl.CostEstimate(flops=10**8, bytes_accessed=10**6, transcendentals=0),
        name="last",
    )(total, rows, got)


def sharing(n_lat):
    every = tuple(range(1, n_lat))
    if n_lat == 4:
        return (((0,), every), ((0, 3), (1, 2)))
    return (((0,), every), ((0,), every))


def paired(latent, norm_gain, qkv_weight, out_weight, rel_bias, bias_index, region_ids):
    n_fsdp, n_lat = lax.axis_size("fsdp"), lax.axis_size("lat")
    part = qkv_weight.shape[1] // n_lat
    plan = sharing(n_lat)

    def swap(block):
        return passed_along(block, "lon", 1)

    def spread(block, axis, steps):
        got = []
        for k in steps:
            got.append(heard_from(block, axis, k))
        return got

    part0, part1, tile = open_call(
        jnp.transpose(latent[0], (1, 2, 0, 3)).reshape(WIN // WZ, WZ, D),
        jnp.transpose(region_ids, (1, 0, 2)),
        qkv_weight,
        out_weight,
        part,
        plan[1][0],
    )
    far0 = spread(part0, "fsdp", range(1, n_fsdp))
    mirrored = n_lat == 4
    side = heard_from(tile, "lat", 1) if mirrored else passed_along(tile, "lat", 1)
    cross = heard_from(tile, "lat", 3) if mirrored else passed_along(tile, "lat", -1)
    far1 = spread(part1, "fsdp", range(1, n_fsdp))
    near0 = spread(give_call(part, far0), "lat", plan[0][1])
    near1 = spread(give_call(part, far1), "lat", plan[1][1])
    three = (side, tile, cross)
    pair = [swap(t) for t in three]
    x, normed, tag_row, tag_col = enter_call(mirrored, three, pair, norm_gain)
    table = jnp.transpose(rel_bias, (0, 2, 1))
    params = (qkv_weight, out_weight)
    w0, wo0 = join_call(0, n_lat, plan[0][1], plan[0][0], *params, far0, near0)
    bias0, tail0, index, flip = bias_call(bias0_kernel, MY_HEADS, True, True, table, bias_index)
    o0 = first_call(normed, w0, bias0, tail0, wo0)
    w1, wo1 = join_call(1, n_lat, plan[1][1], plan[1][0], *params, far1, near1)
    half = MY_HEADS // 2
    (bias_a,) = bias_call(functools.partial(bias1_kernel, 0), half, False, False, table, index)
    bias_b, tail1 = bias_call(
        functools.partial(bias1_tail_kernel, half), half, True, False, table, index, flip
    )
    mid, windows = middle_call(o0, swap(o0), x, norm_gain)
    keep, send = second_call(windows, w1, bias_a, bias_b, tail1, tag_row, tag_col)
    total, rows = most_call(mid, keep, wo1, swap(wo1))
    out = last_call(total, rows, swap(send))
    return jnp.transpose(out.reshape(WH, WW, WZ, D), (2, 0, 1, 3))[None]


def solution(mesh):
    pair = mesh.shape["lon"] == PAIR

    def local(latent, norm_gain, qkv_weight, out_weight, *rest):
        one_window = latent.shape[:4] == (1, WZ, WH, WW)
        even = qkv_weight.shape[1] % (16 * mesh.shape["lat"]) == 0
        program = paired if pair and one_window and even else any_mesh
        return program(latent, norm_gain, qkv_weight, out_weight, *rest)

    return jax.shard_map(
        local,
        mesh=mesh,
        in_specs=(
            P("fsdp", None, "lat", "lon", None),
            P(),
            P(None, "fsdp", None),
            P(None, "fsdp", None),
            P(),
            P(),
            P(None, "lat", "lon"),
        ),
        out_specs=P("fsdp", None, "lat", "lon", None),
        check_vma=False,
    )
```

```python
import functools

import jax
import jax.numpy as jnp
from jax import lax
from jax.experimental import pallas as pl
from jax.experimental.pallas import tpu as pltpu
from jax.sharding import PartitionSpec as P


D = 512
HEADS = 16
HEAD_DIM = 32
WZ = 2
WH = 6
WW = 12
WIN = 144
BIAS_ROWS = 759
HALF = WIN // 2
LOG2E = 1.4426950408889634
SCALE2 = HEAD_DIM ** (-0.5) * LOG2E
NEG = -1e30


def passed_along(block, axis, distance):
    devices = range(lax.axis_size(axis))
    route = [((i - distance) % len(devices), i) for i in devices]
    return lax.ppermute(block, axis, route)


def layer_norm(hidden, gain_row):
    values = hidden.astype(jnp.float32)
    centre = jnp.mean(values, axis=-1, keepdims=True)
    shifted = values - centre
    variance = jnp.mean(shifted * shifted, axis=-1, keepdims=True)
    return (shifted * lax.rsqrt(variance + 1e-05) * gain_row).astype(jnp.bfloat16)


def bias_table(rel_bias, bias_index, block_index):
    return jnp.take(jnp.transpose(rel_bias[block_index]), bias_index, axis=1)


def split_tile(field_tile):
    sample_count, level_count, row_count, col_count, feature_width = field_tile.shape
    pieces = field_tile.reshape(
        sample_count, level_count // WZ, WZ, row_count // WH, WH, col_count // WW, WW, feature_width
    )
    pieces = jnp.transpose(pieces, (0, 1, 3, 5, 2, 4, 6, 7))
    return pieces.reshape(-1, WIN, feature_width)


def merge_tile(windows, tile_shape):
    sample_count, level_count, row_count, col_count, feature_width = tile_shape
    pieces = windows.reshape(
        sample_count, level_count // WZ, row_count // WH, col_count // WW, WZ, WH, WW, feature_width
    )
    pieces = jnp.transpose(pieces, (0, 1, 4, 2, 5, 3, 6, 7))
    return pieces.reshape(tile_shape)


def attend(normed, weight, bias_heads, region_tags):
    packed = jnp.dot(normed.reshape(-1, D), weight, preferred_element_type=jnp.float32).astype(
        jnp.bfloat16
    )
    packed = split_tile(packed.reshape(normed.shape[:-1] + (3 * D,)))
    packed = packed.reshape(-1, WIN, 3, HEADS, HEAD_DIM)
    scores = jnp.einsum(
        "gqhd,gkhd->ghqk", packed[:, :, 0], packed[:, :, 1], preferred_element_type=jnp.float32
    )
    scores = scores * HEAD_DIM ** (-0.5) + bias_heads[None]
    if region_tags is not None:
        window_tags = split_tile(region_tags[..., None])[..., 0]
        allowed = window_tags[:, :, None] == window_tags[:, None, :]
        blocked = jnp.where(allowed, jnp.float32(0.0), -jnp.inf)
        scores = scores + blocked[:, None]
    row_peak = jnp.max(scores, axis=-1, keepdims=True)
    exponent = jnp.exp(scores - row_peak)
    row_total = jnp.sum(exponent, axis=-1, keepdims=True)
    attn_probs = (exponent / row_total).astype(jnp.bfloat16)
    mixed_out = jnp.einsum(
        "ghqk,gkhd->gqhd", attn_probs, packed[:, :, 2], preferred_element_type=jnp.float32
    )
    return merge_tile(mixed_out.astype(jnp.bfloat16).reshape(-1, WIN, D), normed.shape)


def any_mesh(latent, norm_gain, qkv_weight, out_weight, rel_bias, bias_index, region_ids):
    half_rows = WH // 2
    half_cols = WW // 2
    row_count = latent.shape[2]
    col_count = latent.shape[3]
    gathered_qkv, gathered_out = (
        lax.all_gather(qkv_weight, "fsdp", axis=1, tiled=True),
        lax.all_gather(out_weight, "fsdp", axis=1, tiled=True),
    )

    def fetch_weights(block_index):
        return (gathered_qkv[block_index], gathered_out[block_index])

    first_qkv, first_out = fetch_weights(0)
    normed = layer_norm(latent, norm_gain[0])
    mixed_out = attend(normed, first_qkv, bias_table(rel_bias, bias_index, 0), None)
    projected = jnp.dot(mixed_out.reshape(-1, D), first_out, preferred_element_type=jnp.float32)
    middle = (latent.astype(jnp.float32) + projected.reshape(latent.shape)).astype(jnp.bfloat16)
    second_qkv, second_out = fetch_weights(1)
    normed = jnp.roll(layer_norm(middle, norm_gain[1]), -1, axis=1)
    east_strip = passed_along(normed[:, :, :, :half_cols], "lon", -1)
    widened = jnp.concatenate([normed[:, :, :, half_cols:], east_strip], axis=3)
    north_strip = passed_along(widened[:, :, :half_rows], "lat", -1)
    rolled = jnp.concatenate([widened[:, :, half_rows:], north_strip], axis=2)
    level_pos = lax.broadcasted_iota(jnp.int32, region_ids.shape, 0)
    row_pos = (
        lax.broadcasted_iota(jnp.int32, region_ids.shape, 1) + lax.axis_index("lat") * row_count
    )
    region_tags = region_ids * 4 + (level_pos == region_ids.shape[0] - 1).astype(jnp.int32) * 2
    region_tags = region_tags + (row_pos >= row_count * lax.axis_size("lat") - half_rows).astype(
        jnp.int32
    )
    region_tags = region_tags[None]
    mixed_out = attend(rolled, second_qkv, bias_table(rel_bias, bias_index, 1), region_tags)
    south_strip = passed_along(mixed_out[:, :, row_count - half_rows :], "lat", 1)
    widened = jnp.concatenate([south_strip, mixed_out[:, :, : row_count - half_rows]], axis=2)
    west_strip = passed_along(widened[:, :, :, col_count - half_cols :], "lon", 1)
    mixed_out = jnp.concatenate([west_strip, widened[:, :, :, : col_count - half_cols]], axis=3)
    mixed_out = jnp.roll(mixed_out, 1, axis=1)
    projected = jnp.dot(mixed_out.reshape(-1, D), second_out, preferred_element_type=jnp.float32)
    return (middle.astype(jnp.float32) + projected.reshape(latent.shape)).astype(jnp.bfloat16)


PAIR = 2
MY_HEADS = HEADS // PAIR
MINE = MY_HEADS * HEAD_DIM
QKV = 3 * MINE
OUT = D // PAIR
COLS = QKV + OUT
TALL = 3 * WIN
KEEP0 = 64
KEEP1 = TALL - 64
KEPT = KEEP1 - KEEP0
PART = WIN - KEEP0
MAIN = 128
TAIL = WIN - MAIN
LAG = 1
REGION_ROWS = 8
GROUP = 128 // HEAD_DIM
F32 = jnp.float32
BF16 = jnp.bfloat16


def vmem(mib):
    return pltpu.CompilerParams(vmem_limit_bytes=mib * 2**20)


def partner(index, step, size):
    if size & (size - 1) == 0:
        return index ^ step
    return (index + size - step) % size


def heard_from(block, axis, step):
    size = lax.axis_size(axis)
    return lax.ppermute(block, axis, [(partner(i, step, size), i) for i in range(size)])


def as_column(lanes, size):
    return jnp.transpose(lanes.astype(F32))[0:size, 0:1].astype(jnp.int32)


def window_sources():
    token = lax.broadcasted_iota(jnp.int32, (8, 3 * 128), 1)
    v, dh = token // WIN, token % WIN // (WW * WZ)
    dw, dz = token % (WW * WZ) // WZ, token % WZ
    col = (WW // 2 + WW * v + dw) % (2 * WW)
    level = (dz + 1) % WZ
    return as_column(col // WW * WIN + dh * WW * WZ + col % WW * WZ + level, 2 * WIN)


def tile_sources():
    token = lax.broadcasted_iota(jnp.int32, (8, 3 * 128), 1)
    tile = token // WIN
    row, cw, level = token % WIN // (WW * WZ), token % (WW * WZ) // WZ, token % WZ
    a = row // (WH // 2)
    dh = (row + WH // 2) % WH
    col = (WW * tile + cw + 2 * WW - WW // 2) % (2 * WW)
    dz = (level + WZ - 1) % WZ
    found = (a * 2 + col // WW) * PART + dh * WW * WZ + col % WW * WZ + dz - KEEP0 * (1 - a)
    return as_column(found, 2 * WIN)


def one_hot(sources, width):
    lanes = lax.broadcasted_iota(jnp.int32, (sources.shape[0], width), 1)
    return jnp.where(lanes == sources, 1.0, 0.0).astype(BF16)


def nt_dot(a, b):
    return lax.dot_general(a, b, (((1,), (1,)), ((), ())), preferred_element_type=F32)


def nn_dot(a, b):
    return jnp.dot(a, b, preferred_element_type=F32)


def norm_rows(values, gain_row):
    centre = jnp.mean(values, axis=-1, keepdims=True)
    shifted = values - centre
    variance = jnp.mean(shifted * shifted, axis=-1, keepdims=True)
    return (shifted * lax.rsqrt(variance + 1e-05) * gain_row).astype(BF16)


def look_up(table, at, heads, put):
    chunks = (BIAS_ROWS + 127) // 128
    low = at & 127
    chunk = at >> 7
    masks = [chunk == k for k in range(chunks)]
    for h in heads:
        acc = None
        for k in range(chunks):
            row = jnp.broadcast_to(table[h : h + 1, 128 * k : 128 * k + 128], (8, 128))
            got = jnp.take_along_axis(row, low, axis=1, mode="promise_in_bounds")
            acc = got if acc is None else jnp.where(masks[k], got, acc)
        put(h, acc)


def load_table(b, table_ref, table):
    me = lax.axis_index("lon")
    heads = table_ref[b, pl.ds(pl.multiple_of(MY_HEADS * me, MY_HEADS), MY_HEADS), :]
    table[:, 0:BIAS_ROWS] = heads * LOG2E


def gather_main(start, index_ref, table, bias_ref):
    def step(g, carry):
        rows = pl.ds(pl.multiple_of(g * 8, 8), 8)

        def put(h, value):
            bias_ref[h - start, rows, :] = value

        look_up(table, index_ref[rows, 0:MAIN], range(start, start + bias_ref.shape[0]), put)
        return carry

    lax.fori_loop(0, WIN // 8, step, 0, unroll=9)


def gather_tail(flip_ref, table, tail_ref, flipped):
    for t in range(0, TAIL, 8):
        for lo in (0, 128):

            def put(h, value, t=t, lo=lo):
                flipped[TAIL * h + t : TAIL * h + t + 8, lo : lo + 128] = value

            look_up(table, flip_ref[t : t + 8, lo : lo + 128], range(MY_HEADS), put)
    tail_ref[...] = jnp.transpose(flipped[...])[0:WIN]


def bias0_kernel(table_ref, index_ref, bias_ref, tail_ref, moved_ref, flip_ref, table, flipped):
    to = lax.broadcasted_iota(jnp.int32, (WIN, WIN), 0)
    frm = lax.broadcasted_iota(jnp.int32, (WIN, WIN), 1)
    move = jnp.where((to & 1) * HALF + (to >> 1) == frm, 1.0, 0.0).astype(BF16)
    whole = index_ref[...]
    parts = jnp.concatenate([whole >> 8, whole & 255], axis=0).astype(F32).astype(BF16)
    parts = nt_dot(parts, move).astype(BF16)
    high, low = parts[0:WIN], parts[WIN : 2 * WIN]
    moved = nn_dot(move, high) * 256.0 + nn_dot(move, low)
    moved_ref[...] = moved.astype(jnp.int32)
    flip_ref[:, WIN:256] = jnp.zeros((TAIL, 256 - WIN), jnp.int32)
    flip_ref[:, 0:WIN] = jnp.transpose(moved[:, MAIN:WIN]).astype(jnp.int32)
    load_table(0, table_ref, table)
    gather_main(0, moved_ref, table, bias_ref)
    gather_tail(flip_ref, table, tail_ref, flipped)


def bias1_kernel(start, table_ref, index_ref, bias_ref, table, flipped):
    load_table(1, table_ref, table)
    gather_main(start, index_ref, table, bias_ref)


def bias1_tail_kernel(start, table_ref, index_ref, flip_ref, bias_ref, tail_ref, table, flipped):
    load_table(1, table_ref, table)
    gather_main(start, index_ref, table, bias_ref)
    gather_tail(flip_ref, table, tail_ref, flipped)


def bias_call(kernel, heads, tail, first, *operands):
    out = [jax.ShapeDtypeStruct((heads, WIN, MAIN), F32)]
    out += [jax.ShapeDtypeStruct((WIN, MY_HEADS * TAIL), F32)] * tail
    if first:
        out += [jax.ShapeDtypeStruct((WIN, WIN), jnp.int32), jax.ShapeDtypeStruct((TAIL, 256), jnp.int32)]
    return pl.pallas_call(
        kernel,
        out_shape=out,
        scratch_shapes=[
            pltpu.VMEM((MY_HEADS, (BIAS_ROWS + 127) // 128 * 128), F32),
            pltpu.VMEM((MY_HEADS * TAIL, 256), F32),
        ],
        compiler_params=vmem(8),
        cost_estimate=pl.CostEstimate(flops=10**9, bytes_accessed=10**6, transcendentals=0),
    )(*operands)


def columns(qkv_ref, out_ref, b, rows, me, dst, at, sems):
    mine = pl.ds(pl.multiple_of(MINE * me, MINE), MINE)
    sources = [
        qkv_ref.at[b, rows, pl.ds(pl.multiple_of(D * k + MINE * me, MINE), MINE)] for k in range(3)
    ]
    sources += [out_ref.at[b, rows, mine]]
    to = pl.ds(at, rows.size)
    return [
        pltpu.make_async_copy(source, dst.at[to, pl.ds(MINE * k, MINE)], sems.at[k])
        for k, source in enumerate(sources)
    ]


def open_kernel(
    wide, latent_ref, region_ref, qkv_ref, out_ref, part0_ref, part1_ref, tile_ref,
    latent, regions, sems, own_sems,
):
    part = part0_ref.shape[0]
    me, lat = lax.axis_index("lon"), lax.axis_index("lat")

    def cut(b, dst, step, at, n):
        rows = pl.ds(pl.multiple_of((lat ^ step) * part, part), part)
        return columns(qkv_ref, out_ref, b, rows, me, dst, at, sems.at[n])

    copies = cut(0, part0_ref, 0, 0, 0)
    for i, step in enumerate(wide):
        copies += cut(1, part1_ref, step, part * i, 1 + i)
    inputs = [
        pltpu.make_async_copy(latent_ref, latent, own_sems.at[0]),
        pltpu.make_async_copy(region_ref, regions, own_sems.at[1]),
    ]
    for copy in copies + inputs:
        copy.start()
    for copy in inputs:
        copy.wait()
    tile_ref[0:WIN, :] = latent[...].reshape(WIN, D)
    col = lax.broadcasted_iota(jnp.int32, (WW, WIN), 0)
    token = lax.broadcasted_iota(jnp.int32, (WW, WIN), 1)
    spread = jnp.where(token % (WW * WZ) // WZ == col, 1.0, 0.0).astype(BF16)
    level = lax.broadcasted_iota(jnp.int32, (WZ, WIN), 0)
    token = lax.broadcasted_iota(jnp.int32, (WZ, WIN), 1)
    total = jnp.zeros((WZ, WIN), F32)
    for dh in range(WH):
        here = (token // (WW * WZ) == dh) & (token % WZ == level)
        total += jnp.where(here, nn_dot(regions[dh].astype(F32).astype(BF16), spread), 0.0)
    row = jnp.sum(total, axis=0, keepdims=True)
    tile_ref[WIN : WIN + REGION_ROWS, 0:WIN] = jnp.broadcast_to(row, (REGION_ROWS, WIN)).astype(BF16)
    tile_ref[WIN : WIN + REGION_ROWS, WIN:D] = jnp.zeros((REGION_ROWS, D - WIN), BF16)
    for copy in copies:
        copy.wait()


STAY = pl.BlockSpec(memory_space=pltpu.HBM)


def open_call(latent, regions, qkv, out, part, wide):
    return pl.pallas_call(
        functools.partial(open_kernel, wide),
        out_shape=(
            jax.ShapeDtypeStruct((part, COLS), BF16),
            jax.ShapeDtypeStruct((part * len(wide), COLS), BF16),
            jax.ShapeDtypeStruct((WIN + REGION_ROWS, D), BF16),
        ),
        in_specs=[STAY] * 4,
        scratch_shapes=[
            pltpu.VMEM(latent.shape, BF16),
            pltpu.VMEM(regions.shape, jnp.int32),
            pltpu.SemaphoreType.DMA((1 + len(wide), 4)),
            pltpu.SemaphoreType.DMA((2,)),
        ],
        compiler_params=pltpu.CompilerParams(vmem_limit_bytes=67043328-400*1024),
        cost_estimate=pl.CostEstimate(flops=10**6, bytes_accessed=10**6, transcendentals=0),
        name="open",
    )(latent, regions, qkv, out)


def enter_kernel(mirrored, *refs):
    mine, other = refs[0:3], refs[3:6]
    gain_ref, x_ref, n_ref, row_ref, col_ref = refs[6:]
    me = lax.axis_index("lon")
    n_lat = lax.axis_size("lat")
    lat = lax.axis_index("lat")
    odd = lat & 1 if mirrored else 1
    places = (2 - 2 * odd, 1, 2 * odd)
    for k, place in enumerate(places):
        rows = pl.ds(pl.multiple_of(WIN * place, WIN), WIN)
        for ref, l in ((mine[k], me), (other[k], 1 - me)):
            tokens = ref[0:WIN, :]
            x_ref[l, rows, :] = tokens
            n_ref[l, rows, :] = norm_rows(tokens.astype(F32), gain_ref[0:1, :])
    lanes = lax.broadcasted_iota(jnp.int32, (1, WIN), 1)
    level = lanes & 1
    dh = lanes // (WW * WZ)

    def regions(three):
        found = [ref[WIN : WIN + REGION_ROWS, 0:WIN].astype(F32)[0:1] for ref in three]
        return jnp.where(odd == 1, found[0], found[2]), found[1]

    rows = []
    for a, (own, pair) in enumerate(zip(regions(mine), regions(other))):
        window = (lat + n_lat - 1 + a) % n_lat
        late = window * WH + dh >= n_lat * WH - WH // 2
        extra = jnp.where(level == WZ - 1, 2.0, 0.0) + jnp.where(late, 1.0, 0.0)
        west = jnp.where(me == 0, own, pair)
        east = jnp.where(me == 0, pair, own)
        rows += [4.0 * west + extra, 4.0 * east + extra]
    tags = jnp.concatenate(rows + rows, axis=0)
    row_ref[:, 0:MAIN] = tags[:, 0:MAIN]
    row_ref[:, MAIN:] = jnp.concatenate([tags[:, MAIN:WIN]] * MY_HEADS, axis=1)
    to = lax.broadcasted_iota(jnp.int32, (WIN, WIN), 0)
    frm = lax.broadcasted_iota(jnp.int32, (WIN, WIN), 1)
    col_ref[...] = nt_dot(jnp.where(to == frm, 1.0, 0.0).astype(BF16), tags.astype(BF16))


def enter_call(mirrored, mine, other, gain):
    return pl.pallas_call(
        functools.partial(enter_kernel, mirrored),
        out_shape=(
            jax.ShapeDtypeStruct((PAIR, TALL, D), BF16),
            jax.ShapeDtypeStruct((PAIR, TALL, D), BF16),
            jax.ShapeDtypeStruct((8, MAIN + MY_HEADS * TAIL), F32),
            jax.ShapeDtypeStruct((WIN, 8), F32),
        ),
        compiler_params=vmem(16),
        cost_estimate=pl.CostEstimate(flops=10**8, bytes_accessed=2 * 10**6, transcendentals=0),
        name="enter",
    )(*mine, *other, gain)


def give_kernel(part, *refs):
    for k, ref in enumerate(refs[:-1]):
        refs[-1][part * k : part * (k + 1), :] = ref[0:part, :]


def give_call(part, pieces):
    return pl.pallas_call(
        functools.partial(give_kernel, part),
        out_shape=jax.ShapeDtypeStruct((part * len(pieces), COLS), BF16),
        compiler_params=vmem(4),
        cost_estimate=pl.CostEstimate(flops=0, bytes_accessed=10**6, transcendentals=0),
    )(*pieces)


def join_kernel(b, n_fsdp, n_lat, steps, wide, own_qkv_ref, own_out_ref, *refs):
    far, near = refs[: n_fsdp - 1], refs[n_fsdp - 1 : n_fsdp - 1 + len(steps)]
    qkv_ref, out_ref = refs[-2:]
    z, lat = lax.axis_index("fsdp"), lax.axis_index("lat")
    depth = own_qkv_ref.shape[1]
    part = depth // n_lat
    me = lax.axis_index("lon")

    def put(first, size, piece):
        rows = pl.ds(pl.multiple_of(first, size), size)
        qkv_ref[rows, :] = piece[:, 0:QKV]
        out_ref[rows, :] = piece[:, QKV:COLS]

    own = pl.ds(pl.multiple_of(z * depth, depth), depth)
    for k in range(3):
        mine = pl.ds(pl.multiple_of(D * k + MINE * me, MINE), MINE)
        qkv_ref[own, MINE * k : MINE * (k + 1)] = own_qkv_ref[b, :, mine]
    out_ref[own, :] = own_out_ref[b, :, pl.ds(pl.multiple_of(OUT * me, OUT), OUT)]
    for k in range(1, n_fsdp):
        base = partner(z, k, n_fsdp) * depth
        for i, step in enumerate(wide):
            put(base + (lat ^ step) * part, part, far[k - 1][part * i : part * (i + 1), :])
        for j, step in enumerate(steps):
            row = base + partner(lat, step, n_lat) * part
            put(row, part, near[j][part * (k - 1) : part * k, :])


def join_call(b, n_lat, steps, wide, qkv, out, far, near):
    rows = qkv.shape[1] * (len(far) + 1)
    return pl.pallas_call(
        functools.partial(join_kernel, b, len(far) + 1, n_lat, steps, wide),
        out_shape=(
            jax.ShapeDtypeStruct((rows, QKV), BF16),
            jax.ShapeDtypeStruct((rows, OUT), BF16),
        ),
        compiler_params=vmem(8),
        cost_estimate=pl.CostEstimate(flops=10**6, bytes_accessed=2 * 10**6, transcendentals=0),
    )(qkv, out, *far, *near)


def window_attend(q, k, v, bias_at, tail_bias, allowed, tail_allowed, put):
    n = q.shape[0]
    width = MY_HEADS * TAIL
    lanes = lax.broadcasted_iota(jnp.int32, (n, 128), 1)
    owns = [lanes // HEAD_DIM == j for j in range(GROUP)]
    blocks = [lanes // TAIL == h for h in range(MY_HEADS)]
    row = lax.broadcasted_iota(jnp.int32, (width, MINE), 0)
    col = lax.broadcasted_iota(jnp.int32, (width, MINE), 1)
    same = row // TAIL == col // HEAD_DIM
    groups = range(MINE // 128)

    def spread(x):
        x = jnp.concatenate([x[MAIN:WIN]] * MY_HEADS, axis=0)
        return jnp.where(same, x, jnp.zeros_like(x))

    tail = nt_dot(q, spread(k)) + tail_bias
    scores = []
    for g in groups:
        cols = slice(128 * g, 128 * (g + 1))
        q_g = q[:, cols]
        q_all = jnp.concatenate([jnp.where(o, q_g, jnp.zeros_like(q_g)) for o in owns], axis=0)
        scores.append(nt_dot(q_all, k[0:MAIN, cols]))
    yield
    if tail_allowed is not None:
        tail = jnp.where(tail_allowed, tail, NEG)
    tail_peak = jnp.zeros_like(tail)
    probs = []
    for h in range(MY_HEADS):
        j = h % GROUP
        s = scores[h // GROUP][n * j : n * (j + 1)] + bias_at(h)
        if allowed is not None:
            s = jnp.where(allowed, s, NEG)
        peak = jnp.max(jnp.maximum(s, jnp.where(blocks[h], tail, NEG)), axis=-1, keepdims=True)
        tail_peak = jnp.where(blocks[h], peak, tail_peak)
        probs.append(jnp.exp2(s - peak).astype(BF16))
    tail = jnp.exp2(tail - tail_peak).astype(BF16)
    yield
    rest = nn_dot(tail, spread(v))
    ones = jnp.where(same, 1.0, 0.0).astype(BF16)
    rest_total = nn_dot(tail, ones)
    for g in groups:
        cols = slice(128 * g, 128 * (g + 1))
        wide = jnp.concatenate([v[0:MAIN, cols], jnp.ones((MAIN, 128), BF16)], axis=1)
        mixed = nn_dot(jnp.concatenate(probs[GROUP * g : GROUP * (g + 1)], axis=0), wide)
        value, total = mixed[0:n, 0:128], mixed[0:n, 128:256]
        for j in range(1, GROUP):
            value = jnp.where(owns[j], mixed[n * j : n * (j + 1), 0:128], value)
            total = jnp.where(owns[j], mixed[n * j : n * (j + 1), 128:256], total)
        put(128 * g, ((value + rest[:, cols]) / (total + rest_total[:, cols])).astype(BF16))
    yield


def staggered(windows, lag):
    for at in range(len(windows) + 2 * lag):
        for stage in range(3):
            if 0 <= at - stage * lag < len(windows):
                next(windows[at - stage * lag])


def project(n, w_ref, q_s, k_s, v_s):
    both = nn_dot(n, w_ref[...])
    q_s[...] = (both[:, 0:MINE] * SCALE2).astype(BF16)
    k_s[...] = both[:, MINE : 2 * MINE].astype(BF16)
    v_s[...] = both[:, 2 * MINE : 3 * MINE].astype(BF16)


def first_kernel(n_ref, w_ref, bias_ref, tail_ref, wo_ref, o_ref, q_s, k_s, v_s):
    o_ref[PAIR * KEPT :, :] = wo_ref[...]
    project(n_ref[...].reshape(PAIR * TALL, D), w_ref, q_s, k_s, v_s)
    windows = []
    for l in range(PAIR):
        for part, (q0, q1, o0) in enumerate(
            ((KEEP0, WIN, 0), (0, WIN, PART), (0, PART, PART + WIN))
        ):
            t = TALL * l + WIN * part

            def put(col, value, l=l, o0=o0, q0=q0, q1=q1):
                o_ref[KEPT * l + o0 : KEPT * l + o0 + q1 - q0, col : col + 128] = value

            windows.append(window_attend(
                q_s[t + q0 : t + q1, :],
                k_s[t : t + WIN, :],
                v_s[t : t + WIN, :],
                lambda h, q0=q0, q1=q1: bias_ref[h, q0:q1, :],
                tail_ref[q0:q1, :],
                None,
                None,
                put,
            ))
    staggered(windows, LAG)


def first_call(normed, weight, bias, tail, wo):
    scratch = pltpu.VMEM((PAIR * TALL, MINE), BF16)
    return pl.pallas_call(
        first_kernel,
        out_shape=jax.ShapeDtypeStruct((PAIR * KEPT + D, MINE), BF16),
        scratch_shapes=[scratch, scratch, scratch],
        compiler_params=vmem(24),
        cost_estimate=pl.CostEstimate(flops=2 * 10**9, bytes_accessed=4 * 10**6, transcendentals=10**6),
        name="first",
    )(normed, weight, bias, tail, wo)


def pair_columns(me, ref, mine, other):
    width = mine.shape[-1]
    ref[:, pl.ds(pl.multiple_of(width * me, width), width)] = mine
    ref[:, pl.ds(pl.multiple_of(width * (1 - me), width), width)] = other


def middle_kernel(
    mine_ref, other_ref, x_ref, gain_ref, mid_ref, win_ref, o_s, wo_s, m_s, n_s
):
    me = lax.axis_index("lon")
    tokens = PAIR * KEPT
    pair_columns(me, o_s, mine_ref[0:tokens, :], other_ref[0:tokens, :])
    pair_columns(me, wo_s, mine_ref[tokens:, :], other_ref[tokens:, :])
    pick = one_hot(window_sources(), 2 * WIN)
    for l in range(PAIR):
        rows = slice(KEPT * l, KEPT * (l + 1))
        value = x_ref[l, KEEP0:KEEP1, :].astype(F32) + nn_dot(o_s[rows, :], wo_s[...])
        value = value.astype(BF16)
        m_s[l] = value
        normed = norm_rows(value.astype(F32), gain_ref[1:2, :])
        for a in range(2):
            at = HALF - KEEP0 + WIN * a
            n_s[a, WIN * l : WIN * (l + 1), :] = normed[at : at + WIN]
    mid_ref[...] = m_s[me, PART : PART + WIN, :]
    for a in range(2):
        win_ref[2 * WIN * a : 2 * WIN * (a + 1), :] = nn_dot(pick, n_s[a]).astype(BF16)


def middle_call(mine, other, x, gain):
    tokens = PAIR * KEPT
    return pl.pallas_call(
        middle_kernel,
        out_shape=(
            jax.ShapeDtypeStruct((WIN, D), BF16),
            jax.ShapeDtypeStruct((4 * WIN, D), BF16),
        ),
        scratch_shapes=[
            pltpu.VMEM((tokens, D), BF16),
            pltpu.VMEM((D, D), BF16),
            pltpu.VMEM((PAIR, KEPT, D), BF16),
            pltpu.VMEM((2, 2 * WIN, D), BF16),
        ],
        compiler_params=vmem(16),
        cost_estimate=pl.CostEstimate(flops=10**9, bytes_accessed=3 * 10**6, transcendentals=0),
        name="middle",
    )(mine, other, x, gain)


def second_kernel(
    win_ref, w_ref, bias_a, bias_b, tail_ref, row_ref, col_ref, keep_ref, send_ref, q_s, k_s, v_s, a_s, t_s
):
    me = lax.axis_index("lon")
    half = MY_HEADS // 2
    project(win_ref[...], w_ref, q_s, k_s, v_s)
    windows = []
    for w in range(4):
        q0, q1 = (KEEP0, WIN) if w < 2 else (0, PART)
        t = WIN * w
        allowed = col_ref[q0:q1, w : w + 1] == row_ref[w : w + 1, :]

        def put(col, value, w=w):
            a_s[PART * w : PART * (w + 1), col : col + 128] = value

        windows.append(window_attend(
            q_s[t + q0 : t + q1, :],
            k_s[t : t + WIN, :],
            v_s[t : t + WIN, :],
            lambda h, q0=q0, q1=q1: (bias_a, bias_b)[h // half][h % half, q0:q1, :],
            tail_ref[q0:q1, :],
            allowed[:, 0:MAIN],
            allowed[:, MAIN:],
            put,
        ))
    staggered(windows, LAG)
    tiles = nn_dot(one_hot(tile_sources(), 4 * PART), a_s[...]).astype(BF16)
    t_s[0] = tiles[0:WIN]
    t_s[1] = tiles[WIN : 2 * WIN]
    keep_ref[...] = t_s[me]
    send_ref[...] = t_s[1 - me]


def second_call(windows, weight, bias_a, bias_b, tail, row, col):
    qkv = pltpu.VMEM((4 * WIN, MINE), BF16)
    half = jax.ShapeDtypeStruct((WIN, MINE), BF16)
    return pl.pallas_call(
        second_kernel,
        out_shape=(half, half),
        scratch_shapes=[
            qkv,
            qkv,
            qkv,
            pltpu.VMEM((4 * PART, MINE), BF16),
            pltpu.VMEM((PAIR, WIN, MINE), BF16),
        ],
        compiler_params=vmem(24),
        cost_estimate=pl.CostEstimate(flops=2 * 10**9, bytes_accessed=4 * 10**6, transcendentals=10**6),
        name="second",
    )(windows, weight, bias_a, bias_b, tail, row, col)


def most_kernel(mid_ref, keep_ref, wo_mine_ref, wo_other_ref, sum_ref, rows_ref, wo_s):
    me = lax.axis_index("lon")
    pair_columns(me, wo_s, wo_mine_ref[...], wo_other_ref[...])
    mine = pl.ds(pl.multiple_of(MINE * me, MINE), MINE)
    rows_ref[...] = wo_s[pl.ds(pl.multiple_of(MINE * (1 - me), MINE), MINE), :]
    sum_ref[...] = mid_ref[...].astype(F32) + nn_dot(keep_ref[...], wo_s[mine, :])


def most_call(mid, keep, wo_mine, wo_other):
    return pl.pallas_call(
        most_kernel,
        out_shape=(jax.ShapeDtypeStruct((WIN, D), F32), jax.ShapeDtypeStruct((MINE, D), BF16)),
        scratch_shapes=[pltpu.VMEM((D, D), BF16)],
        compiler_params=vmem(8),
        cost_estimate=pl.CostEstimate(flops=10**8, bytes_accessed=10**6, transcendentals=0),
        name="most",
    )(mid, keep, wo_mine, wo_other)


def last_kernel(sum_ref, rows_ref, got_ref, out_ref):
    value = sum_ref[...] + nn_dot(got_ref[...], rows_ref[...])
    out_ref[...] = value.reshape(WIN // WZ, WZ, D).astype(BF16)


def last_call(total, rows, got):
    return pl.pallas_call(
        last_kernel,
        out_shape=jax.ShapeDtypeStruct((WIN // WZ, WZ, D), BF16),
        compiler_params=vmem(8),
        cost_estimate=pl.CostEstimate(flops=10**8, bytes_accessed=10**6, transcendentals=0),
        name="last",
    )(total, rows, got)


def sharing(n_lat):
    every = tuple(range(1, n_lat))
    if n_lat == 4:
        return (((0,), every), ((0, 3), (1, 2)))
    return (((0,), every), ((0,), every))


def paired(latent, norm_gain, qkv_weight, out_weight, rel_bias, bias_index, region_ids):
    n_fsdp, n_lat = lax.axis_size("fsdp"), lax.axis_size("lat")
    part = qkv_weight.shape[1] // n_lat
    plan = sharing(n_lat)

    def swap(block):
        return passed_along(block, "lon", 1)

    def spread(block, axis, steps):
        got = []
        for k in steps:
            got.append(heard_from(block, axis, k))
        return got

    part0, part1, tile = open_call(
        jnp.transpose(latent[0], (1, 2, 0, 3)).reshape(WIN // WZ, WZ, D),
        jnp.transpose(region_ids, (1, 0, 2)),
        qkv_weight,
        out_weight,
        part,
        plan[1][0],
    )
    far0 = spread(part0, "fsdp", range(1, n_fsdp))
    mirrored = n_lat == 4
    side = heard_from(tile, "lat", 1) if mirrored else passed_along(tile, "lat", 1)
    cross = heard_from(tile, "lat", 3) if mirrored else passed_along(tile, "lat", -1)
    far1 = spread(part1, "fsdp", range(1, n_fsdp))
    near0 = spread(give_call(part, far0), "lat", plan[0][1])
    near1 = spread(give_call(part, far1), "lat", plan[1][1])
    three = (side, tile, cross)
    pair = [swap(t) for t in three]
    x, normed, tag_row, tag_col = enter_call(mirrored, three, pair, norm_gain)
    table = jnp.transpose(rel_bias, (0, 2, 1))
    params = (qkv_weight, out_weight)
    w0, wo0 = join_call(0, n_lat, plan[0][1], plan[0][0], *params, far0, near0)
    bias0, tail0, index, flip = bias_call(bias0_kernel, MY_HEADS, True, True, table, bias_index)
    o0 = first_call(normed, w0, bias0, tail0, wo0)
    w1, wo1 = join_call(1, n_lat, plan[1][1], plan[1][0], *params, far1, near1)
    half = MY_HEADS // 2
    (bias_a,) = bias_call(functools.partial(bias1_kernel, 0), half, False, False, table, index)
    bias_b, tail1 = bias_call(
        functools.partial(bias1_tail_kernel, half), half, True, False, table, index, flip
    )
    mid, windows = middle_call(o0, swap(o0), x, norm_gain)
    keep, send = second_call(windows, w1, bias_a, bias_b, tail1, tag_row, tag_col)
    total, rows = most_call(mid, keep, wo1, swap(wo1))
    out = last_call(total, rows, swap(send))
    return jnp.transpose(out.reshape(WH, WW, WZ, D), (2, 0, 1, 3))[None]


def solution(mesh):
    pair = mesh.shape["lon"] == PAIR

    def local(latent, norm_gain, qkv_weight, out_weight, *rest):
        one_window = latent.shape[:4] == (1, WZ, WH, WW)
        even = qkv_weight.shape[1] % (16 * mesh.shape["lat"]) == 0
        program = paired if pair and one_window and even else any_mesh
        return program(latent, norm_gain, qkv_weight, out_weight, *rest)

    return jax.shard_map(
        local,
        mesh=mesh,
        in_specs=(
            P("fsdp", None, "lat", "lon", None),
            P(),
            P(None, "fsdp", None),
            P(None, "fsdp", None),
            P(),
            P(),
            P(None, "lat", "lon"),
        ),
        out_specs=P("fsdp", None, "lat", "lon", None),
        check_vma=False,
    )
```
